32 devices in a mesh: dp: 4 (over x, core), space: 8 (over z, y).
Axes of the slice: x: 2, y: 2, z: 4, core: 2. Of those that a mesh axis runs over, the one named last changes fastest.
Arguments:
- positions: float32 [4, 3, 4096], P('dp', None, 'space'), may hold values from 0 to 2, as said below
- species: int32 [4, 4096], P('dp', 'space'), may hold values from 0 to 3
- ref_forces: float32 [4, 3, 4096], P('dp', None, 'space'), may hold values from -6 to 6
- send_lists: int32 [4, 16, 256], P('dp', 'space'), may hold values from 0 to 511, as said below
- tile_lists: int32 [4, 64, 2], P('dp', 'space'), may hold values from -1 to 15, as said below
- weights: int32 [4], P('dp'), may hold values from 1 to 8
- w_rad: float32 [8, 256], replicated, may hold values from -24 to 24
- emb_center: float32 [4, 256], replicated, may hold values from -10 to 10
- emb_other: float32 [4, 256], replicated, may hold values from -10 to 10
- w_out: float32 [256], replicated, may hold values from -0.004 to 0.004
Outputs:
- forces: float32 [4, 3, 4096], P('dp', None, 'space')
- loss: float32 [], replicated
- grad_rad: float32 [8, 256], replicated
- grad_center: float32 [4, 256], replicated
- grad_other: float32 [4, 256], replicated
- grad_out: float32 [256], replicated
The draws below stay inside these ranges and needn't reach their ends.
Inputs may be any that keep to these rules, and one draw needn't show every extreme that they name: `send_lists`: for each snapshot and domain the two send rows together name each of the domain's 512 atoms once; row 0 names exactly the atoms whose first coordinate is below 1. `positions`: the first coordinate lies in [0, 2), the other two in [0, 2). `tile_lists`: each row names distinct pool tiles, live entries first, then -1; every row has one or more live entries; in every snapshot some domain has all 2 slots of every tile live.
All inputs are finite; a program needn't handle non-finite values.
Results may differ from the reference program's by a relative error of at most 0.0003.
Values sent between devices are 32-bit elements; how exact they have to be, the bound alone decides.
A program may use at most 64 MiB of HBM per device.

```python
import jax
import jax.numpy as jnp
from jax import lax

HID = 256
NB = 8
NS = 4
KS = 2
TILES_DEV = 8
A_DEV = 512
HALF = 256
ATOMS = 4096
N_DP = 4
N_SPACE = 8


DOMAIN_WIDTH = 2.0


def layout(key):
    keys = jax.random.split(jax.random.fold_in(key, 11), N_DP * N_SPACE)
    perms = jax.vmap(lambda one_key: jax.random.permutation(one_key, A_DEV))(keys)
    return perms.reshape(N_DP, N_SPACE, 2, HALF).astype(jnp.int32)


def draw_send_lists(key, part):
    return layout(key).reshape(N_DP, 2 * N_SPACE, HALF).astype(jnp.int32)


def draw_positions(key, part):
    perms = layout(key).reshape(N_DP, N_SPACE, A_DEV)
    rank = jnp.argsort(perms, axis=-1)
    lower = (rank < HALF).astype(jnp.float32)
    first_key, second_key = jax.random.split(jax.random.fold_in(key, 23))
    spread = jax.random.uniform(first_key, (N_DP, N_SPACE, A_DEV), jnp.float32)
    across = jax.random.uniform(second_key, (N_DP, 2, N_SPACE, A_DEV), jnp.float32)
    along = 0.5 * DOMAIN_WIDTH * (spread + 1.0 - lower)
    along = jnp.minimum(along, DOMAIN_WIDTH * (1.0 - 0.5 * lower) - 0.0001)
    coords = jnp.concatenate([along[:, None], across * DOMAIN_WIDTH * 0.9999], axis=1)
    return coords.reshape(N_DP, 3, ATOMS).astype(jnp.float32)


def draw_tile_lists(key, part):
    first_key, second_key, third_key, fourth_key = jax.random.split(jax.random.fold_in(key, 37), 4)
    keys = jax.random.split(first_key, N_DP * N_SPACE * TILES_DEV)
    chosen = jax.vmap(lambda one_key: jax.random.permutation(one_key, 2 * TILES_DEV)[:KS])(keys)
    chosen = chosen.reshape(N_DP, N_SPACE, TILES_DEV, KS)
    dense = jax.random.randint(second_key, (N_DP, N_SPACE), 0, 8) == 0
    forced = jax.random.randint(third_key, (N_DP,), 0, N_SPACE)
    dense = dense | (jnp.arange(N_SPACE, dtype=jnp.int32)[None, :] == forced[:, None])
    light = jax.random.randint(fourth_key, (N_DP, N_SPACE, TILES_DEV), 1, KS + 1)
    count = jnp.where(dense[:, :, None], KS, light)
    slot = jnp.arange(KS, dtype=jnp.int32)
    lists = jnp.where(slot < count[..., None], chosen, -1)
    return lists.reshape(N_DP, N_SPACE * TILES_DEV, KS).astype(jnp.int32)


def draw_w_rad(key, part):
    sign_key, size_key = jax.random.split(jax.random.fold_in(key, 41))
    magnitude = jax.random.uniform(size_key, (NB, HID), jnp.float32, 12.0, 22.0)
    channel_sign = jnp.where(jax.random.uniform(sign_key, (1, HID), jnp.float32) < 0.5, 1.0, -1.0)
    basis_sign = jnp.where(jnp.arange(NB, dtype=jnp.int32) % 2 == 0, 1.0, -1.0)[:, None]
    return (magnitude * channel_sign * basis_sign).astype(jnp.float32)


def draw_w_out(key, part):
    value_key = jax.random.fold_in(key, 53)
    values = 0.001 * jnp.clip(jax.random.normal(value_key, (HID,), jnp.float32), -3.9, 3.9)
    return values.astype(jnp.float32)


def touch_ends(drawn, own_key, smallest, top_value):
    longest = drawn.shape.index(max(drawn.shape))
    spots = []
    for shift in (0, 1):
        where = [jax.random.randint(jax.random.fold_in(own_key, axis), (), 0, length) for axis, length in enumerate(drawn.shape)]
        where[longest] = (where[longest] + shift) % drawn.shape[longest]
        spots.append(tuple(where))
    return drawn.at[spots[0]].set(smallest).at[spots[1]].set(top_value)


def shard_levels(stream_key, dims, cuts, least, top_value):
    level = 1.0
    for position, blocks in cuts:
        draws = jax.random.uniform(jax.random.fold_in(jax.random.fold_in(stream_key, 6), position), (blocks,), jnp.float32, least / len(cuts), top_value / len(cuts))
        level = level * jnp.repeat(jnp.exp(draws), dims[position] // blocks).reshape((-1,) + (1,) * (len(dims) - 1 - position))
    return level


def normal_values(rng, dims, deviation, most, cuts=(), kind=jnp.bfloat16):
    level = shard_levels(rng, dims, cuts, -0.22, 0.18) if cuts else 1.0
    values = jax.random.normal(rng, dims, jnp.float32) * deviation * level
    return jnp.minimum(jnp.maximum(values, -most), most).astype(kind)


def setup_inputs(seed: int = 0) -> dict:
    streams_of = jax.random.split(jax.random.key(seed), 11)
    positions = draw_positions(jax.random.fold_in(streams_of[10], 71), 0)
    species = touch_ends(jax.random.randint(streams_of[1], (N_DP, ATOMS), 0, NS), jax.random.fold_in(streams_of[1], 1), 0, NS - 1).astype(jnp.int32)
    ref_forces = normal_values(streams_of[2], (N_DP, 3, ATOMS), 1.0, 6.0, ((0, 4), (2, 8)), jnp.float32)
    send_lists = draw_send_lists(jax.random.fold_in(streams_of[10], 71), 0)
    tile_lists = draw_tile_lists(jax.random.fold_in(streams_of[10], 71), 0)
    weights = touch_ends(jax.random.randint(streams_of[5], (N_DP,), 1, 9), jax.random.fold_in(streams_of[5], 1), 1, 8).astype(jnp.int32)
    w_rad = draw_w_rad(jax.random.fold_in(streams_of[10], 71), 0)
    emb_center = jnp.clip(jax.random.uniform(streams_of[7], (NS, HID), jnp.float32, -10.0, 10.0), -10.0, 10.0)
    emb_other = jnp.clip(jax.random.uniform(streams_of[8], (NS, HID), jnp.float32, -10.0, 10.0), -10.0, 10.0)
    w_out = draw_w_out(jax.random.fold_in(streams_of[10], 71), 0)
    return dict(positions=positions, species=species, ref_forces=ref_forces, send_lists=send_lists, tile_lists=tile_lists, weights=weights, w_rad=w_rad, emb_center=emb_center, emb_other=emb_other, w_out=w_out)


CUTOFF = 1.0
DOMAIN_WIDTH = 2.0
PRECISE = lax.Precision.HIGHEST

def tile_energy(params, first_tile, second_tile, first_kind, second_kind, same_tile):
    radial_weight, center_table, other_table, out_weight = params
    basis_count = radial_weight.shape[0]
    channels = radial_weight.shape[1]
    tile_size = first_tile.shape[1]
    species_count = center_table.shape[0]
    offsets = first_tile[:, :, None] - second_tile[:, None, :]
    scaled = lax.optimization_barrier(jnp.sum(offsets * offsets, axis=0)).reshape(1, tile_size * tile_size) / (CUTOFF * CUTOFF)
    centers = jnp.arange(basis_count, dtype=jnp.float32)[:, None] / (basis_count - 1)
    basis = jnp.exp(-jnp.square((scaled - centers) * (basis_count - 1)))
    radial = jnp.dot(radial_weight.T, basis, precision=PRECISE, preferred_element_type=jnp.float32)
    labels = jnp.arange(species_count, dtype=jnp.int32)[:, None]
    center = jnp.dot(center_table.T, (first_kind[None, :] == labels).astype(jnp.float32), precision=PRECISE, preferred_element_type=jnp.float32)
    other = jnp.dot(other_table.T, (second_kind[None, :] == labels).astype(jnp.float32), precision=PRECISE, preferred_element_type=jnp.float32)
    latent = radial.reshape(channels, tile_size, tile_size) + center[:, :, None] + other[:, None, :]
    pair = jnp.dot(out_weight[None, :], jax.nn.silu(latent).reshape(channels, tile_size * tile_size), precision=PRECISE, preferred_element_type=jnp.float32)
    envelope = jnp.square(jnp.maximum(1.0 - scaled, 0.0))
    weighted = (pair * envelope).reshape(tile_size, tile_size)
    keep = 1.0 - same_tile * jnp.eye(tile_size, dtype=jnp.float32)
    return jnp.sum(weighted * keep)

def add_tile(total, piece, start):
    current = lax.dynamic_slice_in_dim(total, start, piece.shape[1], 1)
    return lax.dynamic_update_slice_in_dim(total, current + piece, start, 1)

def pool_gradient(params, pool_pos, pool_kind, tile_list):
    tiles_own = tile_list.shape[0]
    slots = tile_list.shape[1]
    tile_size = pool_pos.shape[1] // (2 * tiles_own)

    def visit(total, number):
        own_tile = number // slots + tiles_own // 2
        entry = tile_list[number // slots, number % slots]
        live = (entry >= 0).astype(jnp.float32)
        other_tile = jnp.maximum(entry, 0)
        first_start = (own_tile * tile_size).astype(jnp.int32)
        second_start = (other_tile * tile_size).astype(jnp.int32)
        first_tile = lax.dynamic_slice_in_dim(pool_pos, first_start, tile_size, 1)
        second_tile = lax.dynamic_slice_in_dim(pool_pos, second_start, tile_size, 1)
        first_kind = lax.dynamic_slice_in_dim(pool_kind, first_start, tile_size, 0)
        second_kind = lax.dynamic_slice_in_dim(pool_kind, second_start, tile_size, 0)
        same = (other_tile == own_tile).astype(jnp.float32)
        first_grad, second_grad = jax.grad(tile_energy, argnums=(1, 2))(params, first_tile, second_tile, first_kind, second_kind, same)
        total = add_tile(total, first_grad * live, first_start)
        total = add_tile(total, second_grad * live, second_start)
        return (total, None)
    total, _ = lax.scan(visit, jnp.zeros_like(pool_pos), jnp.arange(tiles_own * slots, dtype=jnp.int32))
    return total

def snapshot_gradient(params, coords, kinds, sends, tiles):
    own = coords.reshape(3, N_SPACE, A_DEV).transpose(1, 0, 2)
    own_kind = kinds.reshape(N_SPACE, A_DEV)
    rows = sends.reshape(N_SPACE, 2, HALF)
    lower = rows[:, 0, :]
    upper = rows[:, 1, :]
    take_pos = jax.vmap(lambda block, index: block[:, index])
    take_kind = jax.vmap(lambda block, index: block[index])
    shift = jnp.array([DOMAIN_WIDTH, 0.0, 0.0], dtype=jnp.float32)[None, :, None]
    left_pos = jnp.roll(take_pos(own, upper), 1, axis=0) - shift
    right_pos = jnp.roll(take_pos(own, lower), -1, axis=0) + shift
    left_kind = jnp.roll(take_kind(own_kind, upper), 1, axis=0)
    right_kind = jnp.roll(take_kind(own_kind, lower), -1, axis=0)
    pool_pos = jnp.concatenate([left_pos, own, right_pos], axis=2)
    pool_kind = jnp.concatenate([left_kind, own_kind, right_kind], axis=1)
    tile_rows = tiles.reshape(N_SPACE, TILES_DEV, KS)
    checked = jax.checkpoint(pool_gradient)
    grads = lax.map(lambda items: checked(params, items[0], items[1], items[2]), (pool_pos, pool_kind, tile_rows))
    own_grad = grads[:, :, HALF:HALF + A_DEV]
    to_upper = jnp.roll(grads[:, :, :HALF], -1, axis=0)
    to_lower = jnp.roll(grads[:, :, HALF + A_DEV:], 1, axis=0)
    scatter = jax.vmap(lambda block, index, values: block.at[:, index].add(values))
    own_grad = scatter(own_grad, lower, to_lower)
    own_grad = scatter(own_grad, upper, to_upper)
    return own_grad.transpose(1, 0, 2).reshape(3, ATOMS)

def reference(positions, species, ref_forces, send_lists, tile_lists, weights, w_rad, emb_center, emb_other, w_out):
    params = (w_rad, emb_center, emb_other, w_out)

    def total_loss(weights_now):
        loss_sum = jnp.zeros((), jnp.float32)
        force_list = []
        for snapshot in range(N_DP):
            grads = snapshot_gradient(weights_now, positions[snapshot], species[snapshot], send_lists[snapshot], tile_lists[snapshot])
            predicted = -grads
            residual = predicted - ref_forces[snapshot]
            loss_sum = loss_sum + weights[snapshot].astype(jnp.float32) * jnp.sum(residual * residual)
            force_list.append(predicted)
        scale = 3.0 * ATOMS * jnp.sum(weights).astype(jnp.float32)
        return (loss_sum / scale, jnp.stack(force_list))
    (loss, forces), grads = jax.value_and_grad(total_loss, has_aux=True)(params)
    return (forces, loss, grads[0], grads[1], grads[2], grads[3])
```

```python
import functools

import jax
import jax.numpy as jnp
from jax import lax
from jax.experimental import pallas as pl
from jax.experimental.pallas import tpu as pltpu
from jax.sharding import PartitionSpec as P

CUTOFF = 1.0
DOMAIN_WIDTH = 2.0
F32 = jnp.float32
BF16 = jnp.bfloat16
I32 = jnp.int32
LAST = (((1,), (1,)), ((), ()))
LANES = 128
HIGHEST = lax.Precision.HIGHEST


def split(x, parts):
    pieces = []
    for _ in range(parts - 1):
        high = x.astype(BF16).astype(F32)
        pieces.append(high)
        x = x - high
    pieces.append(x.astype(BF16).astype(F32))
    return pieces


def left_operand(x, exact):
    w1, w2, w3 = split(x, 3)
    return jnp.concatenate([w1, w1, w2, w1, w2, w3] + exact, axis=1).astype(BF16)


def right_operand(x, exact):
    b1, b2, b3 = split(x, 3)
    return jnp.concatenate([b1, b2, b1, b3, b2, b1] + exact, axis=0).astype(BF16)


def mxu(a, b):
    return jnp.dot(a, b, preferred_element_type=F32)


def mxu_t(a, b):
    return lax.dot_general(a, b, LAST, preferred_element_type=F32)


def radial_terms(offsets, nb):
    q = jnp.sum(offsets * offsets, axis=0, keepdims=True) / (CUTOFF * CUTOFF)
    scale = float(nb - 1)
    centers = lax.broadcasted_iota(I32, (nb, 1), 0).astype(F32) / scale
    arg = (q - centers) * scale
    basis = jnp.exp(-(arg * arg))
    slope = (-2.0 * scale) * arg * basis
    inner = jnp.maximum(1.0 - q, 0.0)
    return basis, slope, inner * inner, -2.0 * inner


def tables(rad_ref, center_ref, other_ref, out_ref):
    stack = jnp.concatenate([rad_ref[...], center_ref[...], other_ref[...]], axis=0)
    w_row = out_ref[...]
    both = jnp.concatenate([stack, jnp.broadcast_to(w_row, (8, w_row.shape[1]))], axis=0).T
    count = stack.shape[0]
    return stack, w_row, both[:, :count], both[:, count : count + 1]


def one_hot_rows(code_a, code_b, ns, width):
    row = lax.broadcasted_iota(I32, (2 * ns, width), 0).astype(F32)
    code = jnp.where(row < ns, code_a, code_b + float(ns))
    return jnp.where(code == row, 1.0, 0.0)


def prepare(t, slots, own, list_ref, rows_ref, cols_ref, e_ref, bound_ref, feat_ref, count_ref, ns):
    tile = rows_ref.shape[2]
    wide = slots * tile
    entries = [list_ref[t, k] for k in range(slots)]
    safe = [jnp.maximum(c, 0) for c in entries]
    xa = rows_ref[own]
    xb = jnp.concatenate([cols_ref[c] for c in safe], axis=0)
    q = jnp.zeros((wide, tile), F32)
    for i in range(3):
        diff = xb[:, i : i + 1] - xa[i : i + 1, :]
        q = q + diff * diff
    b_row = lax.broadcasted_iota(I32, (tile, tile), 0)
    a_lane = lax.broadcasted_iota(I32, (tile, tile), 1)
    allowed = []
    for c in entries:
        limit = jnp.where(c >= 0, 1.0, 0.0)
        allowed.append(jnp.where((b_row == a_lane) & (c == own), 0.0, limit))
    near = jnp.where(q / (CUTOFF * CUTOFF) < 1.0, jnp.concatenate(allowed, axis=0), 0.0)
    near_b = near.astype(BF16)
    r = lax.broadcasted_iota(I32, (wide, wide), 0)
    c = lax.broadcasted_iota(I32, (wide, wide), 1)
    lower = jnp.where(c < r, 1.0, 0.0).astype(BF16)
    rank = jnp.where(near > 0.0, mxu(lower, near_b) + 1.0, 0.0)
    row2 = lax.broadcasted_iota(I32, (2 * tile, tile), 0)
    col2 = lax.broadcasted_iota(I32, (2 * tile, tile), 1)
    reach = jnp.where(row2 < tile, row2 - 1, row2 - tile)
    below = jnp.where(col2 <= reach, 1.0, 0.0).astype(BF16)
    edges = jnp.sum(mxu_t(below, near_b), axis=1, keepdims=True)
    bound_ref[t] = jnp.broadcast_to(edges, (2 * tile, LANES))
    per_atom = jnp.sum(near, axis=0, keepdims=True)
    before = jnp.where(b_row < a_lane, 1.0, 0.0).astype(BF16)
    start = mxu(jnp.broadcast_to(per_atom, (16, tile)).astype(BF16), before)
    high = jnp.floor(start * (1.0 / 128.0))
    rest = start - 128.0 * high
    which = lax.broadcasted_iota(I32, (16, tile), 0)
    codes = jnp.where(which == 0, high, jnp.where(which == 1, rest, 0.0))
    e_ref[t] = jnp.concatenate([rank, codes], axis=0).astype(BF16)
    count_ref[t] = jnp.sum(per_atom).astype(I32)
    row = lax.broadcasted_iota(I32, (8, tile), 0)
    lane = lax.broadcasted_iota(I32, (8, tile), 1).astype(F32)
    kind_row = row.astype(F32)
    kind = xa[3:4, :]
    first = jnp.where(row < 3, xa, jnp.where(row == 4, lane, jnp.where(row == 6, kind, 0.0)))
    first_kind = jnp.where((row < ns) & (kind == kind_row), 1.0, 0.0)
    parts = [jnp.concatenate([first, first_kind], axis=0)]
    for k in range(slots):
        other = rows_ref[safe[k]]
        kind = other[3:4, :]
        second = jnp.where(
            row < 3, -other, jnp.where(row == 5, lane + float(k * tile), jnp.where(row == 7, kind, 0.0))
        )
        second_kind = jnp.where((row >= ns) & (kind + float(ns) == kind_row), 1.0, 0.0)
        parts.append(jnp.concatenate([second, second_kind], axis=0))
    feat_ref[t] = jnp.concatenate(split(jnp.concatenate(parts, axis=1), 3), axis=0).astype(BF16)


def force_kernel(
    nb, ns, width, list_ref, rows_ref, cols_ref, rad_ref, center_ref, other_ref, out_ref,
    grad_ref, pair_ref, plan_ref,
    e_ref, bound_ref, feat_ref, count_ref, rep_ref, y_ref, r_ref, wb_ref, acc_ref,
):
    tiles_own, slots = list_ref.shape
    tile = rows_ref.shape[2]
    wide_b = slots * tile
    half_tiles = tiles_own // 2
    hid = rad_ref.shape[1]
    for t in range(tiles_own):
        prepare(t, slots, t + half_tiles, list_ref, rows_ref, cols_ref, e_ref, bound_ref, feat_ref, count_ref, ns)
    total = jnp.int32(0)
    for t in range(tiles_own):
        pieces = (count_ref[t] + (width - 1)) // width

        def note(i, carry, t=t, total=total):
            plan_ref[1 + 2 * (total + i)] = t
            plan_ref[2 + 2 * (total + i)] = i * width
            return carry

        lax.fori_loop(0, pieces, note, 0)
        total = total + pieces
    plan_ref[0] = total
    acc_ref[...] = jnp.zeros_like(acc_ref)
    stack, w_row, cols, w_col = tables(rad_ref, center_ref, other_ref, out_ref)
    half_cols = 0.5 * cols
    weighted = 0.5 * w_row * stack[:nb]
    linear = jnp.dot(
        jnp.concatenate([weighted, w_row, jnp.zeros((7, hid), F32)], axis=0), half_cols,
        precision=HIGHEST, preferred_element_type=F32,
    )
    base = jnp.sum(weighted, axis=1, keepdims=True)
    y_rows = jnp.concatenate([half_cols, linear], axis=0)
    a_y = left_operand(y_rows[:, :nb], split(y_rows[:, nb:], 3))
    a_r = left_operand((0.5 * w_col) * cols[:, :nb], [])
    wb_ref[...] = jnp.broadcast_to(w_col, wb_ref.shape)

    def chunk(step, carry):
        t = plan_ref[1 + 2 * step]
        start = plan_ref[2 + 2 * step]
        count = count_ref[t]
        spot = (start + lax.broadcasted_iota(I32, (1, width), 1)).astype(F32)
        bounds = bound_ref[t]
        firsts = []
        for lane in range(0, width, LANES):
            here = spot[:, lane : lane + LANES]
            inside = (here >= bounds[:tile]) & (here < bounds[tile:])
            firsts.append(jnp.where(inside, 1.0, 0.0))
        first = jnp.concatenate(firsts, axis=1).astype(BF16)
        found = mxu(e_ref[t], first)
        valid = spot < count.astype(F32)
        begin = 128.0 * found[wide_b : wide_b + 1] + found[wide_b + 1 : wide_b + 2]
        rank = jnp.where(valid, spot - begin + 1.0, -1.0)
        second = jnp.where(found[:wide_b] == rank, 1.0, 0.0).astype(BF16)
        rep_ref[:tile] = first
        rep_ref[tile:] = second
        pieces = mxu(feat_ref[t], rep_ref[...])
        wide = pieces[:16] + (pieces[16:32] + pieces[32:])
        keep = jnp.where(valid, 1.0, 0.0)
        record = wide[:8]
        row = lax.broadcasted_iota(I32, (8, width), 0)
        pair_ref[step] = jnp.where(row == 3, keep, record)
        kinds = wide[8:16]
        basis, slope, env, denv = radial_terms(wide[0:3], nb)
        x = right_operand(basis, [kinds, kinds, kinds])
        dx = right_operand(slope, [])
        y_ref[...] = mxu(a_y, x)
        r_ref[...] = mxu(a_r, dx)
        s_rows, t_rows = [], []
        for lane in range(0, width, LANES):
            s = jnp.zeros((8, LANES), F32)
            u = jnp.zeros((8, LANES), F32)
            for h in range(0, hid, 8):
                y = y_ref[h : h + 8, lane : lane + LANES]
                r = r_ref[h : h + 8, lane : lane + LANES]
                th = jnp.tanh(y)
                a = y * th
                g = th * (1.0 - a)
                s = s + wb_ref[h : h + 8, :] * a
                u = u + r * g
            s_rows.append(jnp.sum(s, axis=0, keepdims=True))
            t_rows.append(jnp.sum(u, axis=0, keepdims=True))
        lin = y_ref[hid : hid + 16, :]
        s_all = jnp.concatenate(s_rows, axis=1) + lin[8:9]
        t_all = jnp.concatenate(t_rows, axis=1) + jnp.sum(slope * (base + lin[:8]), axis=0, keepdims=True)
        g = keep * (denv * s_all + env * t_all)
        gd = (2.0 * g) * record
        back = mxu_t(jnp.concatenate(split(gd, 3), axis=0).astype(BF16), rep_ref[...])
        acc_ref[t] = acc_ref[t] + (back[0:8] + (back[8:16] + back[16:24]))
        return carry

    lax.fori_loop(0, total, chunk, 0)
    grad_ref[...] = jnp.zeros_like(grad_ref)
    for t in range(tiles_own):
        own = t + half_tiles
        grad_ref[own] = grad_ref[own] + acc_ref[t, :, :tile]
        for k in range(slots):
            entry = jnp.maximum(list_ref[t, k], 0)
            grad_ref[entry] = grad_ref[entry] - acc_ref[t, :, (k + 1) * tile : (k + 2) * tile]


def param_kernel(
    nb, ns, plan_ref, list_ref, v_ref, pair_ref, rad_ref, center_ref, other_ref, out_ref,
    grads_ref,
    va_ref, vb_ref, y_ref, gh_ref, gl_ref, fh_ref, fl_ref, acc_g, acc_f, acc_s, gram_ref,
):
    tiles_own, slots = list_ref.shape
    tile = v_ref.shape[2]
    half_tiles = tiles_own // 2
    hid = rad_ref.shape[1]
    width = pair_ref.shape[2]
    mid = nb + 2 * ns
    acc_g[...] = jnp.zeros_like(acc_g)
    acc_f[...] = jnp.zeros_like(acc_f)
    acc_s[...] = jnp.zeros_like(acc_s)
    gram_ref[...] = jnp.zeros_like(gram_ref)
    for t in range(tiles_own):
        va_ref[t] = jnp.concatenate([v_ref[t + half_tiles], jnp.zeros((8, LANES - tile), F32)], axis=1)
        vb_ref[t] = jnp.concatenate([v_ref[jnp.maximum(list_ref[t, k], 0)] for k in range(slots)], axis=1)
    stack, w_row, cols, w_col = tables(rad_ref, center_ref, other_ref, out_ref)
    half_cols = 0.5 * cols
    a_y = left_operand(half_cols[:, :nb], split(half_cols[:, nb:], 3))

    def chunk(step, carry):
        t = plan_ref[1 + 2 * step]
        record = pair_ref[step]
        offsets = record[0:3]
        keep = record[3:4]
        index_a = jnp.broadcast_to(record[4:5].astype(I32), (8, width))
        index_b = jnp.broadcast_to(record[5:6].astype(I32), (8, width))
        va, vb = va_ref[t], vb_ref[t]
        diffs = []
        for lane in range(0, width, LANES):
            part_a = jnp.take_along_axis(va, index_a[:, lane : lane + LANES], axis=1, mode="promise_in_bounds")
            part_b = jnp.take_along_axis(vb, index_b[:, lane : lane + LANES], axis=1, mode="promise_in_bounds")
            diffs.append(part_a - part_b)
        dv = jnp.concatenate(diffs, axis=1)
        kinds = one_hot_rows(record[6:7], record[7:8], ns, width)
        basis, slope, env, denv = radial_terms(offsets, nb)
        c = (2.0 * keep) * jnp.sum(offsets * dv[0:3], axis=0, keepdims=True)
        alpha = c * denv
        beta_slope = (c * env) * slope
        y_ref[...] = mxu(a_y, right_operand(basis, [kinds, kinds, kinds]))
        for h in range(0, hid, 16):
            s = acc_s[h : h + 16, :]
            for lane in range(0, width, LANES):
                y = y_ref[h : h + 16, lane : lane + LANES]
                th = jnp.tanh(y)
                a = y * th
                u = 1.0 - a
                g = th * u
                f = u - th * g
                s = s + alpha[:, lane : lane + LANES] * a
                g_high = g.astype(BF16)
                f_high = f.astype(BF16)
                gh_ref[h : h + 16, lane : lane + LANES] = g_high
                gl_ref[h : h + 16, lane : lane + LANES] = (g - g_high.astype(F32)).astype(BF16)
                fh_ref[h : h + 16, lane : lane + LANES] = f_high
                fl_ref[h : h + 16, lane : lane + LANES] = (f - f_high.astype(F32)).astype(BF16)
            acc_s[h : h + 16, :] = s
        x = jnp.concatenate([basis, kinds], axis=0)
        one = jnp.ones((8, width), F32)
        g_cols = jnp.concatenate(split(jnp.concatenate([alpha * x, beta_slope], axis=0), 2), axis=0).astype(BF16)
        f_cols = jnp.concatenate(
            split(jnp.concatenate([beta_slope[j : j + 1] * x for j in range(nb)], axis=0), 2), axis=0
        ).astype(BF16)
        x_rows = jnp.concatenate(split(x, 2) + [one, one], axis=0).astype(BF16)
        acc_g[...] += mxu_t(gh_ref[...], g_cols) + mxu_t(gl_ref[...], g_cols)
        acc_f[...] += mxu_t(fh_ref[...], f_cols) + mxu_t(fl_ref[...], f_cols)
        gram_ref[...] += mxu_t(x_rows, g_cols)
        return carry

    lax.fori_loop(0, plan_ref[0], chunk, 0)
    cols_g = mid + nb
    gram = gram_ref[:, :cols_g] + gram_ref[:, cols_g:]
    gram_x = gram[:mid] + gram[mid : 2 * mid]
    gram_one = gram[2 * mid : 2 * mid + 1]
    curved = acc_g[:, :cols_g] + acc_g[:, cols_g:]
    spread = jnp.dot(half_cols, gram_x, precision=HIGHEST, preferred_element_type=F32)
    first = 0.5 * (gram_one + spread + curved)
    sharp = 0.5 * (acc_f[:, : nb * mid] + acc_f[:, nb * mid :])
    d = first[:, :mid]
    for j in range(nb):
        d = d + cols[:, j : j + 1] * sharp[:, j * mid : (j + 1) * mid]
    slope_part = first[:, mid:]
    grad_rad = w_col * (d[:, :nb] + slope_part)
    grad_tables = w_col * d[:, nb:]
    grad_out = (
        jnp.sum(acc_s[...], axis=1, keepdims=True)
        + jnp.sum(half_cols * gram_one[:, :mid], axis=1, keepdims=True)
        + jnp.sum(slope_part * cols[:, :nb], axis=1, keepdims=True)
    )
    grads_ref[...] = jnp.concatenate([grad_rad, grad_tables, grad_out], axis=1)


SMEM_SPEC = pl.BlockSpec(memory_space=pltpu.SMEM)
VMEM_SPEC = pl.BlockSpec(memory_space=pltpu.VMEM)


def pool_force(tile_list, rows, cols, params, width):
    tiles, _, tile = rows.shape
    own, slots = tile_list.shape
    rad, center = params[0], params[1]
    nb, hid = rad.shape
    ns = center.shape[0]
    most = own * (-(-slots * tile * tile // width))
    wide_b = slots * tile
    return pl.pallas_call(
        functools.partial(force_kernel, nb, ns, width),
        out_shape=(
            jax.ShapeDtypeStruct((tiles, 8, tile), F32),
            jax.ShapeDtypeStruct((most, 8, width), F32),
            jax.ShapeDtypeStruct((2 * most + 1,), I32),
        ),
        in_specs=[SMEM_SPEC] + [VMEM_SPEC] * 6,
        out_specs=(VMEM_SPEC, VMEM_SPEC, SMEM_SPEC),
        scratch_shapes=[
            pltpu.VMEM((own, wide_b + 16, tile), BF16),
            pltpu.VMEM((own, 2 * tile, LANES), F32),
            pltpu.VMEM((own, 48, tile + wide_b), BF16),
            pltpu.SMEM((own,), I32),
            pltpu.VMEM((tile + wide_b, width), BF16),
            pltpu.VMEM((hid + 16, width), F32),
            pltpu.VMEM((hid, width), F32),
            pltpu.VMEM((hid, LANES), F32),
            pltpu.VMEM((own, 8, tile + wide_b), F32),
        ],
        compiler_params=pltpu.CompilerParams(vmem_limit_bytes=48 * 1024 * 1024),
        name="pool_force",
    )(tile_list, rows, cols, *params)


def pool_params(plan, tile_list, pool_v, pairs, params):
    own = tile_list.shape[0]
    width = pairs.shape[2]
    rad, center = params[0], params[1]
    nb, hid = rad.shape
    ns = center.shape[0]
    mid = nb + 2 * ns
    return pl.pallas_call(
        functools.partial(param_kernel, nb, ns),
        out_shape=jax.ShapeDtypeStruct((hid, mid + 1), F32),
        in_specs=[SMEM_SPEC, SMEM_SPEC] + [VMEM_SPEC] * 6,
        out_specs=VMEM_SPEC,
        scratch_shapes=[
            pltpu.VMEM((own, 8, LANES), F32),
            pltpu.VMEM((own, 8, LANES), F32),
            pltpu.VMEM((hid, width), F32),
            pltpu.VMEM((hid, width), BF16),
            pltpu.VMEM((hid, width), BF16),
            pltpu.VMEM((hid, width), BF16),
            pltpu.VMEM((hid, width), BF16),
            pltpu.VMEM((hid, 2 * (mid + nb)), F32),
            pltpu.VMEM((hid, 2 * nb * mid), F32),
            pltpu.VMEM((hid, LANES), F32),
            pltpu.VMEM((2 * mid + 16, 2 * (mid + nb)), F32),
        ],
        compiler_params=pltpu.CompilerParams(vmem_limit_bytes=48 * 1024 * 1024),
        name="pool_params",
    )(plan, tile_list, pool_v, pairs, *params)


def exchange(to_lower, to_upper):
    count = lax.axis_size("space")
    up = [(i, (i + 1) % count) for i in range(count)]
    down = [(j, i) for i, j in up]
    return lax.ppermute(to_upper, "space", up), lax.ppermute(to_lower, "space", down)


def tiled(rows, tile):
    return rows.reshape(rows.shape[0], -1, tile).transpose(1, 0, 2)


def body(positions, species, ref_forces, send_lists, tile_lists, weights, w_rad, emb_center, emb_other, w_out):
    nb, hid = w_rad.shape
    ns = emb_center.shape[0]
    own_pos = positions[0]
    tile_list = tile_lists[0]
    atoms = own_pos.shape[1]
    half = atoms // 2
    tile = atoms // tile_list.shape[0]
    params = (w_rad, emb_center, emb_other, w_out[None])
    order = send_lists[0].reshape(1, atoms)
    pick = (lax.broadcasted_iota(I32, (atoms, atoms), 0) == order).astype(F32)
    own = jnp.concatenate([own_pos, species.astype(F32)], axis=0)
    sent = jnp.dot(own, pick, precision=HIGHEST)
    left, right = exchange(sent[:, :half], sent[:, half:])
    shift = jnp.zeros((own.shape[0], 1), F32).at[0].set(DOMAIN_WIDTH)
    pool = jnp.concatenate([left - shift, own, right + shift], axis=1)
    rows = tiled(jnp.concatenate([pool, jnp.zeros_like(pool)], axis=0), tile)
    tile_grad, pairs, plan = pool_force(tile_list, rows, rows.transpose(0, 2, 1), params, 4 * LANES)
    pool_grad = tile_grad.transpose(1, 0, 2).reshape(8, -1)[:3]
    from_lower, from_upper = exchange(pool_grad[:, :half], pool_grad[:, half + atoms :])
    returned = jnp.concatenate([from_lower, from_upper], axis=1)
    atom_grad = pool_grad[:, half : half + atoms] + lax.dot_general(returned, pick, LAST, precision=HIGHEST)
    forces = -atom_grad
    residual = forces - ref_forces[0]
    weight = weights[0].astype(F32)
    adjoint = -2.0 * weight * residual
    sent_adjoint = jnp.dot(adjoint, pick, precision=HIGHEST)
    left_v, right_v = exchange(sent_adjoint[:, :half], sent_adjoint[:, half:])
    pool_v = jnp.concatenate([left_v, adjoint, right_v], axis=1)
    pool_v = tiled(jnp.concatenate([pool_v, jnp.zeros((5, pool.shape[1]), F32)], axis=0), tile)
    grads = pool_params(plan, tile_list, pool_v, pairs, params)
    local_loss = weight * jnp.sum(residual * residual)
    extra = jnp.stack([local_loss, weight])
    extra = jnp.concatenate([extra, jnp.zeros((hid - 2,), F32)])[None]
    summed = lax.psum(jnp.concatenate([grads.T, extra], axis=0), ("dp", "space"))
    domains = lax.axis_size("space")
    weight_total = summed[-1, 1] / domains
    summed = summed * (1.0 / (3.0 * atoms * domains * weight_total))
    return (
        forces[None],
        summed[-1, 0],
        summed[:nb],
        summed[nb : nb + ns],
        summed[nb + ns : nb + 2 * ns],
        summed[nb + 2 * ns],
    )


def solution(mesh):
    return jax.shard_map(
        body,
        mesh=mesh,
        in_specs=(
            P("dp", None, "space"),
            P("dp", "space"),
            P("dp", None, "space"),
            P("dp", "space", None),
            P("dp", "space", None),
            P("dp"),
            P(),
            P(),
            P(),
            P(),
        ),
        out_specs=(P("dp", None, "space"), P(), P(), P(), P(), P()),
        check_vma=False,
    )
```

```python
import functools

import jax
import jax.numpy as jnp
from jax import lax
from jax.experimental import pallas as pl
from jax.experimental.pallas import tpu as pltpu
from jax.sharding import PartitionSpec as P

CUTOFF = 1.0
DOMAIN_WIDTH = 2.0
F32 = jnp.float32
BF16 = jnp.bfloat16
I32 = jnp.int32
LAST = (((1,), (1,)), ((), ()))
LANES = 128
HIGHEST = lax.Precision.HIGHEST


def split(x, parts):
    pieces = []
    for _ in range(parts - 1):
        high = x.astype(BF16).astype(F32)
        pieces.append(high)
        x = x - high
    pieces.append(x.astype(BF16).astype(F32))
    return pieces


def left_operand(x, exact):
    w1, w2, w3 = split(x, 3)
    return jnp.concatenate([w1, w1, w2, w1, w2, w3] + exact, axis=1).astype(BF16)


def right_operand(x, exact):
    b1, b2, b3 = split(x, 3)
    return jnp.concatenate([b1, b2, b1, b3, b2, b1] + exact, axis=0).astype(BF16)


def mxu(a, b):
    return jnp.dot(a, b, preferred_element_type=F32)


def mxu_t(a, b):
    return lax.dot_general(a, b, LAST, preferred_element_type=F32)


def radial_terms(offsets, nb):
    q = jnp.sum(offsets * offsets, axis=0, keepdims=True) / (CUTOFF * CUTOFF)
    scale = float(nb - 1)
    centers = lax.broadcasted_iota(I32, (nb, 1), 0).astype(F32) / scale
    arg = (q - centers) * scale
    basis = jnp.exp(-(arg * arg))
    slope = (-2.0 * scale) * arg * basis
    inner = jnp.maximum(1.0 - q, 0.0)
    return basis, slope, inner * inner, -2.0 * inner


def tables(rad_ref, center_ref, other_ref, out_ref):
    stack = jnp.concatenate([rad_ref[...], center_ref[...], other_ref[...]], axis=0)
    w_row = out_ref[...]
    both = jnp.concatenate([stack, jnp.broadcast_to(w_row, (8, w_row.shape[1]))], axis=0).T
    count = stack.shape[0]
    return stack, w_row, both[:, :count], both[:, count : count + 1]


def one_hot_rows(code_a, code_b, ns, width):
    row = lax.broadcasted_iota(I32, (2 * ns, width), 0).astype(F32)
    code = jnp.where(row < ns, code_a, code_b + float(ns))
    return jnp.where(code == row, 1.0, 0.0)


def prepare(t, slots, own, list_ref, rows_ref, cols_ref, e_ref, bound_ref, feat_ref, count_ref, ns):
    tile = rows_ref.shape[2]
    wide = slots * tile
    entries = [list_ref[t, k] for k in range(slots)]
    safe = [jnp.maximum(c, 0) for c in entries]
    xa = rows_ref[own]
    xb = jnp.concatenate([cols_ref[c] for c in safe], axis=0)
    q = jnp.zeros((wide, tile), F32)
    for i in range(3):
        diff = xb[:, i : i + 1] - xa[i : i + 1, :]
        q = q + diff * diff
    b_row = lax.broadcasted_iota(I32, (tile, tile), 0)
    a_lane = lax.broadcasted_iota(I32, (tile, tile), 1)
    allowed = []
    for c in entries:
        limit = jnp.where(c >= 0, 1.0, 0.0)
        allowed.append(jnp.where((b_row == a_lane) & (c == own), 0.0, limit))
    near = jnp.where(q / (CUTOFF * CUTOFF) < 1.0, jnp.concatenate(allowed, axis=0), 0.0)
    near_b = near.astype(BF16)
    r = lax.broadcasted_iota(I32, (wide, wide), 0)
    c = lax.broadcasted_iota(I32, (wide, wide), 1)
    lower = jnp.where(c < r, 1.0, 0.0).astype(BF16)
    rank = jnp.where(near > 0.0, mxu(lower, near_b) + 1.0, 0.0)
    row2 = lax.broadcasted_iota(I32, (2 * tile, tile), 0)
    col2 = lax.broadcasted_iota(I32, (2 * tile, tile), 1)
    reach = jnp.where(row2 < tile, row2 - 1, row2 - tile)
    below = jnp.where(col2 <= reach, 1.0, 0.0).astype(BF16)
    edges = jnp.sum(mxu_t(below, near_b), axis=1, keepdims=True)
    bound_ref[t] = jnp.broadcast_to(edges, (2 * tile, LANES))
    per_atom = jnp.sum(near, axis=0, keepdims=True)
    before = jnp.where(b_row < a_lane, 1.0, 0.0).astype(BF16)
    start = mxu(jnp.broadcast_to(per_atom, (16, tile)).astype(BF16), before)
    high = jnp.floor(start * (1.0 / 128.0))
    rest = start - 128.0 * high
    which = lax.broadcasted_iota(I32, (16, tile), 0)
    codes = jnp.where(which == 0, high, jnp.where(which == 1, rest, 0.0))
    e_ref[t] = jnp.concatenate([rank, codes], axis=0).astype(BF16)
    count_ref[t] = jnp.sum(per_atom).astype(I32)
    row = lax.broadcasted_iota(I32, (8, tile), 0)
    lane = lax.broadcasted_iota(I32, (8, tile), 1).astype(F32)
    kind_row = row.astype(F32)
    kind = xa[3:4, :]
    first = jnp.where(row < 3, xa, jnp.where(row == 4, lane, jnp.where(row == 6, kind, 0.0)))
    first_kind = jnp.where((row < ns) & (kind == kind_row), 1.0, 0.0)
    parts = [jnp.concatenate([first, first_kind], axis=0)]
    for k in range(slots):
        other = rows_ref[safe[k]]
        kind = other[3:4, :]
        second = jnp.where(
            row < 3, -other, jnp.where(row == 5, lane + float(k * tile), jnp.where(row == 7, kind, 0.0))
        )
        second_kind = jnp.where((row >= ns) & (kind + float(ns) == kind_row), 1.0, 0.0)
        parts.append(jnp.concatenate([second, second_kind], axis=0))
    feat_ref[t] = jnp.concatenate(split(jnp.concatenate(parts, axis=1), 3), axis=0).astype(BF16)


def selection(order_ref, k, atoms):
    count = order_ref.shape[2]
    row = lax.broadcasted_iota(I32, (atoms, count), 0)
    return jnp.where(row == order_ref[0, k : k + 1, :], 1.0, 0.0).astype(BF16)


def stacked(x):
    return jnp.concatenate(split(x, 3), axis=0).astype(BF16)


def unstacked(x):
    rows = x.shape[0] // 3
    return x[:rows] + (x[rows : 2 * rows] + x[2 * rows :])


def pad_rows(parts, width):
    count = sum(p.shape[0] for p in parts)
    return jnp.concatenate(parts + [jnp.zeros((8 - count, width), F32)], axis=0)


def fill_pool(pos_ref, spec_ref, lower_ref, upper_ref, rows_ref, cols_ref):
    tiles, _, tile = rows_ref.shape
    half = lower_ref.shape[1]
    atoms = pos_ref.shape[2]
    own = pad_rows([pos_ref[0], spec_ref[...].astype(F32)], atoms)
    row = lax.broadcasted_iota(I32, (8, half), 0)
    shift = jnp.where(row == 0, DOMAIN_WIDTH, 0.0)
    left = jnp.where(row < 4, lower_ref[...] - shift, 0.0)
    right = jnp.where(row < 4, upper_ref[...] + shift, 0.0)
    pool = jnp.concatenate([left, own, right], axis=1)
    turned = pool.T
    for i in range(tiles):
        rows_ref[i] = pool[:, i * tile : (i + 1) * tile]
        cols_ref[i] = turned[i * tile : (i + 1) * tile, :]


def force_kernel(
    nb, ns, width, list_ref, pos_ref, spec_ref, order_ref, lower_ref, upper_ref,
    rad_ref, center_ref, other_ref, out_ref,
    own_ref, to_lower_ref, to_upper_ref, pair_ref, plan_ref,
    rows_ref, cols_ref, grad_ref, e_ref, bound_ref, feat_ref, count_ref, rep_ref, y_ref, r_ref, wb_ref, acc_ref,
):
    list_ref = list_ref.at[0]
    tiles_own, slots = list_ref.shape
    tile = rows_ref.shape[2]
    fill_pool(pos_ref, spec_ref, lower_ref, upper_ref, rows_ref, cols_ref)
    wide_b = slots * tile
    half_tiles = tiles_own // 2
    hid = rad_ref.shape[1]
    for t in range(tiles_own):
        prepare(t, slots, t + half_tiles, list_ref, rows_ref, cols_ref, e_ref, bound_ref, feat_ref, count_ref, ns)
    total = jnp.int32(0)
    for t in range(tiles_own):
        pieces = (count_ref[t] + (width - 1)) // width

        def note(i, carry, t=t, total=total):
            plan_ref[1 + 2 * (total + i)] = t
            plan_ref[2 + 2 * (total + i)] = i * width
            return carry

        lax.fori_loop(0, pieces, note, 0)
        total = total + pieces
    plan_ref[0] = total
    acc_ref[...] = jnp.zeros_like(acc_ref)
    stack, w_row, cols, w_col = tables(rad_ref, center_ref, other_ref, out_ref)
    half_cols = 0.5 * cols
    weighted = 0.5 * w_row * stack[:nb]
    linear = jnp.dot(
        jnp.concatenate([weighted, w_row, jnp.zeros((7, hid), F32)], axis=0), half_cols,
        precision=HIGHEST, preferred_element_type=F32,
    )
    base = jnp.sum(weighted, axis=1, keepdims=True)
    y_rows = jnp.concatenate([half_cols, linear], axis=0)
    a_y = left_operand(y_rows[:, :nb], split(y_rows[:, nb:], 3))
    a_r = left_operand((0.5 * w_col) * cols[:, :nb], [])
    wb_ref[...] = jnp.broadcast_to(w_col, wb_ref.shape)

    def chunk(step, carry):
        t = plan_ref[1 + 2 * step]
        start = plan_ref[2 + 2 * step]
        count = count_ref[t]
        spot = (start + lax.broadcasted_iota(I32, (1, width), 1)).astype(F32)
        bounds = bound_ref[t]
        firsts = []
        for lane in range(0, width, LANES):
            here = spot[:, lane : lane + LANES]
            inside = (here >= bounds[:tile]) & (here < bounds[tile:])
            firsts.append(jnp.where(inside, 1.0, 0.0))
        first = jnp.concatenate(firsts, axis=1).astype(BF16)
        found = mxu(e_ref[t], first)
        valid = spot < count.astype(F32)
        begin = 128.0 * found[wide_b : wide_b + 1] + found[wide_b + 1 : wide_b + 2]
        rank = jnp.where(valid, spot - begin + 1.0, -1.0)
        second = jnp.where(found[:wide_b] == rank, 1.0, 0.0).astype(BF16)
        rep_ref[:tile] = first
        rep_ref[tile:] = second
        pieces = mxu(feat_ref[t], rep_ref[...])
        wide = pieces[:16] + (pieces[16:32] + pieces[32:])
        keep = jnp.where(valid, 1.0, 0.0)
        record = wide[:8]
        row = lax.broadcasted_iota(I32, (8, width), 0)
        pair_ref[step] = jnp.where(row == 3, keep, record)
        kinds = wide[8:16]
        basis, slope, env, denv = radial_terms(wide[0:3], nb)
        x = right_operand(basis, [kinds, kinds, kinds])
        dx = right_operand(slope, [])
        y_ref[...] = mxu(a_y, x)
        r_ref[...] = mxu(a_r, dx)
        s_rows, t_rows = [], []
        for lane in range(0, width, LANES):
            s = jnp.zeros((8, LANES), F32)
            u = jnp.zeros((8, LANES), F32)
            for h in range(0, hid, 8):
                y = y_ref[h : h + 8, lane : lane + LANES]
                r = r_ref[h : h + 8, lane : lane + LANES]
                th = jnp.tanh(y)
                a = y * th
                g = th * (1.0 - a)
                s = s + wb_ref[h : h + 8, :] * a
                u = u + r * g
            s_rows.append(jnp.sum(s, axis=0, keepdims=True))
            t_rows.append(jnp.sum(u, axis=0, keepdims=True))
        lin = y_ref[hid : hid + 16, :]
        s_all = jnp.concatenate(s_rows, axis=1) + lin[8:9]
        t_all = jnp.concatenate(t_rows, axis=1) + jnp.sum(slope * (base + lin[:8]), axis=0, keepdims=True)
        g = keep * (denv * s_all + env * t_all)
        gd = (2.0 * g) * record
        back = mxu_t(jnp.concatenate(split(gd, 3), axis=0).astype(BF16), rep_ref[...])
        acc_ref[t] = acc_ref[t] + (back[0:8] + (back[8:16] + back[16:24]))
        return carry

    lax.fori_loop(0, total, chunk, 0)
    grad_ref[...] = jnp.zeros_like(grad_ref)
    for t in range(tiles_own):
        own = t + half_tiles
        grad_ref[own] = grad_ref[own] + acc_ref[t, :, :tile]
        for k in range(slots):
            entry = jnp.maximum(list_ref[t, k], 0)
            grad_ref[entry] = grad_ref[entry] - acc_ref[t, :, (k + 1) * tile : (k + 2) * tile]
    whole = jnp.concatenate([grad_ref[i] for i in range(grad_ref.shape[0])], axis=1)
    atoms = pos_ref.shape[2]
    half = atoms // 2
    own_grad = whole[:, half : half + atoms]
    own_ref[...] = own_grad
    pieces = stacked(own_grad)
    for k, ref in ((0, to_lower_ref), (1, to_upper_ref)):
        sent = unstacked(mxu(pieces, selection(order_ref, k, atoms)))
        ghost = whole[:, :half] if k == 0 else whole[:, half + atoms :]
        ref[...] = pad_rows([sent[0:3], ghost[0:3]], half)


def finish_forces(
    weight, order_ref, target_ref, lower_ref, upper_ref, own_ref,
    to_lower_ref, to_upper_ref, from_lower_ref, from_upper_ref, forces_ref, v_ref,
):
    tiles, _, tile = v_ref.shape
    atoms = own_ref.shape[1]
    total = own_ref[0:3, :]
    for k, ref in ((0, from_lower_ref), (1, from_upper_ref)):
        total = total + unstacked(mxu_t(stacked(ref[...]), selection(order_ref, k, atoms)))[3:6]
    forces_ref[0] = -total
    miss = total + target_ref[0]
    left = to_lower_ref[3:6, :] + from_lower_ref[0:3, :] + lower_ref[4:7, :]
    right = to_upper_ref[3:6, :] + from_upper_ref[0:3, :] + upper_ref[4:7, :]
    scaled = (2.0 * weight) * jnp.concatenate([left, miss, right], axis=1)
    scaled = pad_rows([scaled], scaled.shape[1])
    for i in range(tiles):
        v_ref[i] = scaled[:, i * tile : (i + 1) * tile]
    return weight * jnp.sum(miss * miss)


def param_kernel(
    nb, ns, plan_ref, list_ref, weight_ref, order_ref, target_ref, lower_ref, upper_ref, own_ref,
    to_lower_ref, to_upper_ref, from_lower_ref, from_upper_ref, pair_ref, rad_ref, center_ref, other_ref, out_ref,
    forces_ref, grads_ref,
    v_ref, va_ref, vb_ref, y_ref, gh_ref, gl_ref, fh_ref, fl_ref, acc_g, acc_f, acc_s, gram_ref,
):
    list_ref = list_ref.at[0]
    tiles_own, slots = list_ref.shape
    tile = v_ref.shape[2]
    half_tiles = tiles_own // 2
    hid = rad_ref.shape[1]
    width = pair_ref.shape[2]
    weight = weight_ref[0].astype(F32)
    loss = finish_forces(
        weight, order_ref, target_ref, lower_ref, upper_ref, own_ref,
        to_lower_ref, to_upper_ref, from_lower_ref, from_upper_ref, forces_ref, v_ref,
    )
    mid = nb + 2 * ns
    acc_g[...] = jnp.zeros_like(acc_g)
    acc_f[...] = jnp.zeros_like(acc_f)
    acc_s[...] = jnp.zeros_like(acc_s)
    gram_ref[...] = jnp.zeros_like(gram_ref)
    for t in range(tiles_own):
        va_ref[t] = jnp.concatenate([v_ref[t + half_tiles], jnp.zeros((8, LANES - tile), F32)], axis=1)
        vb_ref[t] = jnp.concatenate([v_ref[jnp.maximum(list_ref[t, k], 0)] for k in range(slots)], axis=1)
    stack, w_row, cols, w_col = tables(rad_ref, center_ref, other_ref, out_ref)
    half_cols = 0.5 * cols
    a_y = left_operand(half_cols[:, :nb], split(half_cols[:, nb:], 3))

    def chunk(step, carry):
        t = plan_ref[1 + 2 * step]
        record = pair_ref[step]
        offsets = record[0:3]
        keep = record[3:4]
        index_a = jnp.broadcast_to(record[4:5].astype(I32), (8, width))
        index_b = jnp.broadcast_to(record[5:6].astype(I32), (8, width))
        va, vb = va_ref[t], vb_ref[t]
        diffs = []
        for lane in range(0, width, LANES):
            part_a = jnp.take_along_axis(va, index_a[:, lane : lane + LANES], axis=1, mode="promise_in_bounds")
            part_b = jnp.take_along_axis(vb, index_b[:, lane : lane + LANES], axis=1, mode="promise_in_bounds")
            diffs.append(part_a - part_b)
        dv = jnp.concatenate(diffs, axis=1)
        kinds = one_hot_rows(record[6:7], record[7:8], ns, width)
        basis, slope, env, denv = radial_terms(offsets, nb)
        c = (2.0 * keep) * jnp.sum(offsets * dv[0:3], axis=0, keepdims=True)
        alpha = c * denv
        beta_slope = (c * env) * slope
        y_ref[...] = mxu(a_y, right_operand(basis, [kinds, kinds, kinds]))
        for h in range(0, hid, 16):
            s = acc_s[h : h + 16, :]
            for lane in range(0, width, LANES):
                y = y_ref[h : h + 16, lane : lane + LANES]
                th = jnp.tanh(y)
                a = y * th
                u = 1.0 - a
                g = th * u
                f = u - th * g
                s = s + alpha[:, lane : lane + LANES] * a
                g_high = g.astype(BF16)
                f_high = f.astype(BF16)
                gh_ref[h : h + 16, lane : lane + LANES] = g_high
                gl_ref[h : h + 16, lane : lane + LANES] = (g - g_high.astype(F32)).astype(BF16)
                fh_ref[h : h + 16, lane : lane + LANES] = f_high
                fl_ref[h : h + 16, lane : lane + LANES] = (f - f_high.astype(F32)).astype(BF16)
            acc_s[h : h + 16, :] = s
        x = jnp.concatenate([basis, kinds], axis=0)
        one = jnp.ones((8, width), F32)
        g_cols = jnp.concatenate(split(jnp.concatenate([alpha * x, beta_slope], axis=0), 2), axis=0).astype(BF16)
        f_cols = jnp.concatenate(
            split(jnp.concatenate([beta_slope[j : j + 1] * x for j in range(nb)], axis=0), 2), axis=0
        ).astype(BF16)
        x_rows = jnp.concatenate(split(x, 2) + [one, one], axis=0).astype(BF16)
        acc_g[...] += mxu_t(gh_ref[...], g_cols) + mxu_t(gl_ref[...], g_cols)
        acc_f[...] += mxu_t(fh_ref[...], f_cols) + mxu_t(fl_ref[...], f_cols)
        gram_ref[...] += mxu_t(x_rows, g_cols)
        return carry

    lax.fori_loop(0, plan_ref[0], chunk, 0)
    cols_g = mid + nb
    gram = gram_ref[:, :cols_g] + gram_ref[:, cols_g:]
    gram_x = gram[:mid] + gram[mid : 2 * mid]
    gram_one = gram[2 * mid : 2 * mid + 1]
    curved = acc_g[:, :cols_g] + acc_g[:, cols_g:]
    spread = jnp.dot(half_cols, gram_x, precision=HIGHEST, preferred_element_type=F32)
    first = 0.5 * (gram_one + spread + curved)
    sharp = 0.5 * (acc_f[:, : nb * mid] + acc_f[:, nb * mid :])
    d = first[:, :mid]
    for j in range(nb):
        d = d + cols[:, j : j + 1] * sharp[:, j * mid : (j + 1) * mid]
    slope_part = first[:, mid:]
    grad_rad = w_col * (d[:, :nb] + slope_part)
    grad_tables = w_col * d[:, nb:]
    grad_out = (
        jnp.sum(acc_s[...], axis=1, keepdims=True)
        + jnp.sum(half_cols * gram_one[:, :mid], axis=1, keepdims=True)
        + jnp.sum(slope_part * cols[:, :nb], axis=1, keepdims=True)
    )
    spare = jnp.zeros((hid, LANES - mid - 1), F32)
    turned = jnp.concatenate([grad_rad, grad_tables, grad_out, spare], axis=1).T
    rows = grads_ref.shape[0]
    row = lax.broadcasted_iota(I32, (rows, hid), 0)
    lane = lax.broadcasted_iota(I32, (rows, hid), 1)
    extra = jnp.where(lane == 0, loss, jnp.where(lane == 1, weight, 0.0))
    grads_ref[...] = jnp.where(row == mid + 1, extra, turned[:rows])


SMEM_SPEC = pl.BlockSpec(memory_space=pltpu.SMEM)
VMEM_SPEC = pl.BlockSpec(memory_space=pltpu.VMEM)
MESH = pl.DeviceIdType.MESH
VMEM_BYTES = 48 * 1024 * 1024


def swap(to_lower, to_upper, from_lower, from_upper, sems):
    me, count = lax.axis_index("space"), lax.axis_size("space")
    group = lax.axis_index("dp")
    upper, lower = lax.rem(me + 1, count), lax.rem(me + count - 1, count)
    up = pltpu.make_async_remote_copy(
        src_ref=to_upper, dst_ref=from_lower, send_sem=sems.at[0], recv_sem=sems.at[1],
        device_id=(group, upper), device_id_type=MESH,
    )
    down = pltpu.make_async_remote_copy(
        src_ref=to_lower, dst_ref=from_upper, send_sem=sems.at[2], recv_sem=sems.at[3],
        device_id=(group, lower), device_id_type=MESH,
    )
    return up, down


def greet():
    me, count = lax.axis_index("space"), lax.axis_size("space")
    group = lax.axis_index("dp")
    barrier = pltpu.get_barrier_semaphore()
    for other in (lax.rem(me + 1, count), lax.rem(me + count - 1, count)):
        pl.semaphore_signal(barrier, inc=1, device_id=(group, other), device_id_type=MESH)
    return barrier


def face_kernel(
    pos_ref, spec_ref, target_ref, order_ref, lower_ref, upper_ref,
    to_lower, to_upper, from_lower, from_upper, sems,
):
    barrier = greet()
    atoms = pos_ref.shape[2]
    pieces = stacked(pad_rows([pos_ref[0], spec_ref[...].astype(F32), target_ref[0]], atoms))
    to_lower[...] = unstacked(mxu(pieces, selection(order_ref, 0, atoms)))
    to_upper[...] = unstacked(mxu(pieces, selection(order_ref, 1, atoms)))
    pl.semaphore_wait(barrier, 2)
    up, down = swap(to_lower, to_upper, from_lower, from_upper, sems)
    up.start()
    down.start()
    up.wait()
    down.wait()
    lower_ref[...] = from_lower[...]
    upper_ref[...] = from_upper[...]


def ghost_kernel(to_lower, to_upper, lower_ref, upper_ref, from_lower, from_upper, sems):
    barrier = greet()
    pl.semaphore_wait(barrier, 2)
    up, down = swap(to_lower, to_upper, from_lower, from_upper, sems)
    up.start()
    down.start()
    up.wait()
    down.wait()
    lower_ref[...] = from_lower[...]
    upper_ref[...] = from_upper[...]


def sum_kernel(x_ref, out_ref, near, part, far, near_send, near_recv, far_send, far_recv):
    group, me = lax.axis_index("dp"), lax.axis_index("space")
    groups, count = lax.axis_size("dp"), lax.axis_size("space")
    barrier = pltpu.get_barrier_semaphore()
    others = [(lax.rem(group + k, groups), me) for k in range(1, groups)]
    others += [(group, lax.rem(me + k, count)) for k in range(1, count)]
    for other in others:
        pl.semaphore_signal(barrier, inc=1, device_id=other, device_id_type=MESH)
    pl.semaphore_wait(barrier, len(others))

    def share(source, slots, send, recv, spot, peers):
        copies = []
        for k, other in enumerate(peers):
            copies.append(
                pltpu.make_async_remote_copy(
                    src_ref=source, dst_ref=slots.at[spot], send_sem=send.at[k], recv_sem=recv.at[k],
                    device_id=other, device_id_type=MESH,
                )
            )
            copies[-1].start()
        slots[spot] = source[...]
        for copy in copies:
            copy.wait()
        total = slots[0]
        for k in range(1, len(peers) + 1):
            total = total + slots[k]
        return total

    part[...] = share(x_ref, near, near_send, near_recv, group, others[: groups - 1])
    out_ref[...] = share(part, far, far_send, far_recv, me, others[groups - 1 :])


def final_kernel(nb, ns, atoms, domains, sum_ref, loss_ref, rad_ref, center_ref, other_ref, out_ref):
    last = nb + 2 * ns
    weight_total = sum_ref[last + 1 : last + 2, 1:2] / domains
    scale = 1.0 / (3.0 * atoms * domains * weight_total)
    loss_ref[...] = sum_ref[last + 1 : last + 2, 0:1] * scale
    rad_ref[...] = sum_ref[:nb] * scale
    center_ref[...] = sum_ref[nb : nb + ns] * scale
    other_ref[...] = sum_ref[nb + ns : last] * scale
    out_ref[...] = sum_ref[last : last + 1] * scale


def pool_force(tile_list, positions, species, order, lower, upper, params, width):
    atoms = positions.shape[2]
    half = atoms // 2
    _, own, slots = tile_list.shape
    tile = atoms // own
    tiles = 2 * own
    rad, center = params[0], params[1]
    nb, hid = rad.shape
    ns = center.shape[0]
    most = own * (-(-slots * tile * tile // width))
    wide_b = slots * tile
    return pl.pallas_call(
        functools.partial(force_kernel, nb, ns, width),
        out_shape=(
            jax.ShapeDtypeStruct((8, atoms), F32),
            jax.ShapeDtypeStruct((8, half), F32),
            jax.ShapeDtypeStruct((8, half), F32),
            jax.ShapeDtypeStruct((most, 8, width), F32),
            jax.ShapeDtypeStruct((2 * most + 1,), I32),
        ),
        in_specs=[SMEM_SPEC] + [VMEM_SPEC] * 9,
        out_specs=(VMEM_SPEC,) * 4 + (SMEM_SPEC,),
        scratch_shapes=[
            pltpu.VMEM((tiles, 8, tile), F32),
            pltpu.VMEM((tiles, tile, 8), F32),
            pltpu.VMEM((tiles, 8, tile), F32),
            pltpu.VMEM((own, wide_b + 16, tile), BF16),
            pltpu.VMEM((own, 2 * tile, LANES), F32),
            pltpu.VMEM((own, 48, tile + wide_b), BF16),
            pltpu.SMEM((own,), I32),
            pltpu.VMEM((tile + wide_b, width), BF16),
            pltpu.VMEM((hid + 16, width), F32),
            pltpu.VMEM((hid, width), F32),
            pltpu.VMEM((hid, LANES), F32),
            pltpu.VMEM((own, 8, tile + wide_b), F32),
        ],
        compiler_params=pltpu.CompilerParams(vmem_limit_bytes=VMEM_BYTES),
        name="pool_force",
    )(tile_list, positions, species, order, lower, upper, *params)


def pool_params(plan, tile_list, weights, order, targets, ghosts, sums, pairs, params):
    _, own, slots = tile_list.shape
    atoms = targets.shape[2]
    tile = atoms // own
    width = pairs.shape[2]
    rad, center = params[0], params[1]
    nb, hid = rad.shape
    ns = center.shape[0]
    mid = nb + 2 * ns
    rows = -(-(mid + 2) // 8) * 8
    return pl.pallas_call(
        functools.partial(param_kernel, nb, ns),
        out_shape=(
            jax.ShapeDtypeStruct(targets.shape, F32),
            jax.ShapeDtypeStruct((rows, hid), F32),
        ),
        in_specs=[SMEM_SPEC] * 3 + [VMEM_SPEC] * 14,
        out_specs=(VMEM_SPEC,) * 2,
        scratch_shapes=[
            pltpu.VMEM((2 * own, 8, tile), F32),
            pltpu.VMEM((own, 8, LANES), F32),
            pltpu.VMEM((own, 8, LANES), F32),
            pltpu.VMEM((hid, width), F32),
            pltpu.VMEM((hid, width), BF16),
            pltpu.VMEM((hid, width), BF16),
            pltpu.VMEM((hid, width), BF16),
            pltpu.VMEM((hid, width), BF16),
            pltpu.VMEM((hid, 2 * (mid + nb)), F32),
            pltpu.VMEM((hid, 2 * nb * mid), F32),
            pltpu.VMEM((hid, LANES), F32),
            pltpu.VMEM((2 * mid + 16, 2 * (mid + nb)), F32),
        ],
        compiler_params=pltpu.CompilerParams(vmem_limit_bytes=VMEM_BYTES),
        name="pool_params",
    )(plan, tile_list, weights, order, targets, *ghosts, *sums, pairs, *params)


def face_exchange(positions, species, targets, order):
    half = order.shape[2]
    box = jax.ShapeDtypeStruct((8, half), F32)
    return pl.pallas_call(
        face_kernel,
        out_shape=(box, box),
        in_specs=[VMEM_SPEC] * 4,
        out_specs=(VMEM_SPEC,) * 2,
        scratch_shapes=[pltpu.VMEM((8, half), F32)] * 4 + [pltpu.SemaphoreType.DMA((4,))],
        compiler_params=pltpu.CompilerParams(collective_id=0, has_side_effects=True),
        name="face_exchange",
    )(positions, species, targets, order)


def ghost_exchange(to_lower, to_upper):
    box = jax.ShapeDtypeStruct(to_lower.shape, F32)
    return pl.pallas_call(
        ghost_kernel,
        out_shape=(box, box),
        in_specs=[VMEM_SPEC] * 2,
        out_specs=(VMEM_SPEC,) * 2,
        scratch_shapes=[pltpu.VMEM(to_lower.shape, F32)] * 2 + [pltpu.SemaphoreType.DMA((4,))],
        compiler_params=pltpu.CompilerParams(collective_id=1, has_side_effects=True),
        name="ghost_exchange",
    )(to_lower, to_upper)


def sum_everywhere(x):
    groups, count = lax.axis_size("dp"), lax.axis_size("space")
    return pl.pallas_call(
        sum_kernel,
        out_shape=jax.ShapeDtypeStruct(x.shape, F32),
        in_specs=[VMEM_SPEC],
        out_specs=VMEM_SPEC,
        scratch_shapes=[
            pltpu.VMEM((groups,) + x.shape, F32),
            pltpu.VMEM(x.shape, F32),
            pltpu.VMEM((count,) + x.shape, F32),
            pltpu.SemaphoreType.DMA((groups - 1,)),
            pltpu.SemaphoreType.DMA((groups - 1,)),
            pltpu.SemaphoreType.DMA((count - 1,)),
            pltpu.SemaphoreType.DMA((count - 1,)),
        ],
        compiler_params=pltpu.CompilerParams(
            collective_id=2, has_side_effects=True, vmem_limit_bytes=VMEM_BYTES
        ),
        name="sum_everywhere",
    )(x)


def finish(summed, nb, ns, atoms):
    hid = summed.shape[1]
    domains = lax.axis_size("space")
    shapes = ((1, 1), (nb, hid), (ns, hid), (ns, hid), (1, hid))
    return pl.pallas_call(
        functools.partial(final_kernel, nb, ns, float(atoms), float(domains)),
        out_shape=tuple(jax.ShapeDtypeStruct(s, F32) for s in shapes),
        in_specs=[VMEM_SPEC],
        out_specs=(VMEM_SPEC,) * len(shapes),
        name="finish",
    )(summed)


def body(positions, species, ref_forces, send_lists, tile_lists, weights, w_rad, emb_center, emb_other, w_out):
    nb = w_rad.shape[0]
    ns = emb_center.shape[0]
    params = (w_rad, emb_center, emb_other, w_out[None])
    lower, upper = face_exchange(positions, species, ref_forces, send_lists)
    own_grad, to_lower, to_upper, pairs, plan = pool_force(
        tile_lists, positions, species, send_lists, lower, upper, params, 4 * LANES
    )
    from_lower, from_upper = ghost_exchange(to_lower, to_upper)
    forces, grads = pool_params(
        plan, tile_lists, weights, send_lists, ref_forces, (lower, upper),
        (own_grad, to_lower, to_upper, from_lower, from_upper), pairs, params,
    )
    summed = sum_everywhere(grads)
    loss, grad_rad, grad_center, grad_other, grad_out = finish(summed, nb, ns, positions.shape[2])
    return forces, loss[0, 0], grad_rad, grad_center, grad_other, grad_out[0]


def solution(mesh):
    return jax.shard_map(
        body,
        mesh=mesh,
        in_specs=(
            P("dp", None, "space"),
            P("dp", "space"),
            P("dp", None, "space"),
            P("dp", "space", None),
            P("dp", "space", None),
            P("dp"),
            P(),
            P(),
            P(),
            P(),
        ),
        out_specs=(P("dp", None, "space"), P(), P(), P(), P(), P()),
        check_vma=False,
    )
```

```python
import functools

import jax
import jax.numpy as jnp
from jax import lax
from jax.experimental import pallas as pl
from jax.experimental.pallas import tpu as pltpu
from jax.sharding import PartitionSpec as P

CUTOFF = 1.0
DOMAIN_WIDTH = 2.0
F32 = jnp.float32
BF16 = jnp.bfloat16
I32 = jnp.int32
LAST = (((1,), (1,)), ((), ()))
LANES = 128
HIGHEST = lax.Precision.HIGHEST


def split(x, parts):
    pieces = []
    for _ in range(parts - 1):
        high = x.astype(BF16).astype(F32)
        pieces.append(high)
        x = x - high
    pieces.append(x.astype(BF16).astype(F32))
    return pieces


def left_operand(x, exact):
    w1, w2, w3 = split(x, 3)
    return jnp.concatenate([w1, w1, w2, w1, w2, w3] + exact, axis=1).astype(BF16)


def right_operand(x, exact):
    b1, b2, b3 = split(x, 3)
    return jnp.concatenate([b1, b2, b1, b3, b2, b1] + exact, axis=0).astype(BF16)


def mxu(a, b):
    return jnp.dot(a, b, preferred_element_type=F32)


def mxu_t(a, b):
    return lax.dot_general(a, b, LAST, preferred_element_type=F32)


def radial_terms(offsets, nb):
    q = jnp.sum(offsets * offsets, axis=0, keepdims=True) / (CUTOFF * CUTOFF)
    scale = float(nb - 1)
    centers = lax.broadcasted_iota(I32, (nb, 1), 0).astype(F32) / scale
    arg = (q - centers) * scale
    basis = jnp.exp(-(arg * arg))
    slope = (-2.0 * scale) * arg * basis
    inner = jnp.maximum(1.0 - q, 0.0)
    return basis, slope, inner * inner, -2.0 * inner


def tables(rad_ref, center_ref, other_ref, out_ref):
    stack = jnp.concatenate([rad_ref[...], center_ref[...], other_ref[...]], axis=0)
    w_row = out_ref[...]
    both = jnp.concatenate([stack, jnp.broadcast_to(w_row, (8, w_row.shape[1]))], axis=0).T
    count = stack.shape[0]
    return stack, w_row, both[:, :count], both[:, count : count + 1]


def one_hot_rows(code_a, code_b, ns, width):
    row = lax.broadcasted_iota(I32, (2 * ns, width), 0).astype(F32)
    code = jnp.where(row < ns, code_a, code_b + float(ns))
    return jnp.where(code == row, 1.0, 0.0)


def prepare(t, slots, own, list_ref, rows_ref, cols_ref, e_ref, bound_ref, feat_ref, count_ref, ns):
    tile = rows_ref.shape[2]
    wide = slots * tile
    entries = [list_ref[0, k, t] for k in range(slots)]
    safe = [jnp.maximum(c, 0) for c in entries]
    xa = rows_ref[own]
    xb = jnp.concatenate([cols_ref[c] for c in safe], axis=0)
    q = jnp.zeros((wide, tile), F32)
    for i in range(3):
        diff = xb[:, i : i + 1] - xa[i : i + 1, :]
        q = q + diff * diff
    b_row = lax.broadcasted_iota(I32, (tile, tile), 0)
    a_lane = lax.broadcasted_iota(I32, (tile, tile), 1)
    allowed = []
    for c in entries:
        limit = jnp.where(c >= 0, 1.0, 0.0)
        allowed.append(jnp.where((b_row == a_lane) & (c == own), 0.0, limit))
    near = jnp.where(q / (CUTOFF * CUTOFF) < 1.0, jnp.concatenate(allowed, axis=0), 0.0)
    near_b = near.astype(BF16)
    r = lax.broadcasted_iota(I32, (wide, wide), 0)
    c = lax.broadcasted_iota(I32, (wide, wide), 1)
    lower = jnp.where(c < r, 1.0, 0.0).astype(BF16)
    rank = jnp.where(near > 0.0, mxu(lower, near_b) + 1.0, 0.0)
    row2 = lax.broadcasted_iota(I32, (2 * tile, tile), 0)
    col2 = lax.broadcasted_iota(I32, (2 * tile, tile), 1)
    reach = jnp.where(row2 < tile, row2 - 1, row2 - tile)
    below = jnp.where(col2 <= reach, 1.0, 0.0).astype(BF16)
    edges = jnp.sum(mxu_t(below, near_b), axis=1, keepdims=True)
    bound_ref[t] = jnp.broadcast_to(edges, (2 * tile, LANES))
    per_atom = jnp.sum(near, axis=0, keepdims=True)
    before = jnp.where(b_row < a_lane, 1.0, 0.0).astype(BF16)
    start = mxu(jnp.broadcast_to(per_atom, (16, tile)).astype(BF16), before)
    high = jnp.floor(start * (1.0 / 128.0))
    rest = start - 128.0 * high
    which = lax.broadcasted_iota(I32, (16, tile), 0)
    codes = jnp.where(which == 0, high, jnp.where(which == 1, rest, 0.0))
    e_ref[t] = jnp.concatenate([rank, codes], axis=0).astype(BF16)
    count_ref[t] = jnp.sum(per_atom).astype(I32)
    row = lax.broadcasted_iota(I32, (8, tile), 0)
    lane = lax.broadcasted_iota(I32, (8, tile), 1).astype(F32)
    kind_row = row.astype(F32)
    kind = xa[3:4, :]
    first = jnp.where(row < 3, xa, jnp.where(row == 4, lane, jnp.where(row == 6, kind, 0.0)))
    first_kind = jnp.where((row < ns) & (kind == kind_row), 1.0, 0.0)
    parts = [jnp.concatenate([first, first_kind], axis=0)]
    for k in range(slots):
        other = rows_ref[safe[k]]
        kind = other[3:4, :]
        second = jnp.where(
            row < 3, -other, jnp.where(row == 5, lane + float(k * tile), jnp.where(row == 7, kind, 0.0))
        )
        second_kind = jnp.where((row >= ns) & (kind + float(ns) == kind_row), 1.0, 0.0)
        parts.append(jnp.concatenate([second, second_kind], axis=0))
    feat_ref[t] = jnp.concatenate(split(jnp.concatenate(parts, axis=1), 3), axis=0).astype(BF16)


def selection(order_ref, k, atoms):
    count = order_ref.shape[2]
    row = lax.broadcasted_iota(I32, (atoms, count), 0)
    return jnp.where(row == order_ref[0, k : k + 1, :], 1.0, 0.0).astype(BF16)


def stacked(x):
    return jnp.concatenate(split(x, 3), axis=0).astype(BF16)


def unstacked(x):
    rows = x.shape[0] // 3
    return x[:rows] + (x[rows : 2 * rows] + x[2 * rows :])


def pad_rows(parts, width):
    count = sum(p.shape[0] for p in parts)
    return jnp.concatenate(parts + [jnp.zeros((8 - count, width), F32)], axis=0)


def fill_pool(pos_ref, spec_ref, lower_ref, upper_ref, rows_ref, cols_ref):
    tiles, _, tile = rows_ref.shape
    half = lower_ref.shape[1]
    atoms = pos_ref.shape[2]
    own = pad_rows([pos_ref[i] for i in range(3)] + [spec_ref[...].astype(F32)], atoms)
    row = lax.broadcasted_iota(I32, (8, half), 0)
    shift = jnp.where(row == 0, DOMAIN_WIDTH, 0.0)
    left = jnp.where(row < 4, lower_ref[...] - shift, 0.0)
    right = jnp.where(row < 4, upper_ref[...] + shift, 0.0)
    pool = jnp.concatenate([left, own, right], axis=1)
    turned = pool.T
    for i in range(tiles):
        rows_ref[i] = pool[:, i * tile : (i + 1) * tile]
        cols_ref[i] = turned[i * tile : (i + 1) * tile, :]


def force_kernel(
    nb, ns, width, list_ref, pos_ref, spec_ref, order_ref, lower_ref, upper_ref,
    rad_ref, center_ref, other_ref, out_ref,
    own_ref, to_lower_ref, to_upper_ref, pair_ref, plan_ref,
    rows_ref, cols_ref, grad_ref, e_ref, bound_ref, feat_ref, count_ref, rep_ref, y_ref, r_ref, wb_ref, acc_ref,
):
    _, slots, tiles_own = list_ref.shape
    tile = rows_ref.shape[2]
    fill_pool(pos_ref, spec_ref, lower_ref, upper_ref, rows_ref, cols_ref)
    wide_b = slots * tile
    half_tiles = tiles_own // 2
    hid = rad_ref.shape[1]
    for t in range(tiles_own):
        prepare(t, slots, t + half_tiles, list_ref, rows_ref, cols_ref, e_ref, bound_ref, feat_ref, count_ref, ns)
    total = jnp.int32(0)
    for t in range(tiles_own):
        pieces = (count_ref[t] + (width - 1)) // width

        def note(i, carry, t=t, total=total):
            plan_ref[1 + 2 * (total + i)] = t
            plan_ref[2 + 2 * (total + i)] = i * width
            return carry

        lax.fori_loop(0, pieces, note, 0)
        total = total + pieces
    plan_ref[0] = total
    acc_ref[...] = jnp.zeros_like(acc_ref)
    stack, w_row, cols, w_col = tables(rad_ref, center_ref, other_ref, out_ref)
    half_cols = 0.5 * cols
    weighted = 0.5 * w_row * stack[:nb]
    linear = jnp.dot(
        jnp.concatenate([weighted, w_row, jnp.zeros((7, hid), F32)], axis=0), half_cols,
        precision=HIGHEST, preferred_element_type=F32,
    )
    base = jnp.sum(weighted, axis=1, keepdims=True)
    y_rows = jnp.concatenate([half_cols, linear], axis=0)
    a_y = left_operand(y_rows[:, :nb], split(y_rows[:, nb:], 3))
    a_r = left_operand((0.5 * w_col) * cols[:, :nb], [])
    wb_ref[...] = jnp.broadcast_to(w_col, wb_ref.shape)

    def chunk(step, carry):
        t = plan_ref[1 + 2 * step]
        start = plan_ref[2 + 2 * step]
        count = count_ref[t]
        spot = (start + lax.broadcasted_iota(I32, (1, width), 1)).astype(F32)
        bounds = bound_ref[t]
        firsts = []
        for lane in range(0, width, LANES):
            here = spot[:, lane : lane + LANES]
            inside = (here >= bounds[:tile]) & (here < bounds[tile:])
            firsts.append(jnp.where(inside, 1.0, 0.0))
        first = jnp.concatenate(firsts, axis=1).astype(BF16)
        found = mxu(e_ref[t], first)
        valid = spot < count.astype(F32)
        begin = 128.0 * found[wide_b : wide_b + 1] + found[wide_b + 1 : wide_b + 2]
        rank = jnp.where(valid, spot - begin + 1.0, -1.0)
        second = jnp.where(found[:wide_b] == rank, 1.0, 0.0).astype(BF16)
        rep_ref[:tile] = first
        rep_ref[tile:] = second
        pieces = mxu(feat_ref[t], rep_ref[...])
        wide = pieces[:16] + (pieces[16:32] + pieces[32:])
        keep = jnp.where(valid, 1.0, 0.0)
        record = wide[:8]
        row = lax.broadcasted_iota(I32, (8, width), 0)
        pair_ref[step] = jnp.where(row == 3, keep, record)
        kinds = wide[8:16]
        basis, slope, env, denv = radial_terms(wide[0:3], nb)
        x = right_operand(basis, [kinds, kinds, kinds])
        dx = right_operand(slope, [])
        y_ref[...] = mxu(a_y, x)
        r_ref[...] = mxu(a_r, dx)
        s_rows, t_rows = [], []
        for lane in range(0, width, LANES):
            s = jnp.zeros((8, LANES), F32)
            u = jnp.zeros((8, LANES), F32)
            for h in range(0, hid, 8):
                y = y_ref[h : h + 8, lane : lane + LANES]
                r = r_ref[h : h + 8, lane : lane + LANES]
                th = jnp.tanh(y)
                a = y * th
                g = th * (1.0 - a)
                s = s + wb_ref[h : h + 8, :] * a
                u = u + r * g
            s_rows.append(jnp.sum(s, axis=0, keepdims=True))
            t_rows.append(jnp.sum(u, axis=0, keepdims=True))
        lin = y_ref[hid : hid + 16, :]
        s_all = jnp.concatenate(s_rows, axis=1) + lin[8:9]
        t_all = jnp.concatenate(t_rows, axis=1) + jnp.sum(slope * (base + lin[:8]), axis=0, keepdims=True)
        g = keep * (denv * s_all + env * t_all)
        gd = (2.0 * g) * record
        back = mxu_t(jnp.concatenate(split(gd, 3), axis=0).astype(BF16), rep_ref[...])
        acc_ref[t] = acc_ref[t] + (back[0:8] + (back[8:16] + back[16:24]))
        return carry

    lax.fori_loop(0, total, chunk, 0)
    grad_ref[...] = jnp.zeros_like(grad_ref)
    for t in range(tiles_own):
        own = t + half_tiles
        grad_ref[own] = grad_ref[own] + acc_ref[t, :, :tile]
        for k in range(slots):
            entry = jnp.maximum(list_ref[0, k, t], 0)
            grad_ref[entry] = grad_ref[entry] - acc_ref[t, :, (k + 1) * tile : (k + 2) * tile]
    whole = jnp.concatenate([grad_ref[i] for i in range(grad_ref.shape[0])], axis=1)
    atoms = pos_ref.shape[2]
    half = atoms // 2
    own_grad = whole[:, half : half + atoms]
    own_ref[...] = own_grad
    pieces = stacked(own_grad)
    for k, ref in ((0, to_lower_ref), (1, to_upper_ref)):
        sent = unstacked(mxu(pieces, selection(order_ref, k, atoms)))
        ghost = whole[:, :half] if k == 0 else whole[:, half + atoms :]
        ref[...] = pad_rows([sent[0:3], ghost[0:3]], half)


def finish_forces(
    weight, order_ref, target_ref, lower_ref, upper_ref, own_ref,
    to_lower_ref, to_upper_ref, from_lower_ref, from_upper_ref, forces_ref, v_ref,
):
    tiles, _, tile = v_ref.shape
    atoms = own_ref.shape[1]
    total = own_ref[0:3, :]
    for k, ref in ((0, from_lower_ref), (1, from_upper_ref)):
        total = total + unstacked(mxu_t(stacked(ref[...]), selection(order_ref, k, atoms)))[3:6]
    for i in range(3):
        forces_ref[i] = -total[i : i + 1]
    miss = total + jnp.concatenate([target_ref[i] for i in range(3)], axis=0)
    left = to_lower_ref[3:6, :] + from_lower_ref[0:3, :] + lower_ref[4:7, :]
    right = to_upper_ref[3:6, :] + from_upper_ref[0:3, :] + upper_ref[4:7, :]
    scaled = (2.0 * weight) * jnp.concatenate([left, miss, right], axis=1)
    scaled = pad_rows([scaled], scaled.shape[1])
    for i in range(tiles):
        v_ref[i] = scaled[:, i * tile : (i + 1) * tile]
    return weight * jnp.sum(miss * miss)


def param_kernel(
    nb, ns, plan_ref, list_ref, weight_ref, order_ref, target_ref, lower_ref, upper_ref, own_ref,
    to_lower_ref, to_upper_ref, from_lower_ref, from_upper_ref, pair_ref, rad_ref, center_ref, other_ref, out_ref,
    forces_ref, grads_ref,
    v_ref, va_ref, vb_ref, y_ref, gh_ref, gl_ref, fh_ref, fl_ref, acc_g, acc_f, acc_s, gram_ref,
):
    _, slots, tiles_own = list_ref.shape
    tile = v_ref.shape[2]
    half_tiles = tiles_own // 2
    hid = rad_ref.shape[1]
    width = pair_ref.shape[2]
    weight = weight_ref[0].astype(F32)
    loss = finish_forces(
        weight, order_ref, target_ref, lower_ref, upper_ref, own_ref,
        to_lower_ref, to_upper_ref, from_lower_ref, from_upper_ref, forces_ref, v_ref,
    )
    mid = nb + 2 * ns
    acc_g[...] = jnp.zeros_like(acc_g)
    acc_f[...] = jnp.zeros_like(acc_f)
    acc_s[...] = jnp.zeros_like(acc_s)
    gram_ref[...] = jnp.zeros_like(gram_ref)
    for t in range(tiles_own):
        va_ref[t] = jnp.concatenate([v_ref[t + half_tiles], jnp.zeros((8, LANES - tile), F32)], axis=1)
        vb_ref[t] = jnp.concatenate([v_ref[jnp.maximum(list_ref[0, k, t], 0)] for k in range(slots)], axis=1)
    stack, w_row, cols, w_col = tables(rad_ref, center_ref, other_ref, out_ref)
    half_cols = 0.5 * cols
    a_y = left_operand(half_cols[:, :nb], split(half_cols[:, nb:], 3))

    def chunk(step, carry):
        t = plan_ref[1 + 2 * step]
        record = pair_ref[step]
        offsets = record[0:3]
        keep = record[3:4]
        index_a = jnp.broadcast_to(record[4:5].astype(I32), (8, width))
        index_b = jnp.broadcast_to(record[5:6].astype(I32), (8, width))
        va, vb = va_ref[t], vb_ref[t]
        diffs = []
        for lane in range(0, width, LANES):
            part_a = jnp.take_along_axis(va, index_a[:, lane : lane + LANES], axis=1, mode="promise_in_bounds")
            part_b = jnp.take_along_axis(vb, index_b[:, lane : lane + LANES], axis=1, mode="promise_in_bounds")
            diffs.append(part_a - part_b)
        dv = jnp.concatenate(diffs, axis=1)
        kinds = one_hot_rows(record[6:7], record[7:8], ns, width)
        basis, slope, env, denv = radial_terms(offsets, nb)
        c = (2.0 * keep) * jnp.sum(offsets * dv[0:3], axis=0, keepdims=True)
        alpha = c * denv
        beta_slope = (c * env) * slope
        y_ref[...] = mxu(a_y, right_operand(basis, [kinds, kinds, kinds]))
        for h in range(0, hid, 16):
            s = acc_s[h : h + 16, :]
            for lane in range(0, width, LANES):
                y = y_ref[h : h + 16, lane : lane + LANES]
                th = jnp.tanh(y)
                a = y * th
                u = 1.0 - a
                g = th * u
                f = u - th * g
                s = s + alpha[:, lane : lane + LANES] * a
                g_high = g.astype(BF16)
                f_high = f.astype(BF16)
                gh_ref[h : h + 16, lane : lane + LANES] = g_high
                gl_ref[h : h + 16, lane : lane + LANES] = (g - g_high.astype(F32)).astype(BF16)
                fh_ref[h : h + 16, lane : lane + LANES] = f_high
                fl_ref[h : h + 16, lane : lane + LANES] = (f - f_high.astype(F32)).astype(BF16)
            acc_s[h : h + 16, :] = s
        x = jnp.concatenate([basis, kinds], axis=0)
        one = jnp.ones((8, width), F32)
        g_cols = jnp.concatenate(split(jnp.concatenate([alpha * x, beta_slope], axis=0), 2), axis=0).astype(BF16)
        f_cols = jnp.concatenate(
            split(jnp.concatenate([beta_slope[j : j + 1] * x for j in range(nb)], axis=0), 2), axis=0
        ).astype(BF16)
        x_rows = jnp.concatenate(split(x, 2) + [one, one], axis=0).astype(BF16)
        acc_g[...] += mxu_t(gh_ref[...], g_cols) + mxu_t(gl_ref[...], g_cols)
        acc_f[...] += mxu_t(fh_ref[...], f_cols) + mxu_t(fl_ref[...], f_cols)
        gram_ref[...] += mxu_t(x_rows, g_cols)
        return carry

    lax.fori_loop(0, plan_ref[0], chunk, 0)
    cols_g = mid + nb
    gram = gram_ref[:, :cols_g] + gram_ref[:, cols_g:]
    gram_x = gram[:mid] + gram[mid : 2 * mid]
    gram_one = gram[2 * mid : 2 * mid + 1]
    curved = acc_g[:, :cols_g] + acc_g[:, cols_g:]
    spread = jnp.dot(half_cols, gram_x, precision=HIGHEST, preferred_element_type=F32)
    first = 0.5 * (gram_one + spread + curved)
    sharp = 0.5 * (acc_f[:, : nb * mid] + acc_f[:, nb * mid :])
    d = first[:, :mid]
    for j in range(nb):
        d = d + cols[:, j : j + 1] * sharp[:, j * mid : (j + 1) * mid]
    slope_part = first[:, mid:]
    grad_rad = w_col * (d[:, :nb] + slope_part)
    grad_tables = w_col * d[:, nb:]
    grad_out = (
        jnp.sum(acc_s[...], axis=1, keepdims=True)
        + jnp.sum(half_cols * gram_one[:, :mid], axis=1, keepdims=True)
        + jnp.sum(slope_part * cols[:, :nb], axis=1, keepdims=True)
    )
    spare = jnp.zeros((hid, LANES - mid - 1), F32)
    turned = jnp.concatenate([grad_rad, grad_tables, grad_out, spare], axis=1).T
    rows = grads_ref.shape[0]
    row = lax.broadcasted_iota(I32, (rows, hid), 0)
    lane = lax.broadcasted_iota(I32, (rows, hid), 1)
    extra = jnp.where(lane == 0, loss, jnp.where(lane == 1, weight, 0.0))
    grads_ref[...] = jnp.where(row == mid + 1, extra, turned[:rows])


SMEM_SPEC = pl.BlockSpec(memory_space=pltpu.SMEM)
VMEM_SPEC = pl.BlockSpec(memory_space=pltpu.VMEM)
MESH = pl.DeviceIdType.MESH
MIB = 1024 * 1024


def swap(to_lower, to_upper, from_lower, from_upper, sems):
    me, count = lax.axis_index("space"), lax.axis_size("space")
    group = lax.axis_index("dp")
    upper, lower = lax.rem(me + 1, count), lax.rem(me + count - 1, count)
    up = pltpu.make_async_remote_copy(
        src_ref=to_upper, dst_ref=from_lower, send_sem=sems.at[0], recv_sem=sems.at[1],
        device_id=(group, upper), device_id_type=MESH,
    )
    down = pltpu.make_async_remote_copy(
        src_ref=to_lower, dst_ref=from_upper, send_sem=sems.at[2], recv_sem=sems.at[3],
        device_id=(group, lower), device_id_type=MESH,
    )
    return up, down


def greet():
    me, count = lax.axis_index("space"), lax.axis_size("space")
    group = lax.axis_index("dp")
    barrier = pltpu.get_barrier_semaphore()
    for other in (lax.rem(me + 1, count), lax.rem(me + count - 1, count)):
        pl.semaphore_signal(barrier, inc=1, device_id=(group, other), device_id_type=MESH)
    return barrier


def face_kernel(
    pos_ref, spec_ref, target_ref, order_ref, *refs,
):
    count = 5
    more, refs = refs[:count], refs[count:]
    lower_ref, upper_ref, pos_out, spec_out, target_out, order_out = refs[:6]
    more_out, refs = refs[6 : 6 + count], refs[6 + count :]
    to_lower, to_upper, from_lower, from_upper, sems, load_sems = refs
    barrier = greet()
    sources = (pos_ref, spec_ref, target_ref, order_ref) + more
    targets = (pos_out, spec_out, target_out, order_out) + more_out
    loads = [pltpu.make_async_copy(s, t, load_sems.at[i]) for i, (s, t) in enumerate(zip(sources, targets))]
    for load in loads:
        load.start()
    for load in loads[:4]:
        load.wait()
    atoms = pos_out.shape[2]
    rows = [pos_out[i] for i in range(3)] + [spec_out[...].astype(F32)] + [target_out[i] for i in range(3)]
    pieces = stacked(pad_rows(rows, atoms))
    to_lower[...] = unstacked(mxu(pieces, selection(order_out, 0, atoms)))
    to_upper[...] = unstacked(mxu(pieces, selection(order_out, 1, atoms)))
    pl.semaphore_wait(barrier, 2)
    up, down = swap(to_lower, to_upper, from_lower, from_upper, sems)
    up.start()
    down.start()
    for load in loads[4:]:
        load.wait()
    up.wait()
    down.wait()
    lower_ref[...] = from_lower[...]
    upper_ref[...] = from_upper[...]


def ghost_kernel(to_lower, to_upper, lower_ref, upper_ref, from_lower, from_upper, sems):
    barrier = greet()
    pl.semaphore_wait(barrier, 2)
    up, down = swap(to_lower, to_upper, from_lower, from_upper, sems)
    up.start()
    down.start()
    up.wait()
    down.wait()
    lower_ref[...] = from_lower[...]
    upper_ref[...] = from_upper[...]


def sum_kernel(x_ref, out_ref, near, part, far, near_send, near_recv, far_send, far_recv):
    group, me = lax.axis_index("dp"), lax.axis_index("space")
    groups, count = lax.axis_size("dp"), lax.axis_size("space")
    barrier = pltpu.get_barrier_semaphore()
    others = [(lax.rem(group + k, groups), me) for k in range(1, groups)]
    others += [(group, lax.rem(me + k, count)) for k in range(1, count)]
    for other in others:
        pl.semaphore_signal(barrier, inc=1, device_id=other, device_id_type=MESH)
    pl.semaphore_wait(barrier, len(others))

    def share(source, slots, send, recv, spot, peers):
        copies = []
        for k, other in enumerate(peers):
            copies.append(
                pltpu.make_async_remote_copy(
                    src_ref=source, dst_ref=slots.at[spot], send_sem=send.at[k], recv_sem=recv.at[k],
                    device_id=other, device_id_type=MESH,
                )
            )
            copies[-1].start()
        slots[spot] = source[...]
        for copy in copies:
            copy.wait()
        total = slots[0]
        for k in range(1, len(peers) + 1):
            total = total + slots[k]
        return total

    part[...] = share(x_ref, near, near_send, near_recv, group, others[: groups - 1])
    out_ref[...] = share(part, far, far_send, far_recv, me, others[groups - 1 :])


def final_kernel(nb, ns, atoms, domains, sum_ref, loss_ref, rad_ref, center_ref, other_ref, out_ref):
    last = nb + 2 * ns
    weight_total = sum_ref[last + 1 : last + 2, 1:2] / domains
    scale = 1.0 / (3.0 * atoms * domains * weight_total)
    loss_ref[...] = sum_ref[last + 1 : last + 2, 0:1] * scale
    rad_ref[...] = sum_ref[:nb] * scale
    center_ref[...] = sum_ref[nb : nb + ns] * scale
    other_ref[...] = sum_ref[nb + ns : last] * scale
    out_ref[...] = sum_ref[last : last + 1] * scale


def pool_force(tile_list, positions, species, order, lower, upper, params, width):
    atoms = positions.shape[2]
    half = atoms // 2
    _, slots, own = tile_list.shape
    tile = atoms // own
    tiles = 2 * own
    rad, center = params[0], params[1]
    nb, hid = rad.shape
    ns = center.shape[0]
    most = own * (-(-slots * tile * tile // width))
    wide_b = slots * tile
    return pl.pallas_call(
        functools.partial(force_kernel, nb, ns, width),
        out_shape=(
            jax.ShapeDtypeStruct((8, atoms), F32),
            jax.ShapeDtypeStruct((8, half), F32),
            jax.ShapeDtypeStruct((8, half), F32),
            jax.ShapeDtypeStruct((most, 8, width), F32),
            jax.ShapeDtypeStruct((2 * most + 1,), I32),
        ),
        in_specs=[SMEM_SPEC] + [VMEM_SPEC] * 9,
        out_specs=(VMEM_SPEC,) * 4 + (SMEM_SPEC,),
        scratch_shapes=[
            pltpu.VMEM((tiles, 8, tile), F32),
            pltpu.VMEM((tiles, tile, 8), F32),
            pltpu.VMEM((tiles, 8, tile), F32),
            pltpu.VMEM((own, wide_b + 16, tile), BF16),
            pltpu.VMEM((own, 2 * tile, LANES), F32),
            pltpu.VMEM((own, 48, tile + wide_b), BF16),
            pltpu.SMEM((own,), I32),
            pltpu.VMEM((tile + wide_b, width), BF16),
            pltpu.VMEM((hid + 16, width), F32),
            pltpu.VMEM((hid, width), F32),
            pltpu.VMEM((hid, LANES), F32),
            pltpu.VMEM((own, 8, tile + wide_b), F32),
        ],
        compiler_params=pltpu.CompilerParams(vmem_limit_bytes=24 * MIB),
        name="pool_force",
    )(tile_list, positions, species, order, lower, upper, *params)


def pool_params(plan, tile_list, weights, order, targets, ghosts, sums, pairs, params):
    _, slots, own = tile_list.shape
    atoms = targets.shape[2]
    tile = atoms // own
    width = pairs.shape[2]
    rad, center = params[0], params[1]
    nb, hid = rad.shape
    ns = center.shape[0]
    mid = nb + 2 * ns
    rows = -(-(mid + 2) // 8) * 8
    return pl.pallas_call(
        functools.partial(param_kernel, nb, ns),
        out_shape=(
            jax.ShapeDtypeStruct(targets.shape, F32),
            jax.ShapeDtypeStruct((rows, hid), F32),
        ),
        in_specs=[SMEM_SPEC] * 3 + [VMEM_SPEC] * 14,
        out_specs=(VMEM_SPEC,) * 2,
        scratch_shapes=[
            pltpu.VMEM((2 * own, 8, tile), F32),
            pltpu.VMEM((own, 8, LANES), F32),
            pltpu.VMEM((own, 8, LANES), F32),
            pltpu.VMEM((hid, width), F32),
            pltpu.VMEM((hid, width), BF16),
            pltpu.VMEM((hid, width), BF16),
            pltpu.VMEM((hid, width), BF16),
            pltpu.VMEM((hid, width), BF16),
            pltpu.VMEM((hid, 2 * (mid + nb)), F32),
            pltpu.VMEM((hid, 2 * nb * mid), F32),
            pltpu.VMEM((hid, LANES), F32),
            pltpu.VMEM((2 * mid + 16, 2 * (mid + nb)), F32),
        ],
        compiler_params=pltpu.CompilerParams(vmem_limit_bytes=24 * MIB),
        name="pool_params",
    )(plan, tile_list, weights, order, targets, *ghosts, *sums, pairs, *params)


def face_exchange(positions, species, targets, order, *others):
    half = order.shape[2]
    box = jax.ShapeDtypeStruct((8, half), F32)
    arrays = (positions, species, targets, order) + others
    held = tuple(jax.ShapeDtypeStruct(x.shape, x.dtype) for x in arrays)
    return pl.pallas_call(
        face_kernel,
        out_shape=(box, box) + held,
        in_specs=[pl.BlockSpec(memory_space=pltpu.HBM)] * len(arrays),
        out_specs=(VMEM_SPEC,) * (2 + len(arrays)),
        scratch_shapes=[pltpu.VMEM((8, half), F32)] * 4
        + [pltpu.SemaphoreType.DMA((4,)), pltpu.SemaphoreType.DMA((len(arrays),))],
        compiler_params=pltpu.CompilerParams(collective_id=0, has_side_effects=True, vmem_limit_bytes=8 * MIB),
        name="face_exchange",
    )(*[pltpu.with_memory_space_constraint(x, pltpu.HBM) for x in arrays])


def ghost_exchange(to_lower, to_upper):
    box = jax.ShapeDtypeStruct(to_lower.shape, F32)
    return pl.pallas_call(
        ghost_kernel,
        out_shape=(box, box),
        in_specs=[VMEM_SPEC] * 2,
        out_specs=(VMEM_SPEC,) * 2,
        scratch_shapes=[pltpu.VMEM(to_lower.shape, F32)] * 2 + [pltpu.SemaphoreType.DMA((4,))],
        compiler_params=pltpu.CompilerParams(collective_id=1, has_side_effects=True, vmem_limit_bytes=4 * MIB),
        name="ghost_exchange",
    )(to_lower, to_upper)


def sum_everywhere(x):
    groups, count = lax.axis_size("dp"), lax.axis_size("space")
    return pl.pallas_call(
        sum_kernel,
        out_shape=jax.ShapeDtypeStruct(x.shape, F32),
        in_specs=[VMEM_SPEC],
        out_specs=VMEM_SPEC,
        scratch_shapes=[
            pltpu.VMEM((groups,) + x.shape, F32),
            pltpu.VMEM(x.shape, F32),
            pltpu.VMEM((count,) + x.shape, F32),
            pltpu.SemaphoreType.DMA((groups - 1,)),
            pltpu.SemaphoreType.DMA((groups - 1,)),
            pltpu.SemaphoreType.DMA((count - 1,)),
            pltpu.SemaphoreType.DMA((count - 1,)),
        ],
        compiler_params=pltpu.CompilerParams(
            collective_id=2, has_side_effects=True, vmem_limit_bytes=8 * MIB
        ),
        name="sum_everywhere",
    )(x)


def finish(summed, nb, ns, atoms):
    hid = summed.shape[1]
    domains = lax.axis_size("space")
    shapes = ((1, 1), (nb, hid), (ns, hid), (ns, hid), (1, hid))
    return pl.pallas_call(
        functools.partial(final_kernel, nb, ns, float(atoms), float(domains)),
        out_shape=tuple(jax.ShapeDtypeStruct(s, F32) for s in shapes),
        in_specs=[VMEM_SPEC],
        out_specs=(VMEM_SPEC,) * len(shapes),
        compiler_params=pltpu.CompilerParams(vmem_limit_bytes=4 * MIB),
        name="finish",
    )(summed)


def body(positions, species, ref_forces, send_lists, tile_lists, weights, w_rad, emb_center, emb_other, w_out):
    nb = w_rad.shape[0]
    ns = emb_center.shape[0]
    positions, ref_forces = positions.transpose(1, 0, 2), ref_forces.transpose(1, 0, 2)
    tile_lists = tile_lists.transpose(0, 2, 1)
    lower, upper, positions, species, ref_forces, send_lists, tile_lists, *params = face_exchange(
        positions, species, ref_forces, send_lists, tile_lists, w_rad, emb_center, emb_other, w_out[None]
    )
    own_grad, to_lower, to_upper, pairs, plan = pool_force(
        tile_lists, positions, species, send_lists, lower, upper, params, 4 * LANES
    )
    from_lower, from_upper = ghost_exchange(to_lower, to_upper)
    forces, grads = pool_params(
        plan, tile_lists, weights, send_lists, ref_forces, (lower, upper),
        (own_grad, to_lower, to_upper, from_lower, from_upper), pairs, params,
    )
    summed = sum_everywhere(grads)
    loss, grad_rad, grad_center, grad_other, grad_out = finish(summed, nb, ns, positions.shape[2])
    forces = forces.transpose(1, 0, 2)
    return forces, loss[0, 0], grad_rad, grad_center, grad_other, grad_out[0]


def solution(mesh):
    return jax.shard_map(
        body,
        mesh=mesh,
        in_specs=(
            P("dp", None, "space"),
            P("dp", "space"),
            P("dp", None, "space"),
            P("dp", "space", None),
            P("dp", "space", None),
            P("dp"),
            P(),
            P(),
            P(),
            P(),
        ),
        out_specs=(P("dp", None, "space"), P(), P(), P(), P(), P()),
        check_vma=False,
    )
```

```python
import functools

import jax
import jax.numpy as jnp
from jax import lax
from jax.experimental import pallas as pl
from jax.experimental.pallas import tpu as pltpu
from jax.sharding import PartitionSpec as P

CUTOFF = 1.0
DOMAIN_WIDTH = 2.0
F32 = jnp.float32
BF16 = jnp.bfloat16
I32 = jnp.int32
LAST = (((1,), (1,)), ((), ()))
LANES = 128
HIGHEST = lax.Precision.HIGHEST


def split(x, parts):
    pieces = []
    for _ in range(parts - 1):
        high = x.astype(BF16).astype(F32)
        pieces.append(high)
        x = x - high
    pieces.append(x.astype(BF16).astype(F32))
    return pieces


def left_operand(x, exact):
    w1, w2, w3 = split(x, 3)
    return jnp.concatenate([w1, w1, w2, w1, w2, w3] + exact, axis=1).astype(BF16)


def right_operand(x, exact):
    b1, b2, b3 = split(x, 3)
    return jnp.concatenate([b1, b2, b1, b3, b2, b1] + exact, axis=0).astype(BF16)


def mxu(a, b):
    return jnp.dot(a, b, preferred_element_type=F32)


def mxu_t(a, b):
    return lax.dot_general(a, b, LAST, preferred_element_type=F32)


def radial_terms(offsets, nb):
    q = jnp.sum(offsets * offsets, axis=0, keepdims=True) / (CUTOFF * CUTOFF)
    scale = float(nb - 1)
    centers = lax.broadcasted_iota(I32, (nb, 1), 0).astype(F32) / scale
    arg = (q - centers) * scale
    basis = jnp.exp(-(arg * arg))
    slope = (-2.0 * scale) * arg * basis
    inner = jnp.maximum(1.0 - q, 0.0)
    return basis, slope, inner * inner, -2.0 * inner


def tables(rad_ref, center_ref, other_ref, out_ref):
    stack = jnp.concatenate([rad_ref[...], center_ref[...], other_ref[...]], axis=0)
    w_row = out_ref[...]
    both = jnp.concatenate([stack, jnp.broadcast_to(w_row, (8, w_row.shape[1]))], axis=0).T
    count = stack.shape[0]
    return stack, w_row, both[:, :count], both[:, count : count + 1]


def one_hot_rows(code_a, code_b, ns, width):
    row = lax.broadcasted_iota(I32, (2 * ns, width), 0).astype(F32)
    code = jnp.where(row < ns, code_a, code_b + float(ns))
    return jnp.where(code == row, 1.0, 0.0)


def prepare(t, slots, own, list_ref, rows_ref, cols_ref, e_ref, bound_ref, feat_ref, count_ref, ns):
    tile = rows_ref.shape[2]
    wide = slots * tile
    entries = [list_ref[0, k, t] for k in range(slots)]
    safe = [jnp.maximum(c, 0) for c in entries]
    xa = rows_ref[own]
    xb = jnp.concatenate([cols_ref[c] for c in safe], axis=0)
    q = jnp.zeros((wide, tile), F32)
    for i in range(3):
        diff = xb[:, i : i + 1] - xa[i : i + 1, :]
        q = q + diff * diff
    b_row = lax.broadcasted_iota(I32, (tile, tile), 0)
    a_lane = lax.broadcasted_iota(I32, (tile, tile), 1)
    allowed = []
    for c in entries:
        limit = jnp.where(c >= 0, 1.0, 0.0)
        allowed.append(jnp.where((b_row == a_lane) & (c == own), 0.0, limit))
    near = jnp.where(q / (CUTOFF * CUTOFF) < 1.0, jnp.concatenate(allowed, axis=0), 0.0)
    near_b = near.astype(BF16)
    r = lax.broadcasted_iota(I32, (wide, wide), 0)
    c = lax.broadcasted_iota(I32, (wide, wide), 1)
    lower = jnp.where(c < r, 1.0, 0.0).astype(BF16)
    rank = jnp.where(near > 0.0, mxu(lower, near_b) + 1.0, 0.0)
    row2 = lax.broadcasted_iota(I32, (2 * tile, tile), 0)
    col2 = lax.broadcasted_iota(I32, (2 * tile, tile), 1)
    reach = jnp.where(row2 < tile, row2 - 1, row2 - tile)
    below = jnp.where(col2 <= reach, 1.0, 0.0).astype(BF16)
    edges = jnp.sum(mxu_t(below, near_b), axis=1, keepdims=True)
    bound_ref[t] = jnp.broadcast_to(edges, (2 * tile, LANES))
    per_atom = jnp.sum(near, axis=0, keepdims=True)
    before = jnp.where(b_row < a_lane, 1.0, 0.0).astype(BF16)
    start = mxu(jnp.broadcast_to(per_atom, (16, tile)).astype(BF16), before)
    high = jnp.floor(start * (1.0 / 128.0))
    rest = start - 128.0 * high
    which = lax.broadcasted_iota(I32, (16, tile), 0)
    codes = jnp.where(which == 0, high, jnp.where(which == 1, rest, 0.0))
    e_ref[t] = jnp.concatenate([rank, codes], axis=0).astype(BF16)
    count_ref[t] = jnp.sum(per_atom).astype(I32)
    row = lax.broadcasted_iota(I32, (8, tile), 0)
    lane = lax.broadcasted_iota(I32, (8, tile), 1).astype(F32)
    kind_row = row.astype(F32)
    kind = xa[3:4, :]
    first = jnp.where(row < 3, xa, jnp.where(row == 4, lane, jnp.where(row == 6, kind, 0.0)))
    first_kind = jnp.where((row < ns) & (kind == kind_row), 1.0, 0.0)
    parts = [jnp.concatenate([first, first_kind], axis=0)]
    for k in range(slots):
        other = rows_ref[safe[k]]
        kind = other[3:4, :]
        second = jnp.where(
            row < 3, -other, jnp.where(row == 5, lane + float(k * tile), jnp.where(row == 7, kind, 0.0))
        )
        second_kind = jnp.where((row >= ns) & (kind + float(ns) == kind_row), 1.0, 0.0)
        parts.append(jnp.concatenate([second, second_kind], axis=0))
    feat_ref[t] = jnp.concatenate(split(jnp.concatenate(parts, axis=1), 3), axis=0).astype(BF16)


def selection(order_ref, k, atoms):
    count = order_ref.shape[2]
    row = lax.broadcasted_iota(I32, (atoms, count), 0)
    return jnp.where(row == order_ref[0, k : k + 1, :], 1.0, 0.0).astype(BF16)


def stacked(x):
    return jnp.concatenate(split(x, 3), axis=0).astype(BF16)


def unstacked(x):
    rows = x.shape[0] // 3
    return x[:rows] + (x[rows : 2 * rows] + x[2 * rows :])


def pad_rows(parts, width):
    count = sum(p.shape[0] for p in parts)
    return jnp.concatenate(parts + [jnp.zeros((8 - count, width), F32)], axis=0)


def fill_pool(pos_ref, spec_ref, lower_ref, upper_ref, rows_ref, cols_ref):
    tiles, _, tile = rows_ref.shape
    half = lower_ref.shape[1]
    atoms = pos_ref.shape[2]
    own = pad_rows([pos_ref[i] for i in range(3)] + [spec_ref[...].astype(F32)], atoms)
    row = lax.broadcasted_iota(I32, (8, half), 0)
    shift = jnp.where(row == 0, DOMAIN_WIDTH, 0.0)
    left = jnp.where(row < 4, lower_ref[...] - shift, 0.0)
    right = jnp.where(row < 4, upper_ref[...] + shift, 0.0)
    pool = jnp.concatenate([left, own, right], axis=1)
    turned = pool.T
    for i in range(tiles):
        rows_ref[i] = pool[:, i * tile : (i + 1) * tile]
        cols_ref[i] = turned[i * tile : (i + 1) * tile, :]


def force_kernel(
    nb, ns, width, list_ref, pos_ref, spec_ref, order_ref, lower_ref, upper_ref,
    rad_ref, center_ref, other_ref, out_ref,
    own_ref, to_lower_ref, to_upper_ref, pair_ref, plan_ref,
    rows_ref, cols_ref, grad_ref, e_ref, bound_ref, feat_ref, count_ref, sets, wb_ref, acc_ref,
):
    _, slots, tiles_own = list_ref.shape
    tile = rows_ref.shape[2]
    fill_pool(pos_ref, spec_ref, lower_ref, upper_ref, rows_ref, cols_ref)
    wide_b = slots * tile
    half_tiles = tiles_own // 2
    hid = rad_ref.shape[1]
    for t in range(tiles_own):
        prepare(t, slots, t + half_tiles, list_ref, rows_ref, cols_ref, e_ref, bound_ref, feat_ref, count_ref, ns)
    total = jnp.int32(0)
    for t in range(tiles_own):
        pieces = (count_ref[t] + (width - 1)) // width

        def note(i, carry, t=t, total=total):
            plan_ref[1 + 2 * (total + i)] = t
            plan_ref[2 + 2 * (total + i)] = i * width
            return carry

        lax.fori_loop(0, pieces, note, 0)
        total = total + pieces
    plan_ref[0] = total
    acc_ref[...] = jnp.zeros_like(acc_ref)
    stack, w_row, cols, w_col = tables(rad_ref, center_ref, other_ref, out_ref)
    half_cols = 0.5 * cols
    weighted = 0.5 * w_row * stack[:nb]
    linear = jnp.dot(
        jnp.concatenate([weighted, w_row, jnp.zeros((7, hid), F32)], axis=0), half_cols,
        precision=HIGHEST, preferred_element_type=F32,
    )
    base = jnp.sum(weighted, axis=1, keepdims=True)
    y_rows = jnp.concatenate([half_cols, linear], axis=0)
    a_y = left_operand(y_rows[:, :nb], split(y_rows[:, nb:], 3))
    a_r = left_operand((0.5 * w_col) * cols[:, :nb], [])
    wb_ref[...] = jnp.broadcast_to(w_col, wb_ref.shape)

    def of_step(step):
        known = jnp.minimum(step, total - 1)
        t = plan_ref[1 + 2 * known]
        spot = (plan_ref[2 + 2 * known] + lax.broadcasted_iota(I32, (1, width), 1)).astype(F32)
        return t, spot, spot < jnp.where(step < total, count_ref[t], 0).astype(F32)

    def choose(step, held):
        rep_ref = held[0]
        t, spot, valid = of_step(step)
        bounds = bound_ref[t]
        firsts = []
        for lane in range(0, width, LANES):
            here = spot[:, lane : lane + LANES]
            inside = (here >= bounds[:tile]) & (here < bounds[tile:])
            firsts.append(jnp.where(inside, 1.0, 0.0))
        first = jnp.concatenate(firsts, axis=1).astype(BF16)
        found = mxu(e_ref[t], first)
        begin = 128.0 * found[wide_b : wide_b + 1] + found[wide_b + 1 : wide_b + 2]
        rank = jnp.where(valid, spot - begin + 1.0, -1.0)
        rep_ref[:tile] = first
        rep_ref[tile:] = jnp.where(found[:wide_b] == rank, 1.0, 0.0).astype(BF16)

    def describe(step, held):
        rep_ref, x_ref, dx_ref, slope_ref, record_ref, side_ref = held[:6]
        t, _, valid = of_step(step)
        wide = unstacked(mxu(feat_ref[t], rep_ref[...]))
        keep = jnp.where(valid, 1.0, 0.0)
        row = lax.broadcasted_iota(I32, (8, width), 0)
        record = jnp.where(row == 3, keep, wide[:8])
        pair_ref[step] = record
        record_ref[...] = record
        kinds = wide[8:16]
        basis, slope, env, denv = radial_terms(wide[0:3], nb)
        x_ref[...] = right_operand(basis, [kinds, kinds, kinds])
        dx_ref[...] = right_operand(slope, [])
        slope_ref[...] = slope
        side_ref[...] = pad_rows([keep * denv, keep * env], width)

    def latent(held):
        _, x_ref, dx_ref, slope_ref, _, _, y_ref, r_ref, line_ref, _ = held
        y = mxu(a_y, x_ref[...])
        r_ref[...] = mxu(a_r, dx_ref[...])
        y_ref[...] = y[:hid]
        lin = jnp.sum(slope_ref[...] * (base + y[hid : hid + 8]), axis=0, keepdims=True)
        line_ref[...] = pad_rows([y[hid + 8 : hid + 9], lin], width)

    def channels(held):
        _, _, _, _, record_ref, side_ref, y_ref, r_ref, line_ref, gd_ref = held
        s_rows, t_rows = [], []
        for lane in range(0, width, LANES):
            s = jnp.zeros((8, LANES), F32)
            u = jnp.zeros((8, LANES), F32)
            for h in range(0, hid, 8):
                y = y_ref[h : h + 8, lane : lane + LANES]
                r = r_ref[h : h + 8, lane : lane + LANES]
                th = jnp.tanh(y)
                a = y * th
                g = th * (1.0 - a)
                s = s + wb_ref[h : h + 8, :] * a
                u = u + r * g
            s_rows.append(jnp.sum(s, axis=0, keepdims=True))
            t_rows.append(jnp.sum(u, axis=0, keepdims=True))
        s_all = jnp.concatenate(s_rows, axis=1) + line_ref[0:1]
        t_all = jnp.concatenate(t_rows, axis=1) + line_ref[1:2]
        g = side_ref[0:1] * s_all + side_ref[1:2] * t_all
        gd_ref[...] = stacked((2.0 * g) * record_ref[...])

    def gather(step, held):
        t = plan_ref[1 + 2 * jnp.clip(step, 0, total - 1)]
        acc_ref[t] = acc_ref[t] + unstacked(mxu_t(held[-1][...], held[0][...]))

    def rounds(i, carry):
        for m in range(4):
            step = 4 * i + m
            gather(step - 1, sets[(m + 3) % 4])
            latent(sets[(m + 1) % 4])
            describe(step + 2, sets[(m + 2) % 4])
            choose(step + 3, sets[(m + 3) % 4])
            channels(sets[m])
        return carry

    for ref in (sets[3][0], sets[3][-1]):
        ref[...] = jnp.zeros_like(ref)
    for step in range(3):
        choose(jnp.int32(step), sets[step])
    for step in range(2):
        describe(jnp.int32(step), sets[step])
    latent(sets[0])
    rotations = (total + 3) // 4
    lax.fori_loop(0, rotations, rounds, 0)
    gather(4 * rotations - 1, sets[3])
    grad_ref[...] = jnp.zeros_like(grad_ref)
    for t in range(tiles_own):
        own = t + half_tiles
        grad_ref[own] = grad_ref[own] + acc_ref[t, :, :tile]
        for k in range(slots):
            entry = jnp.maximum(list_ref[0, k, t], 0)
            grad_ref[entry] = grad_ref[entry] - acc_ref[t, :, (k + 1) * tile : (k + 2) * tile]
    whole = jnp.concatenate([grad_ref[i] for i in range(grad_ref.shape[0])], axis=1)
    atoms = pos_ref.shape[2]
    half = atoms // 2
    own_grad = whole[:, half : half + atoms]
    own_ref[...] = own_grad
    pieces = stacked(own_grad)
    for k, ref in ((0, to_lower_ref), (1, to_upper_ref)):
        sent = unstacked(mxu(pieces, selection(order_ref, k, atoms)))
        ghost = whole[:, :half] if k == 0 else whole[:, half + atoms :]
        ref[...] = pad_rows([sent[0:3], ghost[0:3]], half)


def finish_forces(
    weight, order_ref, target_ref, lower_ref, upper_ref, own_ref,
    to_lower_ref, to_upper_ref, from_lower_ref, from_upper_ref, forces_ref, v_ref,
):
    tiles, _, tile = v_ref.shape
    atoms = own_ref.shape[1]
    total = own_ref[0:3, :]
    for k, ref in ((0, from_lower_ref), (1, from_upper_ref)):
        total = total + unstacked(mxu_t(stacked(ref[...]), selection(order_ref, k, atoms)))[3:6]
    for i in range(3):
        forces_ref[i] = -total[i : i + 1]
    miss = total + jnp.concatenate([target_ref[i] for i in range(3)], axis=0)
    left = to_lower_ref[3:6, :] + from_lower_ref[0:3, :] + lower_ref[4:7, :]
    right = to_upper_ref[3:6, :] + from_upper_ref[0:3, :] + upper_ref[4:7, :]
    scaled = (2.0 * weight) * jnp.concatenate([left, miss, right], axis=1)
    scaled = pad_rows([scaled], scaled.shape[1])
    for i in range(tiles):
        v_ref[i] = scaled[:, i * tile : (i + 1) * tile]
    return weight * jnp.sum(miss * miss)


def param_kernel(
    nb, ns, plan_ref, list_ref, weight_ref, order_ref, target_ref, lower_ref, upper_ref, own_ref,
    to_lower_ref, to_upper_ref, from_lower_ref, from_upper_ref, pair_ref, rad_ref, center_ref, other_ref, out_ref,
    forces_ref, grads_ref,
    v_ref, va_ref, vb_ref, sets, acc_g, acc_f, acc_s, gram_ref,
):
    _, slots, tiles_own = list_ref.shape
    tile = v_ref.shape[2]
    half_tiles = tiles_own // 2
    hid = rad_ref.shape[1]
    width = pair_ref.shape[2]
    weight = weight_ref[0].astype(F32)
    loss = finish_forces(
        weight, order_ref, target_ref, lower_ref, upper_ref, own_ref,
        to_lower_ref, to_upper_ref, from_lower_ref, from_upper_ref, forces_ref, v_ref,
    )
    mid = nb + 2 * ns
    acc_g[...] = jnp.zeros_like(acc_g)
    acc_f[...] = jnp.zeros_like(acc_f)
    acc_s[...] = jnp.zeros_like(acc_s)
    gram_ref[...] = jnp.zeros_like(gram_ref)
    for t in range(tiles_own):
        va_ref[t] = jnp.concatenate([v_ref[t + half_tiles], jnp.zeros((8, LANES - tile), F32)], axis=1)
        vb_ref[t] = jnp.concatenate([v_ref[jnp.maximum(list_ref[0, k, t], 0)] for k in range(slots)], axis=1)
    stack, w_row, cols, w_col = tables(rad_ref, center_ref, other_ref, out_ref)
    half_cols = 0.5 * cols
    a_y = left_operand(half_cols[:, :nb], split(half_cols[:, nb:], 3))

    total = plan_ref[0]

    def front(step, held):
        y_ref, alpha_ref, g_cols, f_cols, x_rows = held[:5]
        t = plan_ref[1 + 2 * jnp.minimum(step, total - 1)]
        record = pair_ref[step]
        offsets = record[0:3]
        keep = record[3:4]
        index_a = jnp.broadcast_to(record[4:5].astype(I32), (8, width))
        index_b = jnp.broadcast_to(record[5:6].astype(I32), (8, width))
        va, vb = va_ref[t], vb_ref[t]
        diffs = []
        for lane in range(0, width, LANES):
            part_a = jnp.take_along_axis(va, index_a[:, lane : lane + LANES], axis=1, mode="promise_in_bounds")
            part_b = jnp.take_along_axis(vb, index_b[:, lane : lane + LANES], axis=1, mode="promise_in_bounds")
            diffs.append(part_a - part_b)
        dv = jnp.concatenate(diffs, axis=1)
        kinds = one_hot_rows(record[6:7], record[7:8], ns, width)
        basis, slope, env, denv = radial_terms(offsets, nb)
        c = (2.0 * keep) * jnp.sum(offsets * dv[0:3], axis=0, keepdims=True)
        alpha = c * denv
        beta_slope = (c * env) * slope
        y_ref[...] = mxu(a_y, right_operand(basis, [kinds, kinds, kinds]))
        alpha_ref[...] = jnp.broadcast_to(alpha, (8, width))
        x = jnp.concatenate([basis, kinds], axis=0)
        one = jnp.ones((8, width), F32)
        g_cols[...] = jnp.concatenate(
            split(jnp.concatenate([alpha * x, beta_slope], axis=0), 2), axis=0
        ).astype(BF16)
        f_cols[...] = jnp.concatenate(
            split(jnp.concatenate([beta_slope[j : j + 1] * x for j in range(nb)], axis=0), 2), axis=0
        ).astype(BF16)
        x_rows[...] = jnp.concatenate(split(x, 2) + [one, one], axis=0).astype(BF16)

    def middle(held, top, bottom):
        y_ref, alpha_ref, _, _, _, g_ref, f_ref = held
        for h in range(top, bottom, 16):
            s = acc_s[h : h + 16, :]
            for lane in range(0, width, LANES):
                alpha = alpha_ref[:, lane : lane + LANES]
                y = y_ref[h : h + 16, lane : lane + LANES]
                th = jnp.tanh(y)
                a = y * th
                u = 1.0 - a
                g = th * u
                f = u - th * g
                s = s + jnp.concatenate([alpha, alpha], axis=0) * a
                for ref, x in ((g_ref, g), (f_ref, f)):
                    high = x.astype(BF16)
                    ref[h : h + 16, lane : lane + LANES] = high
                    ref[hid + h : hid + h + 16, lane : lane + LANES] = (x - high.astype(F32)).astype(BF16)
            acc_s[h : h + 16, :] = s

    def rear(held, part):
        g_cols, f_cols, x_rows, g_ref, f_ref = held[2:]
        if part == 0:
            acc_f[...] += mxu_t(f_ref[...], f_cols[...])
        else:
            acc_g[...] += mxu_t(g_ref[...], g_cols[...])
            gram_ref[...] += mxu_t(x_rows[...], g_cols[...])

    def rounds(i, carry):
        for m in range(4):
            front(4 * i + m + 1, sets[(m + 1) % 4])
            rear(sets[(m + 3) % 4], 0)
            middle(sets[m], 0, hid // 2)
            rear(sets[(m + 3) % 4], 1)
            middle(sets[m], hid // 2, hid)
        return carry

    for ref in sets[3][2:]:
        ref[...] = jnp.zeros_like(ref)
    front(jnp.int32(0), sets[0])
    lax.fori_loop(0, (total + 3) // 4, rounds, 0)
    rear(sets[3], 0)
    rear(sets[3], 1)
    all_g = acc_g[:hid] + acc_g[hid:]
    all_f = acc_f[:hid] + acc_f[hid:]
    cols_g = mid + nb
    gram = gram_ref[:, :cols_g] + gram_ref[:, cols_g:]
    gram_x = gram[:mid] + gram[mid : 2 * mid]
    gram_one = gram[2 * mid : 2 * mid + 1]
    curved = all_g[:, :cols_g] + all_g[:, cols_g:]
    spread = jnp.dot(half_cols, gram_x, precision=HIGHEST, preferred_element_type=F32)
    first = 0.5 * (gram_one + spread + curved)
    sharp = 0.5 * (all_f[:, : nb * mid] + all_f[:, nb * mid :])
    d = first[:, :mid]
    for j in range(nb):
        d = d + cols[:, j : j + 1] * sharp[:, j * mid : (j + 1) * mid]
    slope_part = first[:, mid:]
    grad_rad = w_col * (d[:, :nb] + slope_part)
    grad_tables = w_col * d[:, nb:]
    grad_out = (
        jnp.sum(acc_s[...], axis=1, keepdims=True)
        + jnp.sum(half_cols * gram_one[:, :mid], axis=1, keepdims=True)
        + jnp.sum(slope_part * cols[:, :nb], axis=1, keepdims=True)
    )
    spare = jnp.zeros((hid, LANES - mid - 1), F32)
    turned = jnp.concatenate([grad_rad, grad_tables, grad_out, spare], axis=1).T
    rows = grads_ref.shape[0]
    row = lax.broadcasted_iota(I32, (rows, hid), 0)
    lane = lax.broadcasted_iota(I32, (rows, hid), 1)
    extra = jnp.where(lane == 0, loss, jnp.where(lane == 1, weight, 0.0))
    grads_ref[...] = jnp.where(row == mid + 1, extra, turned[:rows])


SMEM_SPEC = pl.BlockSpec(memory_space=pltpu.SMEM)
VMEM_SPEC = pl.BlockSpec(memory_space=pltpu.VMEM)
MESH = pl.DeviceIdType.MESH
MIB = 1024 * 1024


def swap(to_lower, to_upper, from_lower, from_upper, sems):
    me, count = lax.axis_index("space"), lax.axis_size("space")
    group = lax.axis_index("dp")
    upper, lower = lax.rem(me + 1, count), lax.rem(me + count - 1, count)
    up = pltpu.make_async_remote_copy(
        src_ref=to_upper, dst_ref=from_lower, send_sem=sems.at[0], recv_sem=sems.at[1],
        device_id=(group, upper), device_id_type=MESH,
    )
    down = pltpu.make_async_remote_copy(
        src_ref=to_lower, dst_ref=from_upper, send_sem=sems.at[2], recv_sem=sems.at[3],
        device_id=(group, lower), device_id_type=MESH,
    )
    return up, down


def greet():
    me, count = lax.axis_index("space"), lax.axis_size("space")
    group = lax.axis_index("dp")
    barrier = pltpu.get_barrier_semaphore()
    for other in (lax.rem(me + 1, count), lax.rem(me + count - 1, count)):
        pl.semaphore_signal(barrier, inc=1, device_id=(group, other), device_id_type=MESH)
    return barrier


def face_kernel(
    pos_ref, spec_ref, target_ref, order_ref, *refs,
):
    count = 5
    more, refs = refs[:count], refs[count:]
    lower_ref, upper_ref, pos_out, spec_out, target_out, order_out = refs[:6]
    more_out, refs = refs[6 : 6 + count], refs[6 + count :]
    to_lower, to_upper, from_lower, from_upper, sems, load_sems = refs
    barrier = greet()
    sources = (pos_ref, spec_ref, target_ref, order_ref) + more
    targets = (pos_out, spec_out, target_out, order_out) + more_out
    loads = [pltpu.make_async_copy(s, t, load_sems.at[i]) for i, (s, t) in enumerate(zip(sources, targets))]
    for load in loads:
        load.start()
    for load in loads[:4]:
        load.wait()
    atoms = pos_out.shape[2]
    rows = [pos_out[i] for i in range(3)] + [spec_out[...].astype(F32)] + [target_out[i] for i in range(3)]
    pieces = stacked(pad_rows(rows, atoms))
    to_lower[...] = unstacked(mxu(pieces, selection(order_out, 0, atoms)))
    to_upper[...] = unstacked(mxu(pieces, selection(order_out, 1, atoms)))
    pl.semaphore_wait(barrier, 2)
    up, down = swap(to_lower, to_upper, from_lower, from_upper, sems)
    up.start()
    down.start()
    for load in loads[4:]:
        load.wait()
    up.wait()
    down.wait()
    lower_ref[...] = from_lower[...]
    upper_ref[...] = from_upper[...]


def ghost_kernel(to_lower, to_upper, lower_ref, upper_ref, from_lower, from_upper, sems):
    barrier = greet()
    pl.semaphore_wait(barrier, 2)
    up, down = swap(to_lower, to_upper, from_lower, from_upper, sems)
    up.start()
    down.start()
    up.wait()
    down.wait()
    lower_ref[...] = from_lower[...]
    upper_ref[...] = from_upper[...]


def sum_kernel(x_ref, out_ref, near, part, far, near_send, near_recv, far_send, far_recv):
    group, me = lax.axis_index("dp"), lax.axis_index("space")
    groups, count = lax.axis_size("dp"), lax.axis_size("space")
    barrier = pltpu.get_barrier_semaphore()
    others = [(lax.rem(group + k, groups), me) for k in range(1, groups)]
    others += [(group, lax.rem(me + k, count)) for k in range(1, count)]
    for other in others:
        pl.semaphore_signal(barrier, inc=1, device_id=other, device_id_type=MESH)
    pl.semaphore_wait(barrier, len(others))

    def share(source, slots, send, recv, spot, peers):
        copies = []
        for k, other in enumerate(peers):
            copies.append(
                pltpu.make_async_remote_copy(
                    src_ref=source, dst_ref=slots.at[spot], send_sem=send.at[k], recv_sem=recv.at[k],
                    device_id=other, device_id_type=MESH,
                )
            )
            copies[-1].start()
        slots[spot] = source[...]
        for copy in copies:
            copy.wait()
        total = slots[0]
        for k in range(1, len(peers) + 1):
            total = total + slots[k]
        return total

    part[...] = share(x_ref, near, near_send, near_recv, group, others[: groups - 1])
    out_ref[...] = share(part, far, far_send, far_recv, me, others[groups - 1 :])


def final_kernel(nb, ns, atoms, domains, sum_ref, loss_ref, rad_ref, center_ref, other_ref, out_ref):
    last = nb + 2 * ns
    weight_total = sum_ref[last + 1 : last + 2, 1:2] / domains
    scale = 1.0 / (3.0 * atoms * domains * weight_total)
    loss_ref[...] = sum_ref[last + 1 : last + 2, 0:1] * scale
    rad_ref[...] = sum_ref[:nb] * scale
    center_ref[...] = sum_ref[nb : nb + ns] * scale
    other_ref[...] = sum_ref[nb + ns : last] * scale
    out_ref[...] = sum_ref[last : last + 1] * scale


def pool_force(tile_list, positions, species, order, lower, upper, params, width):
    atoms = positions.shape[2]
    half = atoms // 2
    _, slots, own = tile_list.shape
    tile = atoms // own
    tiles = 2 * own
    rad, center = params[0], params[1]
    nb, hid = rad.shape
    ns = center.shape[0]
    most = own * (-(-slots * tile * tile // width))
    wide_b = slots * tile
    held = (
        pltpu.VMEM((tile + wide_b, width), BF16),
        pltpu.VMEM((6 * nb + 6 * ns, width), BF16),
        pltpu.VMEM((6 * nb, width), BF16),
        pltpu.VMEM((nb, width), F32),
        pltpu.VMEM((8, width), F32),
        pltpu.VMEM((8, width), F32),
        pltpu.VMEM((hid, width), F32),
        pltpu.VMEM((hid, width), F32),
        pltpu.VMEM((8, width), F32),
        pltpu.VMEM((24, width), BF16),
    )
    return pl.pallas_call(
        functools.partial(force_kernel, nb, ns, width),
        out_shape=(
            jax.ShapeDtypeStruct((8, atoms), F32),
            jax.ShapeDtypeStruct((8, half), F32),
            jax.ShapeDtypeStruct((8, half), F32),
            jax.ShapeDtypeStruct((most + 8, 8, width), F32),
            jax.ShapeDtypeStruct((2 * most + 1,), I32),
        ),
        in_specs=[SMEM_SPEC] + [VMEM_SPEC] * 9,
        out_specs=(VMEM_SPEC,) * 4 + (SMEM_SPEC,),
        scratch_shapes=[
            pltpu.VMEM((tiles, 8, tile), F32),
            pltpu.VMEM((tiles, tile, 8), F32),
            pltpu.VMEM((tiles, 8, tile), F32),
            pltpu.VMEM((own, wide_b + 16, tile), BF16),
            pltpu.VMEM((own, 2 * tile, LANES), F32),
            pltpu.VMEM((own, 48, tile + wide_b), BF16),
            pltpu.SMEM((own,), I32),
            (held,) * 4,
            pltpu.VMEM((hid, LANES), F32),
            pltpu.VMEM((own, 8, tile + wide_b), F32),
        ],
        compiler_params=pltpu.CompilerParams(vmem_limit_bytes=32 * MIB),
        name="pool_force",
    )(tile_list, positions, species, order, lower, upper, *params)


def pool_params(plan, tile_list, weights, order, targets, ghosts, sums, pairs, params):
    _, slots, own = tile_list.shape
    atoms = targets.shape[2]
    tile = atoms // own
    width = pairs.shape[2]
    rad, center = params[0], params[1]
    nb, hid = rad.shape
    ns = center.shape[0]
    mid = nb + 2 * ns
    rows = mid + 2
    held = (
        pltpu.VMEM((hid, width), F32),
        pltpu.VMEM((8, width), F32),
        pltpu.VMEM((2 * (mid + nb), width), BF16),
        pltpu.VMEM((2 * nb * mid, width), BF16),
        pltpu.VMEM((2 * mid + 16, width), BF16),
    ) + (pltpu.VMEM((2 * hid, width), BF16),) * 2
    return pl.pallas_call(
        functools.partial(param_kernel, nb, ns),
        out_shape=(
            jax.ShapeDtypeStruct(targets.shape, F32),
            jax.ShapeDtypeStruct((rows, hid), F32),
        ),
        in_specs=[SMEM_SPEC] * 3 + [VMEM_SPEC] * 14,
        out_specs=(VMEM_SPEC,) * 2,
        scratch_shapes=[
            pltpu.VMEM((2 * own, 8, tile), F32),
            pltpu.VMEM((own, 8, LANES), F32),
            pltpu.VMEM((own, 8, LANES), F32),
            (held,) * 4,
            pltpu.VMEM((2 * hid, 2 * (mid + nb)), F32),
            pltpu.VMEM((2 * hid, 2 * nb * mid), F32),
            pltpu.VMEM((hid, LANES), F32),
            pltpu.VMEM((2 * mid + 16, 2 * (mid + nb)), F32),
        ],
        compiler_params=pltpu.CompilerParams(vmem_limit_bytes=32 * MIB),
        name="pool_params",
    )(plan, tile_list, weights, order, targets, *ghosts, *sums, pairs, *params)


def face_exchange(positions, species, targets, order, *others):
    half = order.shape[2]
    box = jax.ShapeDtypeStruct((8, half), F32)
    arrays = (positions, species, targets, order) + others
    held = tuple(jax.ShapeDtypeStruct(x.shape, x.dtype) for x in arrays)
    return pl.pallas_call(
        face_kernel,
        out_shape=(box, box) + held,
        in_specs=[pl.BlockSpec(memory_space=pltpu.HBM)] * len(arrays),
        out_specs=(VMEM_SPEC,) * (2 + len(arrays)),
        scratch_shapes=[pltpu.VMEM((8, half), F32)] * 4
        + [pltpu.SemaphoreType.DMA((4,)), pltpu.SemaphoreType.DMA((len(arrays),))],
        compiler_params=pltpu.CompilerParams(collective_id=0, has_side_effects=True, vmem_limit_bytes=8 * MIB),
        name="face_exchange",
    )(*[pltpu.with_memory_space_constraint(x, pltpu.HBM) for x in arrays])


def ghost_exchange(to_lower, to_upper):
    box = jax.ShapeDtypeStruct(to_lower.shape, F32)
    return pl.pallas_call(
        ghost_kernel,
        out_shape=(box, box),
        in_specs=[VMEM_SPEC] * 2,
        out_specs=(VMEM_SPEC,) * 2,
        scratch_shapes=[pltpu.VMEM(to_lower.shape, F32)] * 2 + [pltpu.SemaphoreType.DMA((4,))],
        compiler_params=pltpu.CompilerParams(collective_id=1, has_side_effects=True, vmem_limit_bytes=4 * MIB),
        name="ghost_exchange",
    )(to_lower, to_upper)


def sum_everywhere(x):
    groups, count = lax.axis_size("dp"), lax.axis_size("space")
    return pl.pallas_call(
        sum_kernel,
        out_shape=jax.ShapeDtypeStruct(x.shape, F32),
        in_specs=[VMEM_SPEC],
        out_specs=VMEM_SPEC,
        scratch_shapes=[
            pltpu.VMEM((groups,) + x.shape, F32),
            pltpu.VMEM(x.shape, F32),
            pltpu.VMEM((count,) + x.shape, F32),
            pltpu.SemaphoreType.DMA((groups - 1,)),
            pltpu.SemaphoreType.DMA((groups - 1,)),
            pltpu.SemaphoreType.DMA((count - 1,)),
            pltpu.SemaphoreType.DMA((count - 1,)),
        ],
        compiler_params=pltpu.CompilerParams(
            collective_id=2, has_side_effects=True, vmem_limit_bytes=8 * MIB
        ),
        name="sum_everywhere",
    )(x)


def finish(summed, nb, ns, atoms):
    hid = summed.shape[1]
    domains = lax.axis_size("space")
    shapes = ((1, 1), (nb, hid), (ns, hid), (ns, hid), (1, hid))
    return pl.pallas_call(
        functools.partial(final_kernel, nb, ns, float(atoms), float(domains)),
        out_shape=tuple(jax.ShapeDtypeStruct(s, F32) for s in shapes),
        in_specs=[VMEM_SPEC],
        out_specs=(VMEM_SPEC,) * len(shapes),
        compiler_params=pltpu.CompilerParams(vmem_limit_bytes=4 * MIB),
        name="finish",
    )(summed)


def body(positions, species, ref_forces, send_lists, tile_lists, weights, w_rad, emb_center, emb_other, w_out):
    nb = w_rad.shape[0]
    ns = emb_center.shape[0]
    positions, ref_forces = positions.transpose(1, 0, 2), ref_forces.transpose(1, 0, 2)
    tile_lists = tile_lists.transpose(0, 2, 1)
    lower, upper, positions, species, ref_forces, send_lists, tile_lists, *params = face_exchange(
        positions, species, ref_forces, send_lists, tile_lists, w_rad, emb_center, emb_other, w_out[None]
    )
    own_grad, to_lower, to_upper, pairs, plan = pool_force(
        tile_lists, positions, species, send_lists, lower, upper, params, 4 * LANES
    )
    from_lower, from_upper = ghost_exchange(to_lower, to_upper)
    forces, grads = pool_params(
        plan, tile_lists, weights, send_lists, ref_forces, (lower, upper),
        (own_grad, to_lower, to_upper, from_lower, from_upper), pairs, params,
    )
    summed = sum_everywhere(grads)
    loss, grad_rad, grad_center, grad_other, grad_out = finish(summed, nb, ns, positions.shape[2])
    forces = forces.transpose(1, 0, 2)
    return forces, loss[0, 0], grad_rad, grad_center, grad_other, grad_out[0]


def solution(mesh):
    return jax.shard_map(
        body,
        mesh=mesh,
        in_specs=(
            P("dp", None, "space"),
            P("dp", "space"),
            P("dp", None, "space"),
            P("dp", "space", None),
            P("dp", "space", None),
            P("dp"),
            P(),
            P(),
            P(),
            P(),
        ),
        out_specs=(P("dp", None, "space"), P(), P(), P(), P(), P()),
        check_vma=False,
    )
```

```python
import functools

import jax
import jax.numpy as jnp
from jax import lax
from jax.experimental import pallas as pl
from jax.experimental.pallas import tpu as pltpu
from jax.sharding import PartitionSpec as P

CUTOFF = 1.0
DOMAIN_WIDTH = 2.0
F32 = jnp.float32
BF16 = jnp.bfloat16
I32 = jnp.int32
LAST = (((1,), (1,)), ((), ()))
LANES = 128
HIGHEST = lax.Precision.HIGHEST


def split(x, parts):
    pieces = []
    for _ in range(parts - 1):
        high = x.astype(BF16).astype(F32)
        pieces.append(high)
        x = x - high
    pieces.append(x.astype(BF16).astype(F32))
    return pieces


def left_operand(x, exact):
    w1, w2, w3 = split(x, 3)
    return jnp.concatenate([w1, w1, w2, w1, w2, w3] + exact, axis=1).astype(BF16)


def right_operand(x, exact):
    b1, b2, b3 = split(x, 3)
    return jnp.concatenate([b1, b2, b1, b3, b2, b1] + exact, axis=0).astype(BF16)


def mxu(a, b):
    return jnp.dot(a, b, preferred_element_type=F32)


def mxu_t(a, b):
    return lax.dot_general(a, b, LAST, preferred_element_type=F32)


def radial_terms(offsets, nb):
    q = jnp.sum(offsets * offsets, axis=0, keepdims=True) / (CUTOFF * CUTOFF)
    scale = float(nb - 1)
    centers = lax.broadcasted_iota(I32, (nb, 1), 0).astype(F32) / scale
    arg = (q - centers) * scale
    basis = jnp.exp(-(arg * arg))
    slope = (-2.0 * scale) * arg * basis
    inner = jnp.maximum(1.0 - q, 0.0)
    return basis, slope, inner * inner, -2.0 * inner


def tables(rad_ref, center_ref, other_ref, out_ref):
    stack = jnp.concatenate([rad_ref[...], center_ref[...], other_ref[...]], axis=0)
    w_row = out_ref[...]
    both = jnp.concatenate([stack, jnp.broadcast_to(w_row, (8, w_row.shape[1]))], axis=0).T
    count = stack.shape[0]
    return stack, w_row, both[:, :count], both[:, count : count + 1]


def one_hot_rows(code_a, code_b, ns, width):
    row = lax.broadcasted_iota(I32, (2 * ns, width), 0).astype(F32)
    code = jnp.where(row < ns, code_a, code_b + float(ns))
    return jnp.where(code == row, 1.0, 0.0)


def prepare(t, slots, own, list_ref, rows_ref, cols_ref, e_ref, bound_ref, feat_ref, ns):
    tile = rows_ref.shape[2]
    wide = slots * tile
    entries = [list_ref[0, k, t] for k in range(slots)]
    safe = [jnp.maximum(c, 0) for c in entries]
    xa = rows_ref[own]
    xb = jnp.concatenate([cols_ref[c] for c in safe], axis=0)
    q = jnp.zeros((wide, tile), F32)
    for i in range(3):
        diff = xb[:, i : i + 1] - xa[i : i + 1, :]
        q = q + diff * diff
    b_row = lax.broadcasted_iota(I32, (tile, tile), 0)
    a_lane = lax.broadcasted_iota(I32, (tile, tile), 1)
    allowed = []
    for c in entries:
        limit = jnp.where(c >= 0, 1.0, 0.0)
        allowed.append(jnp.where((b_row == a_lane) & (c == own), 0.0, limit))
    near = jnp.where(q / (CUTOFF * CUTOFF) < 1.0, jnp.concatenate(allowed, axis=0), 0.0)
    near_b = near.astype(BF16)
    r = lax.broadcasted_iota(I32, (wide, wide), 0)
    c = lax.broadcasted_iota(I32, (wide, wide), 1)
    lower = jnp.where(c < r, 1.0, 0.0).astype(BF16)
    rank = jnp.where(near > 0.0, mxu(lower, near_b) + 1.0, 0.0)
    row2 = lax.broadcasted_iota(I32, (2 * tile, tile), 0)
    col2 = lax.broadcasted_iota(I32, (2 * tile, tile), 1)
    reach = jnp.where(row2 < tile, row2 - 1, row2 - tile)
    below = jnp.where(col2 <= reach, 1.0, 0.0).astype(BF16)
    edges = jnp.sum(mxu_t(below, near_b), axis=1, keepdims=True)
    bound_ref[t] = jnp.broadcast_to(edges, (2 * tile, LANES))
    per_atom = jnp.sum(near, axis=0, keepdims=True)
    before = jnp.where(b_row < a_lane, 1.0, 0.0).astype(BF16)
    start = mxu(jnp.broadcast_to(per_atom, (16, tile)).astype(BF16), before)
    high = jnp.floor(start * (1.0 / 128.0))
    rest = start - 128.0 * high
    which = lax.broadcasted_iota(I32, (16, tile), 0)
    codes = jnp.where(which == 0, high, jnp.where(which == 1, rest, 0.0))
    found = jnp.concatenate([rank, codes], axis=0)
    e_ref[t] = jnp.concatenate([jnp.zeros((wide + 16, tile + wide), F32), found], axis=1).astype(BF16)
    row = lax.broadcasted_iota(I32, (8, tile), 0)
    lane = lax.broadcasted_iota(I32, (8, tile), 1).astype(F32)
    kind_row = row.astype(F32)
    kind = xa[3:4, :]
    first = jnp.where(row < 3, xa, jnp.where(row == 4, lane, jnp.where(row == 6, kind, 0.0)))
    first_kind = jnp.where((row < ns) & (kind == kind_row), 1.0, 0.0)
    parts = [jnp.concatenate([first, first_kind], axis=0)]
    for k in range(slots):
        other = rows_ref[safe[k]]
        kind = other[3:4, :]
        second = jnp.where(
            row < 3, -other, jnp.where(row == 5, lane + float(k * tile), jnp.where(row == 7, kind, 0.0))
        )
        second_kind = jnp.where((row >= ns) & (kind + float(ns) == kind_row), 1.0, 0.0)
        parts.append(jnp.concatenate([second, second_kind], axis=0))
    parts.append(jnp.zeros((16, tile), F32))
    feat_ref[t] = jnp.concatenate(split(jnp.concatenate(parts, axis=1), 3), axis=0).astype(BF16)
    return per_atom


def pieces_of(count_ref, width):
    return [(count_ref[t] + (width - 1)) // width for t in range(count_ref.shape[0])]


def locate(step, pieces, others):
    t, begin, place, end = jnp.int32(0), jnp.int32(0), jnp.int32(0), jnp.int32(0)
    for count, other in zip(pieces[:-1], others[:-1]):
        end = end + count
        past = step >= end
        t = t + jnp.where(past, 1, 0)
        begin = begin + jnp.where(past, count, 0)
        place = place + jnp.where(past, other, 0)
    return t, step - begin, place


def selection(order_ref, k, atoms):
    count = order_ref.shape[2]
    row = lax.broadcasted_iota(I32, (atoms, count), 0)
    return jnp.where(row == order_ref[0, k : k + 1, :], 1.0, 0.0).astype(BF16)


def stacked(x):
    return jnp.concatenate(split(x, 3), axis=0).astype(BF16)


def unstacked(x):
    rows = x.shape[0] // 3
    return x[:rows] + (x[rows : 2 * rows] + x[2 * rows :])


def pad_rows(parts, width):
    count = sum(p.shape[0] for p in parts)
    return jnp.concatenate(parts + [jnp.zeros((8 - count, width), F32)], axis=0)


def fill_pool(pos_ref, spec_ref, lower_ref, upper_ref, rows_ref, cols_ref):
    tiles, _, tile = rows_ref.shape
    half = lower_ref.shape[1]
    atoms = pos_ref.shape[2]
    own = pad_rows([pos_ref[i] for i in range(3)] + [spec_ref[...].astype(F32)], atoms)
    row = lax.broadcasted_iota(I32, (8, half), 0)
    shift = jnp.where(row == 0, DOMAIN_WIDTH, 0.0)
    left = jnp.where(row < 4, lower_ref[...] - shift, 0.0)
    right = jnp.where(row < 4, upper_ref[...] + shift, 0.0)
    pool = jnp.concatenate([left, own, right], axis=1)
    turned = pool.T
    for i in range(tiles):
        rows_ref[i] = pool[:, i * tile : (i + 1) * tile]
        cols_ref[i] = turned[i * tile : (i + 1) * tile, :]


def force_kernel(
    nb, ns, width, list_ref, pos_ref, spec_ref, order_ref, lower_ref, upper_ref,
    rad_ref, center_ref, other_ref, out_ref,
    own_ref, to_lower_ref, to_upper_ref, pair_ref, count_ref,
    rows_ref, cols_ref, grad_ref, e_ref, bound_ref, feat_ref, sets, wb_ref, acc_ref,
):
    _, slots, tiles_own = list_ref.shape
    tile = rows_ref.shape[2]
    fill_pool(pos_ref, spec_ref, lower_ref, upper_ref, rows_ref, cols_ref)
    wide_b = slots * tile
    half_tiles = tiles_own // 2
    hid = rad_ref.shape[1]
    near = [
        prepare(t, slots, t + half_tiles, list_ref, rows_ref, cols_ref, e_ref, bound_ref, feat_ref, ns)
        for t in range(tiles_own)
    ]
    for t in range(tiles_own):
        count_ref[t] = jnp.sum(near[t]).astype(I32)
    pieces = pieces_of(count_ref, width)
    total = sum(pieces)
    acc_ref[...] = jnp.zeros_like(acc_ref)
    stack, w_row, cols, w_col = tables(rad_ref, center_ref, other_ref, out_ref)
    half_cols = 0.5 * cols
    weighted = 0.5 * w_row * stack[:nb]
    linear = jnp.dot(
        jnp.concatenate([weighted, w_row, jnp.zeros((7, hid), F32)], axis=0), half_cols,
        precision=HIGHEST, preferred_element_type=F32,
    )
    base = jnp.sum(weighted, axis=1, keepdims=True)
    y_rows = jnp.concatenate([half_cols, linear], axis=0)
    a_y = left_operand(y_rows[:, :nb], split(y_rows[:, nb:], 3)).astype(F32)
    a_r = left_operand((0.5 * w_col) * cols[:, :nb], []).astype(F32)
    gap = -a_y.shape[1] % 16
    a_y = jnp.concatenate([a_y, jnp.zeros((a_y.shape[0], gap + a_r.shape[1]), F32)], axis=1)
    a_r = jnp.concatenate([jnp.zeros((hid, a_y.shape[1] - a_r.shape[1]), F32), a_r], axis=1)
    a_all = jnp.concatenate([a_y, a_r], axis=0).astype(BF16)
    wb_ref[...] = jnp.broadcast_to(w_col, wb_ref.shape)

    def of_step(step):
        t, local, _ = locate(jnp.minimum(step, total - 1), pieces, pieces)
        spot = (local * width + lax.broadcasted_iota(I32, (1, width), 1)).astype(F32)
        return t, spot, spot < jnp.where(step < total, count_ref[t], 0).astype(F32)

    def first_of(step):
        t, spot, _ = of_step(step)
        bounds = bound_ref[t]
        firsts = []
        for lane in range(0, width, LANES):
            here = spot[:, lane : lane + LANES]
            inside = (here >= bounds[:tile]) & (here < bounds[tile:])
            firsts.append(jnp.where(inside, 1.0, 0.0))
        return jnp.concatenate(firsts, axis=1).astype(BF16)

    def second_of(step, found):
        _, spot, valid = of_step(step)
        begin = 128.0 * found[wide_b : wide_b + 1] + found[wide_b + 1 : wide_b + 2]
        rank = jnp.where(valid, spot - begin + 1.0, -1.0)
        return jnp.where(found[:wide_b] == rank, 1.0, 0.0).astype(BF16)

    def describe(step, held, after):
        rep_ref, x_ref, slope_ref, record_ref, side_ref = held[:5]
        t, _, valid = of_step(step)
        first = first_of(step + 1)
        rep_ref[tile + wide_b :] = first
        after[0][:tile] = first
        left = jnp.concatenate([feat_ref[t], e_ref[of_step(step + 1)[0]]], axis=0)
        both = mxu(left, rep_ref[...])
        after[0][tile : tile + wide_b] = second_of(step + 1, both[48:])
        wide = unstacked(both[:48])
        keep = jnp.where(valid, 1.0, 0.0)
        row = lax.broadcasted_iota(I32, (8, width), 0)
        record = jnp.where(row == 3, keep, wide[:8])
        pair_ref[step] = record
        record_ref[...] = record
        kinds = wide[8:16]
        basis, slope, env, denv = radial_terms(wide[0:3], nb)
        b1, b2, b3 = split(basis, 3)
        s1, s2, s3 = split(slope, 3)
        blank = [jnp.zeros((gap, width), F32)] if gap else []
        x = [b1, b2, b1, b3, b2, b1, kinds, kinds, kinds] + blank + [s1, s2, s1, s3, s2, s1]
        x_ref[...] = jnp.concatenate(x, axis=0).astype(BF16)
        slope_ref[...] = slope
        side_ref[...] = pad_rows([keep * denv, keep * env], width)

    def latent(held):
        x_ref, slope_ref = held[1:3]
        y_ref, r_ref, line_ref = held[5:8]
        y = mxu(a_all, x_ref[...])
        y_ref[...] = y[:hid]
        r_ref[...] = y[hid + 16 :]
        lin = jnp.sum(slope_ref[...] * (base + y[hid : hid + 8]), axis=0, keepdims=True)
        line_ref[...] = pad_rows([y[hid + 8 : hid + 9], lin], width)

    def channels(held):
        record_ref, side_ref, y_ref, r_ref, line_ref, gd_ref = held[3:]
        s_rows, t_rows = [], []
        for lane in range(0, width, LANES):
            s = jnp.zeros((8, LANES), F32)
            u = jnp.zeros((8, LANES), F32)
            for h in range(0, hid, 8):
                y = y_ref[h : h + 8, lane : lane + LANES]
                r = r_ref[h : h + 8, lane : lane + LANES]
                th = jnp.tanh(y)
                a = y * th
                g = th * (1.0 - a)
                s = s + wb_ref[h : h + 8, :] * a
                u = u + r * g
            s_rows.append(jnp.sum(s, axis=0, keepdims=True))
            t_rows.append(jnp.sum(u, axis=0, keepdims=True))
        s_all = jnp.concatenate(s_rows, axis=1) + line_ref[0:1]
        t_all = jnp.concatenate(t_rows, axis=1) + line_ref[1:2]
        g = side_ref[0:1] * s_all + side_ref[1:2] * t_all
        gd_ref[...] = stacked((2.0 * g) * record_ref[...])

    def gather(step, held):
        t, _, _ = locate(jnp.clip(step, 0, total - 1), pieces, pieces)
        acc_ref[t] = acc_ref[t] + unstacked(mxu_t(held[-1][...], held[0][: tile + wide_b]))

    def rounds(i, carry):
        for m in range(4):
            step = 4 * i + m
            gather(step - 1, sets[(m + 3) % 4])
            describe(step + 2, sets[(m + 2) % 4], sets[(m + 3) % 4])
            latent(sets[(m + 1) % 4])
            channels(sets[m])
        return carry

    for ref in (sets[3][0], sets[3][-1]):
        ref[...] = jnp.zeros_like(ref)
    first = first_of(jnp.int32(0))
    sets[0][0][:tile] = first
    found = mxu(e_ref[of_step(jnp.int32(0))[0], :, tile + wide_b :], first)
    sets[0][0][tile : tile + wide_b] = second_of(jnp.int32(0), found)
    for step in range(2):
        describe(jnp.int32(step), sets[step], sets[step + 1])
    latent(sets[0])
    rotations = (total + 3) // 4
    lax.fori_loop(0, rotations, rounds, 0)
    gather(4 * rotations - 1, sets[3])
    grad_ref[...] = jnp.zeros_like(grad_ref)
    for t in range(tiles_own):
        own = t + half_tiles
        grad_ref[own] = grad_ref[own] + acc_ref[t, :, :tile]
        for k in range(slots):
            entry = jnp.maximum(list_ref[0, k, t], 0)
            grad_ref[entry] = grad_ref[entry] - acc_ref[t, :, (k + 1) * tile : (k + 2) * tile]
    whole = jnp.concatenate([grad_ref[i] for i in range(grad_ref.shape[0])], axis=1)
    atoms = pos_ref.shape[2]
    half = atoms // 2
    own_grad = whole[:, half : half + atoms]
    own_ref[...] = own_grad
    pieces = stacked(own_grad)
    for k, ref in ((0, to_lower_ref), (1, to_upper_ref)):
        sent = unstacked(mxu(pieces, selection(order_ref, k, atoms)))
        ghost = whole[:, :half] if k == 0 else whole[:, half + atoms :]
        ref[...] = pad_rows([sent[0:3], ghost[0:3]], half)


def finish_forces(
    weight, order_ref, target_ref, lower_ref, upper_ref, own_ref,
    to_lower_ref, to_upper_ref, from_lower_ref, from_upper_ref, forces_ref, v_ref,
):
    tiles, _, tile = v_ref.shape
    atoms = own_ref.shape[1]
    total = own_ref[0:3, :]
    for k, ref in ((0, from_lower_ref), (1, from_upper_ref)):
        total = total + unstacked(mxu_t(stacked(ref[...]), selection(order_ref, k, atoms)))[3:6]
    for i in range(3):
        forces_ref[i] = -total[i : i + 1]
    miss = total + jnp.concatenate([target_ref[i] for i in range(3)], axis=0)
    left = to_lower_ref[3:6, :] + from_lower_ref[0:3, :] + lower_ref[4:7, :]
    right = to_upper_ref[3:6, :] + from_upper_ref[0:3, :] + upper_ref[4:7, :]
    scaled = (2.0 * weight) * jnp.concatenate([left, miss, right], axis=1)
    scaled = pad_rows([scaled], scaled.shape[1])
    for i in range(tiles):
        v_ref[i] = scaled[:, i * tile : (i + 1) * tile]
    return weight * jnp.sum(miss * miss)


def param_kernel(
    nb, ns, width, count_ref, list_ref, weight_ref, order_ref, target_ref, lower_ref, upper_ref, own_ref,
    to_lower_ref, to_upper_ref, from_lower_ref, from_upper_ref, pair_ref, rad_ref, center_ref, other_ref, out_ref,
    forces_ref, grads_ref,
    v_ref, va_ref, vb_ref, sets, acc_g, acc_f, acc_s, gram_ref,
):
    _, slots, tiles_own = list_ref.shape
    tile = v_ref.shape[2]
    half_tiles = tiles_own // 2
    hid = rad_ref.shape[1]
    outer = pair_ref.shape[2]
    weight = weight_ref[0].astype(F32)
    loss = finish_forces(
        weight, order_ref, target_ref, lower_ref, upper_ref, own_ref,
        to_lower_ref, to_upper_ref, from_lower_ref, from_upper_ref, forces_ref, v_ref,
    )
    mid = nb + 2 * ns
    acc_g[...] = jnp.zeros_like(acc_g)
    acc_f[...] = jnp.zeros_like(acc_f)
    acc_s[...] = jnp.zeros_like(acc_s)
    gram_ref[...] = jnp.zeros_like(gram_ref)
    for t in range(tiles_own):
        va_ref[t] = jnp.concatenate([v_ref[t + half_tiles], jnp.zeros((8, LANES - tile), F32)], axis=1)
        vb_ref[t] = jnp.concatenate([v_ref[jnp.maximum(list_ref[0, k, t], 0)] for k in range(slots)], axis=1)
    stack, w_row, cols, w_col = tables(rad_ref, center_ref, other_ref, out_ref)
    half_cols = 0.5 * cols
    a_y = left_operand(half_cols[:, :nb], split(half_cols[:, nb:], 3))

    pieces, chunks = pieces_of(count_ref, width), pieces_of(count_ref, outer)
    total = sum(pieces)
    share = outer // width

    def front(step, held):
        y_ref, alpha_ref, g_cols, f_cols, x_rows = held[:5]
        t, local, place = locate(jnp.minimum(step, total - 1), pieces, chunks)
        lane = pl.multiple_of(local % share * width, width)
        record = pair_ref[place + local // share, :, pl.ds(lane, width)]
        offsets = record[0:3]
        keep = record[3:4] * jnp.where(step < total, 1.0, 0.0)
        index_a = jnp.broadcast_to(record[4:5].astype(I32), (8, width))
        index_b = jnp.broadcast_to(record[5:6].astype(I32), (8, width))
        va, vb = va_ref[t], vb_ref[t]
        diffs = []
        for lane in range(0, width, LANES):
            part_a = jnp.take_along_axis(va, index_a[:, lane : lane + LANES], axis=1, mode="promise_in_bounds")
            part_b = jnp.take_along_axis(vb, index_b[:, lane : lane + LANES], axis=1, mode="promise_in_bounds")
            diffs.append(part_a - part_b)
        dv = jnp.concatenate(diffs, axis=1)
        kinds = one_hot_rows(record[6:7], record[7:8], ns, width)
        basis, slope, env, denv = radial_terms(offsets, nb)
        c = (2.0 * keep) * jnp.sum(offsets * dv[0:3], axis=0, keepdims=True)
        alpha = c * denv
        beta_slope = (c * env) * slope
        y_ref[...] = mxu(a_y, right_operand(basis, [kinds, kinds, kinds]))
        alpha_ref[...] = jnp.broadcast_to(alpha, (8, width))
        x = jnp.concatenate([basis, kinds], axis=0)
        one = jnp.ones((8, width), F32)
        g_cols[...] = jnp.concatenate(
            split(jnp.concatenate([alpha * x, beta_slope], axis=0), 2), axis=0
        ).astype(BF16)
        f_cols[...] = jnp.concatenate(
            split(jnp.concatenate([beta_slope[j : j + 1] * x for j in range(nb)], axis=0), 2), axis=0
        ).astype(BF16)
        x_rows[...] = jnp.concatenate(split(x, 2) + [one, one], axis=0).astype(BF16)

    def middle(held, top, bottom):
        y_ref, alpha_ref, _, _, _, g_ref, f_ref = held
        for h in range(top, bottom, 16):
            s = acc_s[h : h + 16, :]
            for lane in range(0, width, LANES):
                alpha = alpha_ref[:, lane : lane + LANES]
                y = y_ref[h : h + 16, lane : lane + LANES]
                th = jnp.tanh(y)
                a = y * th
                u = 1.0 - a
                g = th * u
                f = u - th * g
                s = s + jnp.concatenate([alpha, alpha], axis=0) * a
                for ref, x in ((g_ref, g), (f_ref, f)):
                    high = x.astype(BF16)
                    ref[h : h + 16, lane : lane + LANES] = high
                    ref[hid + h : hid + h + 16, lane : lane + LANES] = (x - high.astype(F32)).astype(BF16)
            acc_s[h : h + 16, :] = s

    def rear(held, part):
        g_cols, f_cols, x_rows, g_ref, f_ref = held[2:]
        if part == 0:
            acc_f[...] += mxu_t(f_cols[...], f_ref[:hid])
            acc_f[: nb * mid] += mxu_t(f_cols[: nb * mid], f_ref[hid:])
        else:
            acc_g[...] += mxu_t(g_cols[...], g_ref[:hid])
            acc_g[: mid + nb] += mxu_t(g_cols[: mid + nb], g_ref[hid:])
            gram_ref[...] += mxu_t(x_rows[...], g_cols[...])

    def rounds(i, carry):
        for m in range(4):
            front(4 * i + m + 1, sets[(m + 1) % 4])
            rear(sets[(m + 3) % 4], 0)
            middle(sets[m], 0, hid // 2)
            rear(sets[(m + 3) % 4], 1)
            middle(sets[m], hid // 2, hid)
        return carry

    for ref in sets[3][2:]:
        ref[...] = jnp.zeros_like(ref)
    front(jnp.int32(0), sets[0])
    lax.fori_loop(0, (total + 3) // 4, rounds, 0)
    rear(sets[3], 0)
    rear(sets[3], 1)
    all_g = acc_g[: mid + nb] + acc_g[mid + nb :]
    all_g = jnp.concatenate([all_g, jnp.zeros((LANES - mid - nb, hid), F32)], axis=0).T
    all_f = (acc_f[: nb * mid] + acc_f[nb * mid :]).T
    cols_g = mid + nb
    gram = gram_ref[:, :cols_g] + gram_ref[:, cols_g:]
    gram_x = gram[:mid] + gram[mid : 2 * mid]
    gram_one = gram[2 * mid : 2 * mid + 1]
    curved = all_g[:, :cols_g]
    spread = jnp.dot(half_cols, gram_x, precision=HIGHEST, preferred_element_type=F32)
    first = 0.5 * (gram_one + spread + curved)
    sharp = 0.5 * all_f
    d = first[:, :mid]
    for j in range(nb):
        d = d + cols[:, j : j + 1] * sharp[:, j * mid : (j + 1) * mid]
    slope_part = first[:, mid:]
    grad_rad = w_col * (d[:, :nb] + slope_part)
    grad_tables = w_col * d[:, nb:]
    grad_out = (
        jnp.sum(acc_s[...], axis=1, keepdims=True)
        + jnp.sum(half_cols * gram_one[:, :mid], axis=1, keepdims=True)
        + jnp.sum(slope_part * cols[:, :nb], axis=1, keepdims=True)
    )
    spare = jnp.zeros((hid, LANES - mid - 1), F32)
    turned = jnp.concatenate([grad_rad, grad_tables, grad_out, spare], axis=1).T
    rows = grads_ref.shape[0]
    row = lax.broadcasted_iota(I32, (rows, hid), 0)
    lane = lax.broadcasted_iota(I32, (rows, hid), 1)
    extra = jnp.where(lane == 0, loss, jnp.where(lane == 1, weight, 0.0))
    grads_ref[...] = jnp.where(row == mid + 1, extra, turned[:rows])


SMEM_SPEC = pl.BlockSpec(memory_space=pltpu.SMEM)
VMEM_SPEC = pl.BlockSpec(memory_space=pltpu.VMEM)
MESH = pl.DeviceIdType.MESH
MIB = 1024 * 1024


def swap(to_lower, to_upper, from_lower, from_upper, sems):
    me, count = lax.axis_index("space"), lax.axis_size("space")
    group = lax.axis_index("dp")
    upper, lower = lax.rem(me + 1, count), lax.rem(me + count - 1, count)
    up = pltpu.make_async_remote_copy(
        src_ref=to_upper, dst_ref=from_lower, send_sem=sems.at[0], recv_sem=sems.at[1],
        device_id=(group, upper), device_id_type=MESH,
    )
    down = pltpu.make_async_remote_copy(
        src_ref=to_lower, dst_ref=from_upper, send_sem=sems.at[2], recv_sem=sems.at[3],
        device_id=(group, lower), device_id_type=MESH,
    )
    return up, down


def greet():
    me, count = lax.axis_index("space"), lax.axis_size("space")
    group = lax.axis_index("dp")
    barrier = pltpu.get_barrier_semaphore()
    for other in (lax.rem(me + 1, count), lax.rem(me + count - 1, count)):
        pl.semaphore_signal(barrier, inc=1, device_id=(group, other), device_id_type=MESH)
    return barrier


def face_kernel(
    pos_ref, spec_ref, target_ref, order_ref, *refs,
):
    count = 5
    more, refs = refs[:count], refs[count:]
    lower_ref, upper_ref, pos_out, spec_out, target_out, order_out = refs[:6]
    more_out, refs = refs[6 : 6 + count], refs[6 + count :]
    to_lower, to_upper, from_lower, from_upper, sems, load_sems = refs
    barrier = greet()
    sources = (pos_ref, spec_ref, target_ref, order_ref) + more
    targets = (pos_out, spec_out, target_out, order_out) + more_out
    loads = [pltpu.make_async_copy(s, t, load_sems.at[i]) for i, (s, t) in enumerate(zip(sources, targets))]
    for load in loads:
        load.start()
    for load in loads[:4]:
        load.wait()
    atoms = pos_out.shape[2]
    rows = [pos_out[i] for i in range(3)] + [spec_out[...].astype(F32)] + [target_out[i] for i in range(3)]
    pieces = stacked(pad_rows(rows, atoms))
    to_lower[...] = unstacked(mxu(pieces, selection(order_out, 0, atoms)))
    to_upper[...] = unstacked(mxu(pieces, selection(order_out, 1, atoms)))
    pl.semaphore_wait(barrier, 2)
    up, down = swap(to_lower, to_upper, from_lower, from_upper, sems)
    up.start()
    down.start()
    for load in loads[4:]:
        load.wait()
    up.wait()
    down.wait()
    lower_ref[...] = from_lower[...]
    upper_ref[...] = from_upper[...]


def ghost_kernel(to_lower, to_upper, lower_ref, upper_ref, from_lower, from_upper, sems):
    barrier = greet()
    pl.semaphore_wait(barrier, 2)
    up, down = swap(to_lower, to_upper, from_lower, from_upper, sems)
    up.start()
    down.start()
    up.wait()
    down.wait()
    lower_ref[...] = from_lower[...]
    upper_ref[...] = from_upper[...]


def sum_kernel(x_ref, out_ref, near, part, far, near_send, near_recv, far_send, far_recv):
    group, me = lax.axis_index("dp"), lax.axis_index("space")
    groups, count = lax.axis_size("dp"), lax.axis_size("space")
    barrier = pltpu.get_barrier_semaphore()
    others = [(lax.rem(group + k, groups), me) for k in range(1, groups)]
    others += [(group, lax.rem(me + k, count)) for k in range(1, count)]
    for other in others:
        pl.semaphore_signal(barrier, inc=1, device_id=other, device_id_type=MESH)
    pl.semaphore_wait(barrier, len(others))

    def share(source, slots, send, recv, spot, peers):
        copies = []
        for k, other in enumerate(peers):
            copies.append(
                pltpu.make_async_remote_copy(
                    src_ref=source, dst_ref=slots.at[spot], send_sem=send.at[k], recv_sem=recv.at[k],
                    device_id=other, device_id_type=MESH,
                )
            )
            copies[-1].start()
        slots[spot] = source[...]
        for copy in copies:
            copy.wait()
        total = slots[0]
        for k in range(1, len(peers) + 1):
            total = total + slots[k]
        return total

    part[...] = share(x_ref, near, near_send, near_recv, group, others[: groups - 1])
    out_ref[...] = share(part, far, far_send, far_recv, me, others[groups - 1 :])


def final_kernel(nb, ns, atoms, domains, sum_ref, loss_ref, rad_ref, center_ref, other_ref, out_ref):
    last = nb + 2 * ns
    weight_total = sum_ref[last + 1 : last + 2, 1:2] / domains
    scale = 1.0 / (3.0 * atoms * domains * weight_total)
    loss_ref[...] = sum_ref[last + 1 : last + 2, 0:1] * scale
    rad_ref[...] = sum_ref[:nb] * scale
    center_ref[...] = sum_ref[nb : nb + ns] * scale
    other_ref[...] = sum_ref[nb + ns : last] * scale
    out_ref[...] = sum_ref[last : last + 1] * scale


def pool_force(tile_list, positions, species, order, lower, upper, params, width):
    atoms = positions.shape[2]
    half = atoms // 2
    _, slots, own = tile_list.shape
    tile = atoms // own
    tiles = 2 * own
    rad, center = params[0], params[1]
    nb, hid = rad.shape
    ns = center.shape[0]
    most = own * (-(-slots * tile * tile // width))
    wide_b = slots * tile
    held = (
        pltpu.VMEM((2 * tile + wide_b, width), BF16),
        pltpu.VMEM((-(-(6 * nb + 6 * ns) // 16) * 16 + 6 * nb, width), BF16),
        pltpu.VMEM((nb, width), F32),
        pltpu.VMEM((8, width), F32),
        pltpu.VMEM((8, width), F32),
        pltpu.VMEM((hid, width), F32),
        pltpu.VMEM((hid, width), F32),
        pltpu.VMEM((8, width), F32),
        pltpu.VMEM((24, width), BF16),
    )
    return pl.pallas_call(
        functools.partial(force_kernel, nb, ns, width),
        out_shape=(
            jax.ShapeDtypeStruct((8, atoms), F32),
            jax.ShapeDtypeStruct((8, half), F32),
            jax.ShapeDtypeStruct((8, half), F32),
            jax.ShapeDtypeStruct((most + 8, 8, width), F32),
            jax.ShapeDtypeStruct((own,), I32),
        ),
        in_specs=[SMEM_SPEC] + [VMEM_SPEC] * 9,
        out_specs=(VMEM_SPEC,) * 4 + (SMEM_SPEC,),
        scratch_shapes=[
            pltpu.VMEM((tiles, 8, tile), F32),
            pltpu.VMEM((tiles, tile, 8), F32),
            pltpu.VMEM((tiles, 8, tile), F32),
            pltpu.VMEM((own, wide_b + 16, 2 * tile + wide_b), BF16),
            pltpu.VMEM((own, 2 * tile, LANES), F32),
            pltpu.VMEM((own, 48, 2 * tile + wide_b), BF16),
            (held,) * 4,
            pltpu.VMEM((hid, LANES), F32),
            pltpu.VMEM((own, 8, tile + wide_b), F32),
        ],
        compiler_params=pltpu.CompilerParams(vmem_limit_bytes=32 * MIB),
        name="pool_force",
    )(tile_list, positions, species, order, lower, upper, *params)


def pool_params(counts, tile_list, weights, order, targets, ghosts, sums, pairs, params, width):
    _, slots, own = tile_list.shape
    atoms = targets.shape[2]
    tile = atoms // own
    rad, center = params[0], params[1]
    nb, hid = rad.shape
    ns = center.shape[0]
    mid = nb + 2 * ns
    rows = mid + 2
    held = (
        pltpu.VMEM((hid, width), F32),
        pltpu.VMEM((8, width), F32),
        pltpu.VMEM((2 * (mid + nb), width), BF16),
        pltpu.VMEM((2 * nb * mid, width), BF16),
        pltpu.VMEM((2 * mid + 16, width), BF16),
    ) + (pltpu.VMEM((2 * hid, width), BF16),) * 2
    return pl.pallas_call(
        functools.partial(param_kernel, nb, ns, width),
        out_shape=(
            jax.ShapeDtypeStruct(targets.shape, F32),
            jax.ShapeDtypeStruct((rows, hid), F32),
        ),
        in_specs=[SMEM_SPEC] * 3 + [VMEM_SPEC] * 14,
        out_specs=(VMEM_SPEC,) * 2,
        scratch_shapes=[
            pltpu.VMEM((2 * own, 8, tile), F32),
            pltpu.VMEM((own, 8, LANES), F32),
            pltpu.VMEM((own, 8, LANES), F32),
            (held,) * 4,
            pltpu.VMEM((2 * (mid + nb), hid), F32),
            pltpu.VMEM((2 * nb * mid, hid), F32),
            pltpu.VMEM((hid, LANES), F32),
            pltpu.VMEM((2 * mid + 16, 2 * (mid + nb)), F32),
        ],
        compiler_params=pltpu.CompilerParams(vmem_limit_bytes=32 * MIB),
        name="pool_params",
    )(counts, tile_list, weights, order, targets, *ghosts, *sums, pairs, *params)


def face_exchange(positions, species, targets, order, *others):
    half = order.shape[2]
    box = jax.ShapeDtypeStruct((8, half), F32)
    arrays = (positions, species, targets, order) + others
    held = tuple(jax.ShapeDtypeStruct(x.shape, x.dtype) for x in arrays)
    return pl.pallas_call(
        face_kernel,
        out_shape=(box, box) + held,
        in_specs=[pl.BlockSpec(memory_space=pltpu.HBM)] * len(arrays),
        out_specs=(VMEM_SPEC,) * (2 + len(arrays)),
        scratch_shapes=[pltpu.VMEM((8, half), F32)] * 4
        + [pltpu.SemaphoreType.DMA((4,)), pltpu.SemaphoreType.DMA((len(arrays),))],
        compiler_params=pltpu.CompilerParams(collective_id=0, has_side_effects=True, vmem_limit_bytes=8 * MIB),
        name="face_exchange",
    )(*[pltpu.with_memory_space_constraint(x, pltpu.HBM) for x in arrays])


def ghost_exchange(to_lower, to_upper):
    box = jax.ShapeDtypeStruct(to_lower.shape, F32)
    return pl.pallas_call(
        ghost_kernel,
        out_shape=(box, box),
        in_specs=[VMEM_SPEC] * 2,
        out_specs=(VMEM_SPEC,) * 2,
        scratch_shapes=[pltpu.VMEM(to_lower.shape, F32)] * 2 + [pltpu.SemaphoreType.DMA((4,))],
        compiler_params=pltpu.CompilerParams(collective_id=1, has_side_effects=True, vmem_limit_bytes=4 * MIB),
        name="ghost_exchange",
    )(to_lower, to_upper)


def sum_everywhere(x):
    groups, count = lax.axis_size("dp"), lax.axis_size("space")
    return pl.pallas_call(
        sum_kernel,
        out_shape=jax.ShapeDtypeStruct(x.shape, F32),
        in_specs=[VMEM_SPEC],
        out_specs=VMEM_SPEC,
        scratch_shapes=[
            pltpu.VMEM((groups,) + x.shape, F32),
            pltpu.VMEM(x.shape, F32),
            pltpu.VMEM((count,) + x.shape, F32),
            pltpu.SemaphoreType.DMA((groups - 1,)),
            pltpu.SemaphoreType.DMA((groups - 1,)),
            pltpu.SemaphoreType.DMA((count - 1,)),
            pltpu.SemaphoreType.DMA((count - 1,)),
        ],
        compiler_params=pltpu.CompilerParams(
            collective_id=2, has_side_effects=True, vmem_limit_bytes=8 * MIB
        ),
        name="sum_everywhere",
    )(x)


def finish(summed, nb, ns, atoms):
    hid = summed.shape[1]
    domains = lax.axis_size("space")
    shapes = ((1, 1), (nb, hid), (ns, hid), (ns, hid), (1, hid))
    return pl.pallas_call(
        functools.partial(final_kernel, nb, ns, float(atoms), float(domains)),
        out_shape=tuple(jax.ShapeDtypeStruct(s, F32) for s in shapes),
        in_specs=[VMEM_SPEC],
        out_specs=(VMEM_SPEC,) * len(shapes),
        compiler_params=pltpu.CompilerParams(vmem_limit_bytes=4 * MIB),
        name="finish",
    )(summed)


def body(positions, species, ref_forces, send_lists, tile_lists, weights, w_rad, emb_center, emb_other, w_out):
    nb = w_rad.shape[0]
    ns = emb_center.shape[0]
    positions, ref_forces = positions.transpose(1, 0, 2), ref_forces.transpose(1, 0, 2)
    tile_lists = tile_lists.transpose(0, 2, 1)
    lower, upper, positions, species, ref_forces, send_lists, tile_lists, *params = face_exchange(
        positions, species, ref_forces, send_lists, tile_lists, w_rad, emb_center, emb_other, w_out[None]
    )
    own_grad, to_lower, to_upper, pairs, counts = pool_force(
        tile_lists, positions, species, send_lists, lower, upper, params, 4 * LANES
    )
    from_lower, from_upper = ghost_exchange(to_lower, to_upper)
    forces, grads = pool_params(
        counts, tile_lists, weights, send_lists, ref_forces, (lower, upper),
        (own_grad, to_lower, to_upper, from_lower, from_upper), pairs, params, 2 * LANES,
    )
    summed = sum_everywhere(grads)
    loss, grad_rad, grad_center, grad_other, grad_out = finish(summed, nb, ns, positions.shape[2])
    forces = forces.transpose(1, 0, 2)
    return forces, loss[0, 0], grad_rad, grad_center, grad_other, grad_out[0]


def solution(mesh):
    return jax.shard_map(
        body,
        mesh=mesh,
        in_specs=(
            P("dp", None, "space"),
            P("dp", "space"),
            P("dp", None, "space"),
            P("dp", "space", None),
            P("dp", "space", None),
            P("dp"),
            P(),
            P(),
            P(),
            P(),
        ),
        out_specs=(P("dp", None, "space"), P(), P(), P(), P(), P()),
        check_vma=False,
    )
```

```python
import functools

import jax
import jax.numpy as jnp
from jax import lax
from jax.experimental import pallas as pl
from jax.experimental.pallas import tpu as pltpu
from jax.sharding import PartitionSpec as P

CUTOFF = 1.0
DOMAIN_WIDTH = 2.0
F32 = jnp.float32
BF16 = jnp.bfloat16
I32 = jnp.int32
LAST = (((1,), (1,)), ((), ()))
LANES = 128
HIGHEST = lax.Precision.HIGHEST


def split(x, parts):
    pieces = []
    for _ in range(parts - 1):
        high = x.astype(BF16).astype(F32)
        pieces.append(high)
        x = x - high
    pieces.append(x.astype(BF16).astype(F32))
    return pieces


def left_operand(x, exact):
    w1, w2, w3 = split(x, 3)
    return jnp.concatenate([w1, w1, w2, w1, w2, w3] + exact, axis=1).astype(BF16)


def right_operand(x, exact):
    b1, b2, b3 = split(x, 3)
    return jnp.concatenate([b1, b2, b1, b3, b2, b1] + exact, axis=0).astype(BF16)


def mxu(a, b):
    return jnp.dot(a, b, preferred_element_type=F32)


def mxu_t(a, b):
    return lax.dot_general(a, b, LAST, preferred_element_type=F32)


def radial_terms(offsets, nb):
    q = jnp.sum(offsets * offsets, axis=0, keepdims=True) / (CUTOFF * CUTOFF)
    scale = float(nb - 1)
    centers = lax.broadcasted_iota(I32, (nb, 1), 0).astype(F32) / scale
    arg = (q - centers) * scale
    basis = jnp.exp(-(arg * arg))
    slope = (-2.0 * scale) * arg * basis
    inner = jnp.maximum(1.0 - q, 0.0)
    return basis, slope, inner * inner, -2.0 * inner


def tables(rad_ref, center_ref, other_ref, out_ref):
    stack = jnp.concatenate([rad_ref[...], center_ref[...], other_ref[...]], axis=0)
    w_row = out_ref[...]
    both = jnp.concatenate([stack, jnp.broadcast_to(w_row, (8, w_row.shape[1]))], axis=0).T
    count = stack.shape[0]
    return stack, w_row, both[:, :count], both[:, count : count + 1]


def one_hot_rows(code_a, code_b, ns, width):
    row = lax.broadcasted_iota(I32, (2 * ns, width), 0).astype(F32)
    code = jnp.where(row < ns, code_a, code_b + float(ns))
    return jnp.where(code == row, 1.0, 0.0)


def prepare(t, slots, own, list_ref, rows_ref, cols_ref, e_ref, bound_ref, feat_ref, ns):
    tile = rows_ref.shape[2]
    wide = slots * tile
    entries = [list_ref[0, k, t] for k in range(slots)]
    safe = [jnp.maximum(c, 0) for c in entries]
    xa = rows_ref[own]
    xb = jnp.concatenate([cols_ref[c] for c in safe], axis=0)
    q = jnp.zeros((wide, tile), F32)
    for i in range(3):
        diff = xb[:, i : i + 1] - xa[i : i + 1, :]
        q = q + diff * diff
    b_row = lax.broadcasted_iota(I32, (tile, tile), 0)
    a_lane = lax.broadcasted_iota(I32, (tile, tile), 1)
    allowed = []
    for c in entries:
        limit = jnp.where(c >= 0, 1.0, 0.0)
        allowed.append(jnp.where((b_row == a_lane) & (c == own), 0.0, limit))
    near = jnp.where(q / (CUTOFF * CUTOFF) < 1.0, jnp.concatenate(allowed, axis=0), 0.0)
    near_b = near.astype(BF16)
    r = lax.broadcasted_iota(I32, (wide, wide), 0)
    c = lax.broadcasted_iota(I32, (wide, wide), 1)
    lower = jnp.where(c < r, 1.0, 0.0).astype(BF16)
    rank = jnp.where(near > 0.0, mxu(lower, near_b) + 1.0, 0.0)
    row2 = lax.broadcasted_iota(I32, (2 * tile, tile), 0)
    col2 = lax.broadcasted_iota(I32, (2 * tile, tile), 1)
    reach = jnp.where(row2 < tile, row2 - 1, row2 - tile)
    below = jnp.where(col2 <= reach, 1.0, 0.0).astype(BF16)
    edges = jnp.sum(mxu_t(below, near_b), axis=1, keepdims=True)
    bound_ref[t] = jnp.broadcast_to(edges, (2 * tile, LANES))
    per_atom = jnp.sum(near, axis=0, keepdims=True)
    before = jnp.where(b_row < a_lane, 1.0, 0.0).astype(BF16)
    start = mxu(jnp.broadcast_to(per_atom, (16, tile)).astype(BF16), before)
    high = jnp.floor(start * (1.0 / 128.0))
    rest = start - 128.0 * high
    which = lax.broadcasted_iota(I32, (16, tile), 0)
    codes = jnp.where(which == 0, high, jnp.where(which == 1, rest, 0.0))
    found = jnp.concatenate([rank, codes], axis=0)
    e_ref[t] = jnp.concatenate([jnp.zeros((wide + 16, tile + wide), F32), found], axis=1).astype(BF16)
    row = lax.broadcasted_iota(I32, (8, tile), 0)
    lane = lax.broadcasted_iota(I32, (8, tile), 1).astype(F32)
    kind_row = row.astype(F32)
    kind = xa[3:4, :]
    first = jnp.where(row < 3, xa, jnp.where(row == 4, lane, jnp.where(row == 6, kind, 0.0)))
    first_kind = jnp.where((row < ns) & (kind == kind_row), 1.0, 0.0)
    parts = [jnp.concatenate([first, first_kind], axis=0)]
    for k in range(slots):
        other = rows_ref[safe[k]]
        kind = other[3:4, :]
        second = jnp.where(
            row < 3, -other, jnp.where(row == 5, lane + float(k * tile), jnp.where(row == 7, kind, 0.0))
        )
        second_kind = jnp.where((row >= ns) & (kind + float(ns) == kind_row), 1.0, 0.0)
        parts.append(jnp.concatenate([second, second_kind], axis=0))
    parts.append(jnp.zeros((16, tile), F32))
    feat_ref[t] = jnp.concatenate(split(jnp.concatenate(parts, axis=1), 3), axis=0).astype(BF16)
    return per_atom


def pieces_of(count_ref, width):
    return [(count_ref[t] + (width - 1)) // width for t in range(count_ref.shape[0])]


def locate(step, pieces, others):
    t, begin, place, end = jnp.int32(0), jnp.int32(0), jnp.int32(0), jnp.int32(0)
    for count, other in zip(pieces[:-1], others[:-1]):
        end = end + count
        past = step >= end
        t = t + jnp.where(past, 1, 0)
        begin = begin + jnp.where(past, count, 0)
        place = place + jnp.where(past, other, 0)
    return t, step - begin, place


def selection(order_ref, k, atoms):
    count = order_ref.shape[2]
    row = lax.broadcasted_iota(I32, (atoms, count), 0)
    return jnp.where(row == order_ref[0, k : k + 1, :], 1.0, 0.0).astype(BF16)


def stacked(x):
    return jnp.concatenate(split(x, 3), axis=0).astype(BF16)


def unstacked(x):
    rows = x.shape[0] // 3
    return x[:rows] + (x[rows : 2 * rows] + x[2 * rows :])


def pad_rows(parts, width):
    count = sum(p.shape[0] for p in parts)
    return jnp.concatenate(parts + [jnp.zeros((8 - count, width), F32)], axis=0)


def fill_pool(pos_ref, spec_ref, lower_ref, upper_ref, rows_ref, cols_ref):
    tiles, _, tile = rows_ref.shape
    half = lower_ref.shape[1]
    atoms = pos_ref.shape[2]
    own = pad_rows([pos_ref[i] for i in range(3)] + [spec_ref[...].astype(F32)], atoms)
    row = lax.broadcasted_iota(I32, (8, half), 0)
    shift = jnp.where(row == 0, DOMAIN_WIDTH, 0.0)
    left = jnp.where(row < 4, lower_ref[...] - shift, 0.0)
    right = jnp.where(row < 4, upper_ref[...] + shift, 0.0)
    pool = jnp.concatenate([left, own, right], axis=1)
    turned = pool.T
    for i in range(tiles):
        rows_ref[i] = pool[:, i * tile : (i + 1) * tile]
        cols_ref[i] = turned[i * tile : (i + 1) * tile, :]


def force_kernel(
    nb, ns, width, list_ref, pos_ref, spec_ref, order_ref, lower_ref, upper_ref,
    rad_ref, center_ref, other_ref, out_ref,
    own_ref, to_lower_ref, to_upper_ref, pair_ref, count_ref,
    rows_ref, cols_ref, grad_ref, e_ref, bound_ref, feat_ref, sets, wb_ref, acc_ref,
):
    _, slots, tiles_own = list_ref.shape
    tile = rows_ref.shape[2]
    fill_pool(pos_ref, spec_ref, lower_ref, upper_ref, rows_ref, cols_ref)
    wide_b = slots * tile
    half_tiles = tiles_own // 2
    hid = rad_ref.shape[1]
    near = [
        prepare(t, slots, t + half_tiles, list_ref, rows_ref, cols_ref, e_ref, bound_ref, feat_ref, ns)
        for t in range(tiles_own)
    ]
    for t in range(tiles_own):
        count_ref[t] = jnp.sum(near[t]).astype(I32)
    pieces = pieces_of(count_ref, width)
    total = sum(pieces)
    acc_ref[...] = jnp.zeros_like(acc_ref)
    stack, w_row, cols, w_col = tables(rad_ref, center_ref, other_ref, out_ref)
    half_cols = 0.5 * cols
    weighted = 0.5 * w_row * stack[:nb]
    linear = jnp.dot(
        jnp.concatenate([weighted, w_row, jnp.zeros((7, hid), F32)], axis=0), half_cols,
        precision=HIGHEST, preferred_element_type=F32,
    )
    base = jnp.sum(weighted, axis=1, keepdims=True)
    y_rows = jnp.concatenate([half_cols, linear], axis=0)
    a_y = left_operand(y_rows[:, :nb], split(y_rows[:, nb:], 3)).astype(F32)
    a_r = left_operand((0.5 * w_col) * cols[:, :nb], []).astype(F32)
    gap = -a_y.shape[1] % 16
    a_y = jnp.concatenate([a_y, jnp.zeros((a_y.shape[0], gap + a_r.shape[1]), F32)], axis=1)
    a_r = jnp.concatenate([jnp.zeros((hid, a_y.shape[1] - a_r.shape[1]), F32), a_r], axis=1)
    a_all = jnp.concatenate([a_y, a_r], axis=0).astype(BF16)
    wb_ref[...] = jnp.broadcast_to(w_col, wb_ref.shape)

    def of_step(step):
        t, local, _ = locate(jnp.minimum(step, total - 1), pieces, pieces)
        spot = (local * width + lax.broadcasted_iota(I32, (1, width), 1)).astype(F32)
        return t, spot, spot < jnp.where(step < total, count_ref[t], 0).astype(F32)

    def first_of(step):
        t, spot, _ = of_step(step)
        bounds = bound_ref[t]
        firsts = []
        for lane in range(0, width, LANES):
            here = spot[:, lane : lane + LANES]
            inside = (here >= bounds[:tile]) & (here < bounds[tile:])
            firsts.append(jnp.where(inside, 1.0, 0.0))
        return jnp.concatenate(firsts, axis=1).astype(BF16)

    def second_of(step, found):
        _, spot, valid = of_step(step)
        begin = 128.0 * found[wide_b : wide_b + 1] + found[wide_b + 1 : wide_b + 2]
        rank = jnp.where(valid, spot - begin + 1.0, -1.0)
        return jnp.where(found[:wide_b] == rank, 1.0, 0.0).astype(BF16)

    def describe(step, held, after):
        rep_ref, x_ref, slope_ref, record_ref, side_ref = held[:5]
        t, _, valid = of_step(step)
        first = first_of(step + 1)
        rep_ref[tile + wide_b :] = first
        after[0][:tile] = first
        left = jnp.concatenate([feat_ref[t], e_ref[of_step(step + 1)[0]]], axis=0)
        both = mxu(left, rep_ref[...])
        after[0][tile : tile + wide_b] = second_of(step + 1, both[48:])
        wide = unstacked(both[:48])
        keep = jnp.where(valid, 1.0, 0.0)
        row = lax.broadcasted_iota(I32, (8, width), 0)
        record = jnp.where(row == 3, keep, wide[:8])
        pair_ref[step] = record
        record_ref[...] = record
        kinds = wide[8:16]
        basis, slope, env, denv = radial_terms(wide[0:3], nb)
        b1, b2, b3 = split(basis, 3)
        s1, s2, s3 = split(slope, 3)
        blank = [jnp.zeros((gap, width), F32)] if gap else []
        x = [b1, b2, b1, b3, b2, b1, kinds, kinds, kinds] + blank + [s1, s2, s1, s3, s2, s1]
        x_ref[...] = jnp.concatenate(x, axis=0).astype(BF16)
        slope_ref[...] = slope
        side_ref[...] = pad_rows([keep * denv, keep * env], width)

    def latent(held):
        x_ref, slope_ref = held[1:3]
        y_ref, r_ref, line_ref = held[5:8]
        y = mxu(a_all, x_ref[...])
        y_ref[...] = y[:hid]
        r_ref[...] = y[hid + 16 :]
        lin = jnp.sum(slope_ref[...] * (base + y[hid : hid + 8]), axis=0, keepdims=True)
        line_ref[...] = pad_rows([y[hid + 8 : hid + 9], lin], width)

    def channels(held):
        record_ref, side_ref, y_ref, r_ref, line_ref, gd_ref = held[3:]
        s_rows, t_rows = [], []
        for lane in range(0, width, LANES):
            s = jnp.zeros((8, LANES), F32)
            u = jnp.zeros((8, LANES), F32)
            for h in range(0, hid, 8):
                y = y_ref[h : h + 8, lane : lane + LANES]
                r = r_ref[h : h + 8, lane : lane + LANES]
                th = jnp.tanh(y)
                a = y * th
                g = th * (1.0 - a)
                s = s + wb_ref[h : h + 8, :] * a
                u = u + r * g
            s_rows.append(jnp.sum(s, axis=0, keepdims=True))
            t_rows.append(jnp.sum(u, axis=0, keepdims=True))
        s_all = jnp.concatenate(s_rows, axis=1) + line_ref[0:1]
        t_all = jnp.concatenate(t_rows, axis=1) + line_ref[1:2]
        g = side_ref[0:1] * s_all + side_ref[1:2] * t_all
        gd_ref[...] = stacked((2.0 * g) * record_ref[...])

    def gather(step, held):
        t, _, _ = locate(jnp.clip(step, 0, total - 1), pieces, pieces)
        acc_ref[t] = acc_ref[t] + unstacked(mxu_t(held[-1][...], held[0][: tile + wide_b]))

    def rounds(i, carry):
        for m in range(4):
            step = 4 * i + m
            gather(step - 1, sets[(m + 3) % 4])
            describe(step + 2, sets[(m + 2) % 4], sets[(m + 3) % 4])
            latent(sets[(m + 1) % 4])
            channels(sets[m])
        return carry

    for ref in (sets[3][0], sets[3][-1]):
        ref[...] = jnp.zeros_like(ref)
    first = first_of(jnp.int32(0))
    sets[0][0][:tile] = first
    found = mxu(e_ref[of_step(jnp.int32(0))[0], :, tile + wide_b :], first)
    sets[0][0][tile : tile + wide_b] = second_of(jnp.int32(0), found)
    for step in range(2):
        describe(jnp.int32(step), sets[step], sets[step + 1])
    latent(sets[0])
    rotations = (total + 3) // 4
    lax.fori_loop(0, rotations, rounds, 0)
    gather(4 * rotations - 1, sets[3])
    grad_ref[...] = jnp.zeros_like(grad_ref)
    for t in range(tiles_own):
        own = t + half_tiles
        grad_ref[own] = grad_ref[own] + acc_ref[t, :, :tile]
        for k in range(slots):
            entry = jnp.maximum(list_ref[0, k, t], 0)
            grad_ref[entry] = grad_ref[entry] - acc_ref[t, :, (k + 1) * tile : (k + 2) * tile]
    whole = jnp.concatenate([grad_ref[i] for i in range(grad_ref.shape[0])], axis=1)
    atoms = pos_ref.shape[2]
    half = atoms // 2
    own_grad = whole[:, half : half + atoms]
    own_ref[...] = own_grad
    pieces = stacked(own_grad)
    for k, ref in ((0, to_lower_ref), (1, to_upper_ref)):
        sent = unstacked(mxu(pieces, selection(order_ref, k, atoms)))
        ghost = whole[:, :half] if k == 0 else whole[:, half + atoms :]
        ref[...] = pad_rows([sent[0:3], ghost[0:3]], half)


def finish_forces(
    weight, order_ref, target_ref, lower_ref, upper_ref, own_ref,
    to_lower_ref, to_upper_ref, from_lower_ref, from_upper_ref, forces_ref, v_ref,
):
    tiles, _, tile = v_ref.shape
    atoms = own_ref.shape[1]
    total = own_ref[0:3, :]
    for k, ref in ((0, from_lower_ref), (1, from_upper_ref)):
        total = total + unstacked(mxu_t(stacked(ref[...]), selection(order_ref, k, atoms)))[3:6]
    for i in range(3):
        forces_ref[i] = -total[i : i + 1]
    miss = total + jnp.concatenate([target_ref[i] for i in range(3)], axis=0)
    left = to_lower_ref[3:6, :] + from_lower_ref[0:3, :] + lower_ref[4:7, :]
    right = to_upper_ref[3:6, :] + from_upper_ref[0:3, :] + upper_ref[4:7, :]
    scaled = (2.0 * weight) * jnp.concatenate([left, miss, right], axis=1)
    scaled = pad_rows([scaled], scaled.shape[1])
    for i in range(tiles):
        v_ref[i] = scaled[:, i * tile : (i + 1) * tile]
    return weight * jnp.sum(miss * miss)


def param_kernel(
    nb, ns, width, count_ref, list_ref, weight_ref, order_ref, target_ref, lower_ref, upper_ref, own_ref,
    to_lower_ref, to_upper_ref, from_lower_ref, from_upper_ref, pair_ref, rad_ref, center_ref, other_ref, out_ref,
    forces_ref, grads_ref,
    v_ref, va_ref, vb_ref, sets, acc_g, acc_f, acc_s, gram_ref,
):
    _, slots, tiles_own = list_ref.shape
    tile = v_ref.shape[2]
    half_tiles = tiles_own // 2
    hid = rad_ref.shape[1]
    outer = pair_ref.shape[2]
    weight = weight_ref[0].astype(F32)
    loss = finish_forces(
        weight, order_ref, target_ref, lower_ref, upper_ref, own_ref,
        to_lower_ref, to_upper_ref, from_lower_ref, from_upper_ref, forces_ref, v_ref,
    )
    mid = nb + 2 * ns
    acc_g[...] = jnp.zeros_like(acc_g)
    acc_f[...] = jnp.zeros_like(acc_f)
    acc_s[...] = jnp.zeros_like(acc_s)
    gram_ref[...] = jnp.zeros_like(gram_ref)
    for t in range(tiles_own):
        va_ref[t] = jnp.concatenate([v_ref[t + half_tiles], jnp.zeros((8, LANES - tile), F32)], axis=1)
        vb_ref[t] = jnp.concatenate([v_ref[jnp.maximum(list_ref[0, k, t], 0)] for k in range(slots)], axis=1)
    stack, w_row, cols, w_col = tables(rad_ref, center_ref, other_ref, out_ref)
    half_cols = 0.5 * cols
    a_y = left_operand(half_cols[:, :nb], split(half_cols[:, nb:], 3))

    pieces, chunks = pieces_of(count_ref, width), pieces_of(count_ref, outer)
    total = sum(pieces)
    share = outer // width

    def front(step, held):
        y_ref, alpha_ref, g_cols, f_cols, x_rows = held[:5]
        t, local, place = locate(jnp.minimum(step, total - 1), pieces, chunks)
        lane = pl.multiple_of(local % share * width, width)
        record = pair_ref[place + local // share, :, pl.ds(lane, width)]
        offsets = record[0:3]
        keep = record[3:4] * jnp.where(step < total, 1.0, 0.0)
        index_a = jnp.broadcast_to(record[4:5].astype(I32), (8, width))
        index_b = jnp.broadcast_to(record[5:6].astype(I32), (8, width))
        va, vb = va_ref[t], vb_ref[t]
        diffs = []
        for lane in range(0, width, LANES):
            part_a = jnp.take_along_axis(va, index_a[:, lane : lane + LANES], axis=1, mode="promise_in_bounds")
            part_b = jnp.take_along_axis(vb, index_b[:, lane : lane + LANES], axis=1, mode="promise_in_bounds")
            diffs.append(part_a - part_b)
        dv = jnp.concatenate(diffs, axis=1)
        kinds = one_hot_rows(record[6:7], record[7:8], ns, width)
        basis, slope, env, denv = radial_terms(offsets, nb)
        c = (2.0 * keep) * jnp.sum(offsets * dv[0:3], axis=0, keepdims=True)
        alpha = c * denv
        beta_slope = (c * env) * slope
        y_ref[...] = mxu(a_y, right_operand(basis, [kinds, kinds, kinds]))
        alpha_ref[...] = jnp.broadcast_to(alpha, (8, width))
        x = jnp.concatenate([basis, kinds], axis=0)
        one = jnp.ones((8, width), F32)
        g_cols[...] = jnp.concatenate(
            split(jnp.concatenate([alpha * x, beta_slope], axis=0), 2), axis=0
        ).astype(BF16)
        f_cols[...] = jnp.concatenate(
            split(jnp.concatenate([beta_slope[j : j + 1] * x for j in range(nb)], axis=0), 2), axis=0
        ).astype(BF16)
        x_rows[...] = jnp.concatenate(split(x, 2) + [one, one], axis=0).astype(BF16)

    def middle(held, top, bottom):
        y_ref, alpha_ref, _, _, _, g_ref, f_ref = held
        for h in range(top, bottom, 16):
            s = acc_s[h : h + 16, :]
            for lane in range(0, width, LANES):
                alpha = alpha_ref[:, lane : lane + LANES]
                y = y_ref[h : h + 16, lane : lane + LANES]
                th = jnp.tanh(y)
                a = y * th
                u = 1.0 - a
                g = th * u
                f = u - th * g
                s = s + jnp.concatenate([alpha, alpha], axis=0) * a
                for ref, x in ((g_ref, g), (f_ref, f)):
                    high = x.astype(BF16)
                    ref[h : h + 16, lane : lane + LANES] = high
                    ref[hid + h : hid + h + 16, lane : lane + LANES] = (x - high.astype(F32)).astype(BF16)
            acc_s[h : h + 16, :] = s

    def rear(held, part):
        g_cols, f_cols, x_rows, g_ref, f_ref = held[2:]
        if part == 0:
            acc_f[...] += mxu_t(f_cols[...], f_ref[:hid])
        elif part == 1:
            acc_f[: nb * mid] += mxu_t(f_cols[: nb * mid], f_ref[hid:])
        elif part == 2:
            acc_g[...] += mxu_t(g_cols[...], g_ref[:hid])
        else:
            acc_g[: mid + nb] += mxu_t(g_cols[: mid + nb], g_ref[hid:])
            gram_ref[...] += mxu_t(g_cols[...], x_rows[...])

    def rounds(i, carry):
        for m in range(4):
            for part in range(4):
                rear(sets[(m + 3) % 4], part)
                middle(sets[m], part * hid // 4, (part + 1) * hid // 4)
            front(4 * i + m + 1, sets[(m + 1) % 4])
        return carry

    for ref in sets[3][2:]:
        ref[...] = jnp.zeros_like(ref)
    front(jnp.int32(0), sets[0])
    lax.fori_loop(0, (total + 3) // 4, rounds, 0)
    for part in range(4):
        rear(sets[3], part)
    cols_g = mid + nb
    gram = gram_ref[:cols_g] + gram_ref[cols_g:]
    gram_x = gram[:, :mid] + gram[:, mid : 2 * mid]
    gram_one = gram[:, 2 * mid : 2 * mid + 1]
    half_stack = 0.5 * stack
    spread = jnp.dot(gram_x, half_stack, precision=HIGHEST, preferred_element_type=F32)
    first = 0.5 * (gram_one + spread + (acc_g[:cols_g] + acc_g[cols_g:]))
    sharp = 0.5 * (acc_f[: nb * mid] + acc_f[nb * mid :])
    d = first[:mid]
    for j in range(nb):
        d = d + stack[j : j + 1] * sharp[j * mid : (j + 1) * mid]
    slope_part = first[mid:]
    grad_out = (
        jnp.sum(acc_s[...].T, axis=0, keepdims=True)
        + jnp.sum(half_stack * gram_one[:mid], axis=0, keepdims=True)
        + jnp.sum(slope_part * stack[:nb], axis=0, keepdims=True)
    )
    lane = lax.broadcasted_iota(I32, (1, hid), 1)
    grads_ref[:nb] = w_row * (d[:nb] + slope_part)
    grads_ref[nb:mid] = w_row * d[nb:]
    grads_ref[mid : mid + 1] = grad_out
    grads_ref[mid + 1 :] = jnp.where(lane == 0, loss, jnp.where(lane == 1, weight, 0.0))


SMEM_SPEC = pl.BlockSpec(memory_space=pltpu.SMEM)
VMEM_SPEC = pl.BlockSpec(memory_space=pltpu.VMEM)
MESH = pl.DeviceIdType.MESH
MIB = 1024 * 1024


def swap(to_lower, to_upper, from_lower, from_upper, sems):
    me, count = lax.axis_index("space"), lax.axis_size("space")
    group = lax.axis_index("dp")
    upper, lower = lax.rem(me + 1, count), lax.rem(me + count - 1, count)
    up = pltpu.make_async_remote_copy(
        src_ref=to_upper, dst_ref=from_lower, send_sem=sems.at[0], recv_sem=sems.at[1],
        device_id=(group, upper), device_id_type=MESH,
    )
    down = pltpu.make_async_remote_copy(
        src_ref=to_lower, dst_ref=from_upper, send_sem=sems.at[2], recv_sem=sems.at[3],
        device_id=(group, lower), device_id_type=MESH,
    )
    return up, down


def greet():
    me, count = lax.axis_index("space"), lax.axis_size("space")
    group = lax.axis_index("dp")
    barrier = pltpu.get_barrier_semaphore()
    for other in (lax.rem(me + 1, count), lax.rem(me + count - 1, count)):
        pl.semaphore_signal(barrier, inc=1, device_id=(group, other), device_id_type=MESH)
    return barrier


def face_kernel(
    pos_ref, spec_ref, target_ref, order_ref, *refs,
):
    count = 5
    more, refs = refs[:count], refs[count:]
    lower_ref, upper_ref, pos_out, spec_out, target_out, order_out = refs[:6]
    more_out, refs = refs[6 : 6 + count], refs[6 + count :]
    to_lower, to_upper, from_lower, from_upper, sems, load_sems = refs
    barrier = greet()
    sources = (pos_ref, spec_ref, target_ref, order_ref) + more
    targets = (pos_out, spec_out, target_out, order_out) + more_out
    loads = [pltpu.make_async_copy(s, t, load_sems.at[i]) for i, (s, t) in enumerate(zip(sources, targets))]
    for load in loads:
        load.start()
    for load in loads[:4]:
        load.wait()
    atoms = pos_out.shape[2]
    rows = [pos_out[i] for i in range(3)] + [spec_out[...].astype(F32)] + [target_out[i] for i in range(3)]
    pieces = stacked(pad_rows(rows, atoms))
    to_lower[...] = unstacked(mxu(pieces, selection(order_out, 0, atoms)))
    to_upper[...] = unstacked(mxu(pieces, selection(order_out, 1, atoms)))
    pl.semaphore_wait(barrier, 2)
    up, down = swap(to_lower, to_upper, from_lower, from_upper, sems)
    up.start()
    down.start()
    for load in loads[4:]:
        load.wait()
    up.wait()
    down.wait()
    lower_ref[...] = from_lower[...]
    upper_ref[...] = from_upper[...]


def ghost_kernel(to_lower, to_upper, lower_ref, upper_ref, from_lower, from_upper, sems):
    barrier = greet()
    pl.semaphore_wait(barrier, 2)
    up, down = swap(to_lower, to_upper, from_lower, from_upper, sems)
    up.start()
    down.start()
    up.wait()
    down.wait()
    lower_ref[...] = from_lower[...]
    upper_ref[...] = from_upper[...]


def sum_kernel(x_ref, out_ref, near, part, far, near_send, near_recv, far_send, far_recv):
    group, me = lax.axis_index("dp"), lax.axis_index("space")
    groups, count = lax.axis_size("dp"), lax.axis_size("space")
    barrier = pltpu.get_barrier_semaphore()
    others = [(lax.rem(group + k, groups), me) for k in range(1, groups)]
    others += [(group, lax.rem(me + k, count)) for k in range(1, count)]
    for other in others:
        pl.semaphore_signal(barrier, inc=1, device_id=other, device_id_type=MESH)
    pl.semaphore_wait(barrier, len(others))

    def share(source, slots, send, recv, spot, peers):
        copies = []
        for k, other in enumerate(peers):
            copies.append(
                pltpu.make_async_remote_copy(
                    src_ref=source, dst_ref=slots.at[spot], send_sem=send.at[k], recv_sem=recv.at[k],
                    device_id=other, device_id_type=MESH,
                )
            )
            copies[-1].start()
        slots[spot] = source[...]
        for copy in copies:
            copy.wait()
        total = slots[0]
        for k in range(1, len(peers) + 1):
            total = total + slots[k]
        return total

    part[...] = share(x_ref, near, near_send, near_recv, group, others[: groups - 1])
    out_ref[...] = share(part, far, far_send, far_recv, me, others[groups - 1 :])


def final_kernel(nb, ns, atoms, domains, sum_ref, loss_ref, rad_ref, center_ref, other_ref, out_ref):
    last = nb + 2 * ns
    weight_total = sum_ref[last + 1 : last + 2, 1:2] / domains
    scale = 1.0 / (3.0 * atoms * domains * weight_total)
    loss_ref[...] = sum_ref[last + 1 : last + 2, 0:1] * scale
    rad_ref[...] = sum_ref[:nb] * scale
    center_ref[...] = sum_ref[nb : nb + ns] * scale
    other_ref[...] = sum_ref[nb + ns : last] * scale
    out_ref[...] = sum_ref[last : last + 1] * scale


def pool_force(tile_list, positions, species, order, lower, upper, params, width):
    atoms = positions.shape[2]
    half = atoms // 2
    _, slots, own = tile_list.shape
    tile = atoms // own
    tiles = 2 * own
    rad, center = params[0], params[1]
    nb, hid = rad.shape
    ns = center.shape[0]
    most = own * (-(-slots * tile * tile // width))
    wide_b = slots * tile
    held = (
        pltpu.VMEM((2 * tile + wide_b, width), BF16),
        pltpu.VMEM((-(-(6 * nb + 6 * ns) // 16) * 16 + 6 * nb, width), BF16),
        pltpu.VMEM((nb, width), F32),
        pltpu.VMEM((8, width), F32),
        pltpu.VMEM((8, width), F32),
        pltpu.VMEM((hid, width), F32),
        pltpu.VMEM((hid, width), F32),
        pltpu.VMEM((8, width), F32),
        pltpu.VMEM((24, width), BF16),
    )
    return pl.pallas_call(
        functools.partial(force_kernel, nb, ns, width),
        out_shape=(
            jax.ShapeDtypeStruct((8, atoms), F32),
            jax.ShapeDtypeStruct((8, half), F32),
            jax.ShapeDtypeStruct((8, half), F32),
            jax.ShapeDtypeStruct((most + 8, 8, width), F32),
            jax.ShapeDtypeStruct((own,), I32),
        ),
        in_specs=[SMEM_SPEC] + [VMEM_SPEC] * 9,
        out_specs=(VMEM_SPEC,) * 4 + (SMEM_SPEC,),
        scratch_shapes=[
            pltpu.VMEM((tiles, 8, tile), F32),
            pltpu.VMEM((tiles, tile, 8), F32),
            pltpu.VMEM((tiles, 8, tile), F32),
            pltpu.VMEM((own, wide_b + 16, 2 * tile + wide_b), BF16),
            pltpu.VMEM((own, 2 * tile, LANES), F32),
            pltpu.VMEM((own, 48, 2 * tile + wide_b), BF16),
            (held,) * 4,
            pltpu.VMEM((hid, LANES), F32),
            pltpu.VMEM((own, 8, tile + wide_b), F32),
        ],
        compiler_params=pltpu.CompilerParams(vmem_limit_bytes=32 * MIB),
        name="pool_force",
    )(tile_list, positions, species, order, lower, upper, *params)


def pool_params(counts, tile_list, weights, order, targets, ghosts, sums, pairs, params, width):
    _, slots, own = tile_list.shape
    atoms = targets.shape[2]
    tile = atoms // own
    rad, center = params[0], params[1]
    nb, hid = rad.shape
    ns = center.shape[0]
    mid = nb + 2 * ns
    rows = mid + 2
    held = (
        pltpu.VMEM((hid, width), F32),
        pltpu.VMEM((8, width), F32),
        pltpu.VMEM((2 * (mid + nb), width), BF16),
        pltpu.VMEM((2 * nb * mid, width), BF16),
        pltpu.VMEM((2 * mid + 16, width), BF16),
    ) + (pltpu.VMEM((2 * hid, width), BF16),) * 2
    return pl.pallas_call(
        functools.partial(param_kernel, nb, ns, width),
        out_shape=(
            jax.ShapeDtypeStruct(targets.shape, F32),
            jax.ShapeDtypeStruct((rows, hid), F32),
        ),
        in_specs=[SMEM_SPEC] * 3 + [VMEM_SPEC] * 14,
        out_specs=(VMEM_SPEC,) * 2,
        scratch_shapes=[
            pltpu.VMEM((2 * own, 8, tile), F32),
            pltpu.VMEM((own, 8, LANES), F32),
            pltpu.VMEM((own, 8, LANES), F32),
            (held,) * 4,
            pltpu.VMEM((2 * (mid + nb), hid), F32),
            pltpu.VMEM((2 * nb * mid, hid), F32),
            pltpu.VMEM((hid, LANES), F32),
            pltpu.VMEM((2 * (mid + nb), 2 * mid + 16), F32),
        ],
        compiler_params=pltpu.CompilerParams(vmem_limit_bytes=32 * MIB),
        name="pool_params",
    )(counts, tile_list, weights, order, targets, *ghosts, *sums, pairs, *params)


def face_exchange(positions, species, targets, order, *others):
    half = order.shape[2]
    box = jax.ShapeDtypeStruct((8, half), F32)
    arrays = (positions, species, targets, order) + others
    held = tuple(jax.ShapeDtypeStruct(x.shape, x.dtype) for x in arrays)
    return pl.pallas_call(
        face_kernel,
        out_shape=(box, box) + held,
        in_specs=[pl.BlockSpec(memory_space=pltpu.HBM)] * len(arrays),
        out_specs=(VMEM_SPEC,) * (2 + len(arrays)),
        scratch_shapes=[pltpu.VMEM((8, half), F32)] * 4
        + [pltpu.SemaphoreType.DMA((4,)), pltpu.SemaphoreType.DMA((len(arrays),))],
        compiler_params=pltpu.CompilerParams(collective_id=0, has_side_effects=True, vmem_limit_bytes=8 * MIB),
        name="face_exchange",
    )(*[pltpu.with_memory_space_constraint(x, pltpu.HBM) for x in arrays])


def ghost_exchange(to_lower, to_upper):
    box = jax.ShapeDtypeStruct(to_lower.shape, F32)
    return pl.pallas_call(
        ghost_kernel,
        out_shape=(box, box),
        in_specs=[VMEM_SPEC] * 2,
        out_specs=(VMEM_SPEC,) * 2,
        scratch_shapes=[pltpu.VMEM(to_lower.shape, F32)] * 2 + [pltpu.SemaphoreType.DMA((4,))],
        compiler_params=pltpu.CompilerParams(collective_id=1, has_side_effects=True, vmem_limit_bytes=4 * MIB),
        name="ghost_exchange",
    )(to_lower, to_upper)


def sum_everywhere(x):
    groups, count = lax.axis_size("dp"), lax.axis_size("space")
    return pl.pallas_call(
        sum_kernel,
        out_shape=jax.ShapeDtypeStruct(x.shape, F32),
        in_specs=[VMEM_SPEC],
        out_specs=VMEM_SPEC,
        scratch_shapes=[
            pltpu.VMEM((groups,) + x.shape, F32),
            pltpu.VMEM(x.shape, F32),
            pltpu.VMEM((count,) + x.shape, F32),
            pltpu.SemaphoreType.DMA((groups - 1,)),
            pltpu.SemaphoreType.DMA((groups - 1,)),
            pltpu.SemaphoreType.DMA((count - 1,)),
            pltpu.SemaphoreType.DMA((count - 1,)),
        ],
        compiler_params=pltpu.CompilerParams(
            collective_id=2, has_side_effects=True, vmem_limit_bytes=8 * MIB
        ),
        name="sum_everywhere",
    )(x)


def finish(summed, nb, ns, atoms):
    hid = summed.shape[1]
    domains = lax.axis_size("space")
    shapes = ((1, 1), (nb, hid), (ns, hid), (ns, hid), (1, hid))
    return pl.pallas_call(
        functools.partial(final_kernel, nb, ns, float(atoms), float(domains)),
        out_shape=tuple(jax.ShapeDtypeStruct(s, F32) for s in shapes),
        in_specs=[VMEM_SPEC],
        out_specs=(VMEM_SPEC,) * len(shapes),
        compiler_params=pltpu.CompilerParams(vmem_limit_bytes=4 * MIB),
        name="finish",
    )(summed)


def body(positions, species, ref_forces, send_lists, tile_lists, weights, w_rad, emb_center, emb_other, w_out):
    nb = w_rad.shape[0]
    ns = emb_center.shape[0]
    positions, ref_forces = positions.transpose(1, 0, 2), ref_forces.transpose(1, 0, 2)
    tile_lists = tile_lists.transpose(0, 2, 1)
    lower, upper, positions, species, ref_forces, send_lists, tile_lists, *params = face_exchange(
        positions, species, ref_forces, send_lists, tile_lists, w_rad, emb_center, emb_other, w_out[None]
    )
    own_grad, to_lower, to_upper, pairs, counts = pool_force(
        tile_lists, positions, species, send_lists, lower, upper, params, 4 * LANES
    )
    from_lower, from_upper = ghost_exchange(to_lower, to_upper)
    forces, grads = pool_params(
        counts, tile_lists, weights, send_lists, ref_forces, (lower, upper),
        (own_grad, to_lower, to_upper, from_lower, from_upper), pairs, params, 2 * LANES,
    )
    summed = sum_everywhere(grads)
    loss, grad_rad, grad_center, grad_other, grad_out = finish(summed, nb, ns, positions.shape[2])
    forces = forces.transpose(1, 0, 2)
    return forces, loss[0, 0], grad_rad, grad_center, grad_other, grad_out[0]


def solution(mesh):
    return jax.shard_map(
        body,
        mesh=mesh,
        in_specs=(
            P("dp", None, "space"),
            P("dp", "space"),
            P("dp", None, "space"),
            P("dp", "space", None),
            P("dp", "space", None),
            P("dp"),
            P(),
            P(),
            P(),
            P(),
        ),
        out_specs=(P("dp", None, "space"), P(), P(), P(), P(), P()),
        check_vma=False,
    )
```

```python
import functools

import jax
import jax.numpy as jnp
from jax import lax
from jax.experimental import pallas as pl
from jax.experimental.pallas import tpu as pltpu
from jax.sharding import PartitionSpec as P

CUTOFF = 1.0
DOMAIN_WIDTH = 2.0
F32 = jnp.float32
BF16 = jnp.bfloat16
I32 = jnp.int32
LAST = (((1,), (1,)), ((), ()))
LANES = 128
HIGHEST = lax.Precision.HIGHEST


def split(x, parts):
    pieces = []
    for _ in range(parts - 1):
        high = x.astype(BF16).astype(F32)
        pieces.append(high)
        x = x - high
    pieces.append(x.astype(BF16).astype(F32))
    return pieces


def left_operand(x, exact):
    w1, w2, w3 = split(x, 3)
    return jnp.concatenate([w1, w1, w2, w1, w2, w3] + exact, axis=1).astype(BF16)


def right_operand(x, exact):
    b1, b2, b3 = split(x, 3)
    return jnp.concatenate([b1, b2, b1, b3, b2, b1] + exact, axis=0).astype(BF16)


def mxu(a, b):
    return jnp.dot(a, b, preferred_element_type=F32)


def mxu_t(a, b):
    return lax.dot_general(a, b, LAST, preferred_element_type=F32)


def radial_terms(offsets, nb):
    q = jnp.sum(offsets * offsets, axis=0, keepdims=True) / (CUTOFF * CUTOFF)
    scale = float(nb - 1)
    centers = lax.broadcasted_iota(I32, (nb, 1), 0).astype(F32) / scale
    arg = (q - centers) * scale
    basis = jnp.exp(-(arg * arg))
    slope = (-2.0 * scale) * arg * basis
    inner = jnp.maximum(1.0 - q, 0.0)
    return basis, slope, inner * inner, -2.0 * inner


def tables(rad_ref, center_ref, other_ref, out_ref):
    stack = jnp.concatenate([rad_ref[...], center_ref[...], other_ref[...]], axis=0)
    w_row = out_ref[...]
    both = jnp.concatenate([stack, jnp.broadcast_to(w_row, (8, w_row.shape[1]))], axis=0).T
    count = stack.shape[0]
    return stack, w_row, both[:, :count], both[:, count : count + 1]


def one_hot_rows(code_a, code_b, ns, width):
    row = lax.broadcasted_iota(I32, (2 * ns, width), 0).astype(F32)
    code = jnp.where(row < ns, code_a, code_b + float(ns))
    return jnp.where(code == row, 1.0, 0.0)


def prepare(t, slots, own, list_ref, rows_ref, cols_ref, e_ref, bound_ref, feat_ref, ns):
    tile = rows_ref.shape[2]
    wide = slots * tile
    entries = [list_ref[0, k, t] for k in range(slots)]
    safe = [jnp.maximum(c, 0) for c in entries]
    xa = rows_ref[own]
    xb = jnp.concatenate([cols_ref[c] for c in safe], axis=0)
    q = jnp.zeros((wide, tile), F32)
    for i in range(3):
        diff = xb[:, i : i + 1] - xa[i : i + 1, :]
        q = q + diff * diff
    b_row = lax.broadcasted_iota(I32, (tile, tile), 0)
    a_lane = lax.broadcasted_iota(I32, (tile, tile), 1)
    allowed = []
    for c in entries:
        limit = jnp.where(c >= 0, 1.0, 0.0)
        allowed.append(jnp.where((b_row == a_lane) & (c == own), 0.0, limit))
    near = jnp.where(q / (CUTOFF * CUTOFF) < 1.0, jnp.concatenate(allowed, axis=0), 0.0)
    near_b = near.astype(BF16)
    r = lax.broadcasted_iota(I32, (wide, wide), 0)
    c = lax.broadcasted_iota(I32, (wide, wide), 1)
    lower = jnp.where(c < r, 1.0, 0.0).astype(BF16)
    rank = jnp.where(near > 0.0, mxu(lower, near_b) + 1.0, 0.0)
    row2 = lax.broadcasted_iota(I32, (2 * tile, tile), 0)
    col2 = lax.broadcasted_iota(I32, (2 * tile, tile), 1)
    reach = jnp.where(row2 < tile, row2 - 1, row2 - tile)
    below = jnp.where(col2 <= reach, 1.0, 0.0).astype(BF16)
    edges = jnp.sum(mxu_t(below, near_b), axis=1, keepdims=True)
    bound_ref[t] = jnp.broadcast_to(edges, (2 * tile, LANES))
    per_atom = jnp.sum(near, axis=0, keepdims=True)
    before = jnp.where(b_row < a_lane, 1.0, 0.0).astype(BF16)
    start = mxu(jnp.broadcast_to(per_atom, (16, tile)).astype(BF16), before)
    high = jnp.floor(start * (1.0 / 128.0))
    rest = start - 128.0 * high
    which = lax.broadcasted_iota(I32, (16, tile), 0)
    codes = jnp.where(which == 0, high, jnp.where(which == 1, rest, 0.0))
    found = jnp.concatenate([rank, codes], axis=0)
    e_ref[t] = jnp.concatenate([jnp.zeros((wide + 16, tile + wide), F32), found], axis=1).astype(BF16)
    row = lax.broadcasted_iota(I32, (8, tile), 0)
    lane = lax.broadcasted_iota(I32, (8, tile), 1).astype(F32)
    kind_row = row.astype(F32)
    kind = xa[3:4, :]
    first = jnp.where(row < 3, xa, jnp.where(row == 4, lane, jnp.where(row == 6, kind, 0.0)))
    first_kind = jnp.where((row < ns) & (kind == kind_row), 1.0, 0.0)
    parts = [jnp.concatenate([first, first_kind], axis=0)]
    for k in range(slots):
        other = rows_ref[safe[k]]
        kind = other[3:4, :]
        second = jnp.where(
            row < 3, -other, jnp.where(row == 5, lane + float(k * tile), jnp.where(row == 7, kind, 0.0))
        )
        second_kind = jnp.where((row >= ns) & (kind + float(ns) == kind_row), 1.0, 0.0)
        parts.append(jnp.concatenate([second, second_kind], axis=0))
    parts.append(jnp.zeros((16, tile), F32))
    feat_ref[t] = jnp.concatenate(split(jnp.concatenate(parts, axis=1), 3), axis=0).astype(BF16)
    return per_atom


def pieces_of(count_ref, width):
    return [(count_ref[t] + (width - 1)) // width for t in range(count_ref.shape[0])]


def locate(step, pieces, others):
    t, begin, place, end = jnp.int32(0), jnp.int32(0), jnp.int32(0), jnp.int32(0)
    for count, other in zip(pieces[:-1], others[:-1]):
        end = end + count
        past = step >= end
        t = t + jnp.where(past, 1, 0)
        begin = begin + jnp.where(past, count, 0)
        place = place + jnp.where(past, other, 0)
    return t, step - begin, place


def selection(order_ref, k, atoms):
    count = order_ref.shape[2]
    row = lax.broadcasted_iota(I32, (atoms, count), 0)
    return jnp.where(row == order_ref[0, k : k + 1, :], 1.0, 0.0).astype(BF16)


def stacked(x):
    return jnp.concatenate(split(x, 3), axis=0).astype(BF16)


def unstacked(x):
    rows = x.shape[0] // 3
    return x[:rows] + (x[rows : 2 * rows] + x[2 * rows :])


def pad_rows(parts, width):
    count = sum(p.shape[0] for p in parts)
    return jnp.concatenate(parts + [jnp.zeros((8 - count, width), F32)], axis=0)


def fill_pool(pos_ref, spec_ref, lower_ref, upper_ref, rows_ref, cols_ref):
    tiles, _, tile = rows_ref.shape
    half = lower_ref.shape[1]
    atoms = pos_ref.shape[2]
    own = pad_rows([pos_ref[i] for i in range(3)] + [spec_ref[...].astype(F32)], atoms)
    row = lax.broadcasted_iota(I32, (8, half), 0)
    shift = jnp.where(row == 0, DOMAIN_WIDTH, 0.0)
    left = jnp.where(row < 4, lower_ref[...] - shift, 0.0)
    right = jnp.where(row < 4, upper_ref[...] + shift, 0.0)
    pool = jnp.concatenate([left, own, right], axis=1)
    turned = pool.T
    for i in range(tiles):
        rows_ref[i] = pool[:, i * tile : (i + 1) * tile]
        cols_ref[i] = turned[i * tile : (i + 1) * tile, :]


def force_kernel(
    nb, ns, width, list_ref, pos_ref, spec_ref, order_ref, lower_ref, upper_ref,
    rad_ref, center_ref, other_ref, out_ref,
    own_ref, to_lower_ref, to_upper_ref, pair_ref, count_ref,
    rows_ref, cols_ref, grad_ref, e_ref, bound_ref, feat_ref, sets, wb_ref, acc_ref,
):
    _, slots, tiles_own = list_ref.shape
    tile = rows_ref.shape[2]
    fill_pool(pos_ref, spec_ref, lower_ref, upper_ref, rows_ref, cols_ref)
    wide_b = slots * tile
    half_tiles = tiles_own // 2
    hid = rad_ref.shape[1]
    near = [
        prepare(t, slots, t + half_tiles, list_ref, rows_ref, cols_ref, e_ref, bound_ref, feat_ref, ns)
        for t in range(tiles_own)
    ]
    for t in range(tiles_own):
        count_ref[t] = jnp.sum(near[t]).astype(I32)
    pieces = pieces_of(count_ref, width)
    total = sum(pieces)
    acc_ref[...] = jnp.zeros_like(acc_ref)
    stack, w_row, cols, w_col = tables(rad_ref, center_ref, other_ref, out_ref)
    half_cols = 0.5 * cols
    weighted = 0.5 * w_row * stack[:nb]
    linear = jnp.dot(
        jnp.concatenate([weighted, w_row, jnp.zeros((7, hid), F32)], axis=0), half_cols,
        precision=HIGHEST, preferred_element_type=F32,
    )
    base = jnp.sum(weighted, axis=1, keepdims=True)
    y_rows = jnp.concatenate([half_cols, linear], axis=0)
    a_y = left_operand(y_rows[:, :nb], split(y_rows[:, nb:], 3)).astype(F32)
    a_r = left_operand((0.5 * w_col) * cols[:, :nb], []).astype(F32)
    gap = -a_y.shape[1] % 16
    a_y = jnp.concatenate([a_y, jnp.zeros((a_y.shape[0], gap + a_r.shape[1]), F32)], axis=1)
    a_r = jnp.concatenate([jnp.zeros((hid, a_y.shape[1] - a_r.shape[1]), F32), a_r], axis=1)
    a_all = jnp.concatenate([a_y, a_r], axis=0).astype(BF16)
    wb_ref[...] = jnp.broadcast_to(w_col, wb_ref.shape)

    def of_step(step):
        t, local, _ = locate(jnp.minimum(step, total - 1), pieces, pieces)
        spot = (local * width + lax.broadcasted_iota(I32, (1, width), 1)).astype(F32)
        return t, spot, spot < jnp.where(step < total, count_ref[t], 0).astype(F32)

    def first_of(step):
        t, spot, _ = of_step(step)
        bounds = bound_ref[t]
        firsts = []
        for lane in range(0, width, LANES):
            here = spot[:, lane : lane + LANES]
            inside = (here >= bounds[:tile]) & (here < bounds[tile:])
            firsts.append(jnp.where(inside, 1.0, 0.0))
        return jnp.concatenate(firsts, axis=1).astype(BF16)

    def second_of(step, found):
        _, spot, valid = of_step(step)
        begin = 128.0 * found[wide_b : wide_b + 1] + found[wide_b + 1 : wide_b + 2]
        rank = jnp.where(valid, spot - begin + 1.0, -1.0)
        return jnp.where(found[:wide_b] == rank, 1.0, 0.0).astype(BF16)

    def describe(step, held, after):
        rep_ref, x_ref, slope_ref, record_ref, side_ref = held[:5]
        t, _, valid = of_step(step)
        first = first_of(step + 1)
        rep_ref[tile + wide_b :] = first
        after[0][:tile] = first
        left = jnp.concatenate([feat_ref[t], e_ref[of_step(step + 1)[0]]], axis=0)
        both = mxu(left, rep_ref[...])
        after[0][tile : tile + wide_b] = second_of(step + 1, both[48:])
        wide = unstacked(both[:48])
        keep = jnp.where(valid, 1.0, 0.0)
        row = lax.broadcasted_iota(I32, (8, width), 0)
        record = jnp.where(row == 3, keep, wide[:8])
        pair_ref[step] = record
        record_ref[...] = record
        kinds = wide[8:16]
        basis, slope, env, denv = radial_terms(wide[0:3], nb)
        b1, b2, b3 = split(basis, 3)
        s1, s2, s3 = split(slope, 3)
        blank = [jnp.zeros((gap, width), F32)] if gap else []
        x = [b1, b2, b1, b3, b2, b1, kinds, kinds, kinds] + blank + [s1, s2, s1, s3, s2, s1]
        x_ref[...] = jnp.concatenate(x, axis=0).astype(BF16)
        slope_ref[...] = slope
        side_ref[...] = pad_rows([keep * denv, keep * env], width)

    def latent(held):
        x_ref, slope_ref = held[1:3]
        y_ref, r_ref, line_ref = held[5:8]
        y = mxu(a_all, x_ref[...])
        y_ref[...] = y[:hid]
        r_ref[...] = y[hid + 16 :]
        lin = jnp.sum(slope_ref[...] * (base + y[hid : hid + 8]), axis=0, keepdims=True)
        line_ref[...] = pad_rows([y[hid + 8 : hid + 9], lin], width)

    def channels(held):
        record_ref, side_ref, y_ref, r_ref, line_ref, gd_ref = held[3:]
        s_rows, t_rows = [], []
        for lane in range(0, width, LANES):
            s = jnp.zeros((8, LANES), F32)
            u = jnp.zeros((8, LANES), F32)
            for h in range(0, hid, 8):
                y = y_ref[h : h + 8, lane : lane + LANES]
                r = r_ref[h : h + 8, lane : lane + LANES]
                th = jnp.tanh(y)
                a = y * th
                g = th * (1.0 - a)
                s = s + wb_ref[h : h + 8, :] * a
                u = u + r * g
            s_rows.append(jnp.sum(s, axis=0, keepdims=True))
            t_rows.append(jnp.sum(u, axis=0, keepdims=True))
        s_all = jnp.concatenate(s_rows, axis=1) + line_ref[0:1]
        t_all = jnp.concatenate(t_rows, axis=1) + line_ref[1:2]
        g = side_ref[0:1] * s_all + side_ref[1:2] * t_all
        gd_ref[...] = stacked((2.0 * g) * record_ref[...])

    def gather(step, held):
        t, _, _ = locate(jnp.clip(step, 0, total - 1), pieces, pieces)
        acc_ref[t] = acc_ref[t] + unstacked(mxu_t(held[-1][...], held[0][: tile + wide_b]))

    def rounds(i, carry):
        for m in range(4):
            step = 4 * i + m
            gather(step - 1, sets[(m + 3) % 4])
            describe(step + 2, sets[(m + 2) % 4], sets[(m + 3) % 4])
            latent(sets[(m + 1) % 4])
            channels(sets[m])
        return carry

    for ref in (sets[3][0], sets[3][-1]):
        ref[...] = jnp.zeros_like(ref)
    first = first_of(jnp.int32(0))
    sets[0][0][:tile] = first
    found = mxu(e_ref[of_step(jnp.int32(0))[0], :, tile + wide_b :], first)
    sets[0][0][tile : tile + wide_b] = second_of(jnp.int32(0), found)
    for step in range(2):
        describe(jnp.int32(step), sets[step], sets[step + 1])
    latent(sets[0])
    rotations = (total + 3) // 4
    lax.fori_loop(0, rotations, rounds, 0)
    gather(4 * rotations - 1, sets[3])
    grad_ref[...] = jnp.zeros_like(grad_ref)
    for t in range(tiles_own):
        own = t + half_tiles
        grad_ref[own] = grad_ref[own] + acc_ref[t, :, :tile]
        for k in range(slots):
            entry = jnp.maximum(list_ref[0, k, t], 0)
            grad_ref[entry] = grad_ref[entry] - acc_ref[t, :, (k + 1) * tile : (k + 2) * tile]
    whole = jnp.concatenate([grad_ref[i] for i in range(grad_ref.shape[0])], axis=1)
    atoms = pos_ref.shape[2]
    half = atoms // 2
    own_grad = whole[:, half : half + atoms]
    own_ref[...] = own_grad
    pieces = stacked(own_grad)
    for k, ref in ((0, to_lower_ref), (1, to_upper_ref)):
        sent = unstacked(mxu(pieces, selection(order_ref, k, atoms)))
        ghost = whole[:, :half] if k == 0 else whole[:, half + atoms :]
        ref[...] = pad_rows([sent[0:3], ghost[0:3]], half)


def finish_forces(
    weight, order_ref, target_ref, lower_ref, upper_ref, own_ref,
    to_lower_ref, to_upper_ref, from_lower_ref, from_upper_ref, forces_ref, v_ref,
):
    tiles, _, tile = v_ref.shape
    atoms = own_ref.shape[1]
    total = own_ref[0:3, :]
    for k, ref in ((0, from_lower_ref), (1, from_upper_ref)):
        total = total + unstacked(mxu_t(stacked(ref[...]), selection(order_ref, k, atoms)))[3:6]
    for i in range(3):
        forces_ref[i] = -total[i : i + 1]
    miss = total + jnp.concatenate([target_ref[i] for i in range(3)], axis=0)
    left = to_lower_ref[3:6, :] + from_lower_ref[0:3, :] + lower_ref[4:7, :]
    right = to_upper_ref[3:6, :] + from_upper_ref[0:3, :] + upper_ref[4:7, :]
    scaled = (2.0 * weight) * jnp.concatenate([left, miss, right], axis=1)
    scaled = pad_rows([scaled], scaled.shape[1])
    for i in range(tiles):
        v_ref[i] = scaled[:, i * tile : (i + 1) * tile]
    return weight * jnp.sum(miss * miss)


def param_kernel(
    nb, ns, width, count_ref, list_ref, weight_ref, order_ref, target_ref, lower_ref, upper_ref, own_ref,
    to_lower_ref, to_upper_ref, from_lower_ref, from_upper_ref, pair_ref, rad_ref, center_ref, other_ref, out_ref,
    forces_ref, grads_ref,
    v_ref, va_ref, vb_ref, sets, acc_g, acc_f, acc_s, gram_ref,
):
    _, slots, tiles_own = list_ref.shape
    tile = v_ref.shape[2]
    half_tiles = tiles_own // 2
    hid = rad_ref.shape[1]
    outer = pair_ref.shape[2]
    weight = weight_ref[0].astype(F32)
    loss = finish_forces(
        weight, order_ref, target_ref, lower_ref, upper_ref, own_ref,
        to_lower_ref, to_upper_ref, from_lower_ref, from_upper_ref, forces_ref, v_ref,
    )
    mid = nb + 2 * ns
    acc_g[...] = jnp.zeros_like(acc_g)
    acc_f[...] = jnp.zeros_like(acc_f)
    acc_s[...] = jnp.zeros_like(acc_s)
    gram_ref[...] = jnp.zeros_like(gram_ref)
    for t in range(tiles_own):
        va_ref[t] = jnp.concatenate([v_ref[t + half_tiles], jnp.zeros((8, LANES - tile), F32)], axis=1)
        vb_ref[t] = jnp.concatenate([v_ref[jnp.maximum(list_ref[0, k, t], 0)] for k in range(slots)], axis=1)
    stack, w_row, cols, w_col = tables(rad_ref, center_ref, other_ref, out_ref)
    half_cols = 0.5 * cols
    a_y = left_operand(half_cols[:, :nb], split(half_cols[:, nb:], 3))

    pieces, chunks = pieces_of(count_ref, width), pieces_of(count_ref, outer)
    total = sum(pieces)
    share = outer // width

    def front(step, held):
        y_ref, alpha_ref, g_cols, f_cols, x_rows = held[:5]
        t, local, place = locate(jnp.minimum(step, total - 1), pieces, chunks)
        lane = pl.multiple_of(local % share * width, width)
        record = pair_ref[place + local // share, :, pl.ds(lane, width)]
        offsets = record[0:3]
        keep = record[3:4] * jnp.where(step < total, 1.0, 0.0)
        index_a = jnp.broadcast_to(record[4:5].astype(I32), (8, width))
        index_b = jnp.broadcast_to(record[5:6].astype(I32), (8, width))
        va, vb = va_ref[t], vb_ref[t]
        diffs = []
        for lane in range(0, width, LANES):
            part_a = jnp.take_along_axis(va, index_a[:, lane : lane + LANES], axis=1, mode="promise_in_bounds")
            part_b = jnp.take_along_axis(vb, index_b[:, lane : lane + LANES], axis=1, mode="promise_in_bounds")
            diffs.append(part_a - part_b)
        dv = jnp.concatenate(diffs, axis=1)
        kinds = one_hot_rows(record[6:7], record[7:8], ns, width)
        basis, slope, env, denv = radial_terms(offsets, nb)
        c = (2.0 * keep) * jnp.sum(offsets * dv[0:3], axis=0, keepdims=True)
        alpha = c * denv
        beta_slope = (c * env) * slope
        y_ref[...] = mxu(a_y, right_operand(basis, [kinds, kinds, kinds]))
        alpha_ref[...] = jnp.broadcast_to(alpha, (8, width))
        x = jnp.concatenate([basis, kinds], axis=0)
        one = jnp.ones((8, width), F32)
        g_cols[...] = jnp.concatenate(
            split(jnp.concatenate([alpha * x, beta_slope], axis=0), 2), axis=0
        ).astype(BF16)
        f_cols[...] = jnp.concatenate(
            split(jnp.concatenate([beta_slope[j : j + 1] * x for j in range(nb)], axis=0), 2), axis=0
        ).astype(BF16)
        x_rows[...] = jnp.concatenate(split(x, 2) + [one, one], axis=0).astype(BF16)

    def middle(held, top, bottom):
        y_ref, alpha_ref, _, _, _, g_ref, f_ref = held
        for h in range(top, bottom, 16):
            s = acc_s[h : h + 16, :]
            for lane in range(0, width, LANES):
                alpha = alpha_ref[:, lane : lane + LANES]
                y = y_ref[h : h + 16, lane : lane + LANES]
                th = jnp.tanh(y)
                a = y * th
                u = 1.0 - a
                g = th * u
                f = u - th * g
                s = s + jnp.concatenate([alpha, alpha], axis=0) * a
                for ref, x in ((g_ref, g), (f_ref, f)):
                    high = x.astype(BF16)
                    ref[h : h + 16, lane : lane + LANES] = high
                    ref[hid + h : hid + h + 16, lane : lane + LANES] = (x - high.astype(F32)).astype(BF16)
            acc_s[h : h + 16, :] = s

    def rear(held, part):
        g_cols, f_cols, x_rows, g_ref, f_ref = held[2:]
        if part == 0:
            acc_f[...] += mxu_t(f_cols[...], f_ref[:hid])
        elif part == 1:
            acc_f[: nb * mid] += mxu_t(f_cols[: nb * mid], f_ref[hid:])
        elif part == 2:
            acc_g[...] += mxu_t(g_cols[...], g_ref[:hid])
        else:
            acc_g[: mid + nb] += mxu_t(g_cols[: mid + nb], g_ref[hid:])
            gram_ref[...] += mxu_t(g_cols[...], x_rows[...])

    def rounds(i, carry):
        for m in range(4):
            edges = [0, 5 * hid // 16, 10 * hid // 16, 13 * hid // 16, hid]
            for part in range(4):
                rear(sets[(m + 3) % 4], part)
                middle(sets[m], edges[part], edges[part + 1])
            front(4 * i + m + 1, sets[(m + 1) % 4])
        return carry

    for ref in sets[3][2:]:
        ref[...] = jnp.zeros_like(ref)
    front(jnp.int32(0), sets[0])
    lax.fori_loop(0, (total + 3) // 4, rounds, 0)
    for part in range(4):
        rear(sets[3], part)
    cols_g = mid + nb
    gram = gram_ref[:cols_g] + gram_ref[cols_g:]
    gram_x = gram[:, :mid] + gram[:, mid : 2 * mid]
    gram_one = gram[:, 2 * mid : 2 * mid + 1]
    half_stack = 0.5 * stack
    spread = jnp.dot(gram_x, half_stack, precision=HIGHEST, preferred_element_type=F32)
    first = 0.5 * (gram_one + spread + (acc_g[:cols_g] + acc_g[cols_g:]))
    sharp = 0.5 * (acc_f[: nb * mid] + acc_f[nb * mid :])
    d = first[:mid]
    for j in range(nb):
        d = d + stack[j : j + 1] * sharp[j * mid : (j + 1) * mid]
    slope_part = first[mid:]
    grad_out = (
        jnp.sum(acc_s[...].T, axis=0, keepdims=True)
        + jnp.sum(half_stack * gram_one[:mid], axis=0, keepdims=True)
        + jnp.sum(slope_part * stack[:nb], axis=0, keepdims=True)
    )
    lane = lax.broadcasted_iota(I32, (1, hid), 1)
    grads_ref[:nb] = w_row * (d[:nb] + slope_part)
    grads_ref[nb:mid] = w_row * d[nb:]
    grads_ref[mid : mid + 1] = grad_out
    grads_ref[mid + 1 :] = jnp.where(lane == 0, loss, jnp.where(lane == 1, weight, 0.0))


SMEM_SPEC = pl.BlockSpec(memory_space=pltpu.SMEM)
VMEM_SPEC = pl.BlockSpec(memory_space=pltpu.VMEM)
MESH = pl.DeviceIdType.MESH
MIB = 1024 * 1024


def swap(to_lower, to_upper, from_lower, from_upper, sems):
    me, count = lax.axis_index("space"), lax.axis_size("space")
    group = lax.axis_index("dp")
    upper, lower = lax.rem(me + 1, count), lax.rem(me + count - 1, count)
    up = pltpu.make_async_remote_copy(
        src_ref=to_upper, dst_ref=from_lower, send_sem=sems.at[0], recv_sem=sems.at[1],
        device_id=(group, upper), device_id_type=MESH,
    )
    down = pltpu.make_async_remote_copy(
        src_ref=to_lower, dst_ref=from_upper, send_sem=sems.at[2], recv_sem=sems.at[3],
        device_id=(group, lower), device_id_type=MESH,
    )
    return up, down


def greet():
    me, count = lax.axis_index("space"), lax.axis_size("space")
    group = lax.axis_index("dp")
    barrier = pltpu.get_barrier_semaphore()
    for other in (lax.rem(me + 1, count), lax.rem(me + count - 1, count)):
        pl.semaphore_signal(barrier, inc=1, device_id=(group, other), device_id_type=MESH)
    return barrier


def face_kernel(
    pos_ref, spec_ref, target_ref, order_ref, *refs,
):
    count = 5
    more, refs = refs[:count], refs[count:]
    lower_ref, upper_ref, pos_out, spec_out, target_out, order_out = refs[:6]
    more_out, refs = refs[6 : 6 + count], refs[6 + count :]
    to_lower, to_upper, from_lower, from_upper, sems, load_sems = refs
    barrier = greet()
    sources = (pos_ref, spec_ref, target_ref, order_ref) + more
    targets = (pos_out, spec_out, target_out, order_out) + more_out
    loads = [pltpu.make_async_copy(s, t, load_sems.at[i]) for i, (s, t) in enumerate(zip(sources, targets))]
    for load in loads:
        load.start()
    for load in loads[:4]:
        load.wait()
    atoms = pos_out.shape[2]
    rows = [pos_out[i] for i in range(3)] + [spec_out[...].astype(F32)] + [target_out[i] for i in range(3)]
    pieces = stacked(pad_rows(rows, atoms))
    to_lower[...] = unstacked(mxu(pieces, selection(order_out, 0, atoms)))
    to_upper[...] = unstacked(mxu(pieces, selection(order_out, 1, atoms)))
    pl.semaphore_wait(barrier, 2)
    up, down = swap(to_lower, to_upper, from_lower, from_upper, sems)
    up.start()
    down.start()
    for load in loads[4:]:
        load.wait()
    up.wait()
    down.wait()
    lower_ref[...] = from_lower[...]
    upper_ref[...] = from_upper[...]


def ghost_kernel(to_lower, to_upper, lower_ref, upper_ref, from_lower, from_upper, sems):
    barrier = greet()
    pl.semaphore_wait(barrier, 2)
    up, down = swap(to_lower, to_upper, from_lower, from_upper, sems)
    up.start()
    down.start()
    up.wait()
    down.wait()
    lower_ref[...] = from_lower[...]
    upper_ref[...] = from_upper[...]


def sum_kernel(x_ref, out_ref, near, part, far, near_send, near_recv, far_send, far_recv):
    group, me = lax.axis_index("dp"), lax.axis_index("space")
    groups, count = lax.axis_size("dp"), lax.axis_size("space")
    barrier = pltpu.get_barrier_semaphore()
    others = [(lax.rem(group + k, groups), me) for k in range(1, groups)]
    others += [(group, lax.rem(me + k, count)) for k in range(1, count)]
    for other in others:
        pl.semaphore_signal(barrier, inc=1, device_id=other, device_id_type=MESH)
    pl.semaphore_wait(barrier, len(others))

    def share(source, slots, send, recv, spot, peers):
        copies = []
        for k, other in enumerate(peers):
            copies.append(
                pltpu.make_async_remote_copy(
                    src_ref=source, dst_ref=slots.at[spot], send_sem=send.at[k], recv_sem=recv.at[k],
                    device_id=other, device_id_type=MESH,
                )
            )
            copies[-1].start()
        slots[spot] = source[...]
        for copy in copies:
            copy.wait()
        total = slots[0]
        for k in range(1, len(peers) + 1):
            total = total + slots[k]
        return total

    part[...] = share(x_ref, near, near_send, near_recv, group, others[: groups - 1])
    out_ref[...] = share(part, far, far_send, far_recv, me, others[groups - 1 :])


def final_kernel(nb, ns, atoms, domains, sum_ref, loss_ref, rad_ref, center_ref, other_ref, out_ref):
    last = nb + 2 * ns
    weight_total = sum_ref[last + 1 : last + 2, 1:2] / domains
    scale = 1.0 / (3.0 * atoms * domains * weight_total)
    loss_ref[...] = sum_ref[last + 1 : last + 2, 0:1] * scale
    rad_ref[...] = sum_ref[:nb] * scale
    center_ref[...] = sum_ref[nb : nb + ns] * scale
    other_ref[...] = sum_ref[nb + ns : last] * scale
    out_ref[...] = sum_ref[last : last + 1] * scale


def pool_force(tile_list, positions, species, order, lower, upper, params, width):
    atoms = positions.shape[2]
    half = atoms // 2
    _, slots, own = tile_list.shape
    tile = atoms // own
    tiles = 2 * own
    rad, center = params[0], params[1]
    nb, hid = rad.shape
    ns = center.shape[0]
    most = own * (-(-slots * tile * tile // width))
    wide_b = slots * tile
    held = (
        pltpu.VMEM((2 * tile + wide_b, width), BF16),
        pltpu.VMEM((-(-(6 * nb + 6 * ns) // 16) * 16 + 6 * nb, width), BF16),
        pltpu.VMEM((nb, width), F32),
        pltpu.VMEM((8, width), F32),
        pltpu.VMEM((8, width), F32),
        pltpu.VMEM((hid, width), F32),
        pltpu.VMEM((hid, width), F32),
        pltpu.VMEM((8, width), F32),
        pltpu.VMEM((24, width), BF16),
    )
    return pl.pallas_call(
        functools.partial(force_kernel, nb, ns, width),
        out_shape=(
            jax.ShapeDtypeStruct((8, atoms), F32),
            jax.ShapeDtypeStruct((8, half), F32),
            jax.ShapeDtypeStruct((8, half), F32),
            jax.ShapeDtypeStruct((most + 8, 8, width), F32),
            jax.ShapeDtypeStruct((own,), I32),
        ),
        in_specs=[SMEM_SPEC] + [VMEM_SPEC] * 9,
        out_specs=(VMEM_SPEC,) * 4 + (SMEM_SPEC,),
        scratch_shapes=[
            pltpu.VMEM((tiles, 8, tile), F32),
            pltpu.VMEM((tiles, tile, 8), F32),
            pltpu.VMEM((tiles, 8, tile), F32),
            pltpu.VMEM((own, wide_b + 16, 2 * tile + wide_b), BF16),
            pltpu.VMEM((own, 2 * tile, LANES), F32),
            pltpu.VMEM((own, 48, 2 * tile + wide_b), BF16),
            (held,) * 4,
            pltpu.VMEM((hid, LANES), F32),
            pltpu.VMEM((own, 8, tile + wide_b), F32),
        ],
        compiler_params=pltpu.CompilerParams(vmem_limit_bytes=32 * MIB),
        name="pool_force",
    )(tile_list, positions, species, order, lower, upper, *params)


def pool_params(counts, tile_list, weights, order, targets, ghosts, sums, pairs, params, width):
    _, slots, own = tile_list.shape
    atoms = targets.shape[2]
    tile = atoms // own
    rad, center = params[0], params[1]
    nb, hid = rad.shape
    ns = center.shape[0]
    mid = nb + 2 * ns
    rows = mid + 2
    held = (
        pltpu.VMEM((hid, width), F32),
        pltpu.VMEM((8, width), F32),
        pltpu.VMEM((2 * (mid + nb), width), BF16),
        pltpu.VMEM((2 * nb * mid, width), BF16),
        pltpu.VMEM((2 * mid + 16, width), BF16),
    ) + (pltpu.VMEM((2 * hid, width), BF16),) * 2
    return pl.pallas_call(
        functools.partial(param_kernel, nb, ns, width),
        out_shape=(
            jax.ShapeDtypeStruct(targets.shape, F32),
            jax.ShapeDtypeStruct((rows, hid), F32),
        ),
        in_specs=[SMEM_SPEC] * 3 + [VMEM_SPEC] * 14,
        out_specs=(VMEM_SPEC,) * 2,
        scratch_shapes=[
            pltpu.VMEM((2 * own, 8, tile), F32),
            pltpu.VMEM((own, 8, LANES), F32),
            pltpu.VMEM((own, 8, LANES), F32),
            (held,) * 4,
            pltpu.VMEM((2 * (mid + nb), hid), F32),
            pltpu.VMEM((2 * nb * mid, hid), F32),
            pltpu.VMEM((hid, LANES), F32),
            pltpu.VMEM((2 * (mid + nb), 2 * mid + 16), F32),
        ],
        compiler_params=pltpu.CompilerParams(vmem_limit_bytes=32 * MIB),
        name="pool_params",
    )(counts, tile_list, weights, order, targets, *ghosts, *sums, pairs, *params)


def face_exchange(positions, species, targets, order, *others):
    half = order.shape[2]
    box = jax.ShapeDtypeStruct((8, half), F32)
    arrays = (positions, species, targets, order) + others
    held = tuple(jax.ShapeDtypeStruct(x.shape, x.dtype) for x in arrays)
    return pl.pallas_call(
        face_kernel,
        out_shape=(box, box) + held,
        in_specs=[pl.BlockSpec(memory_space=pltpu.HBM)] * len(arrays),
        out_specs=(VMEM_SPEC,) * (2 + len(arrays)),
        scratch_shapes=[pltpu.VMEM((8, half), F32)] * 4
        + [pltpu.SemaphoreType.DMA((4,)), pltpu.SemaphoreType.DMA((len(arrays),))],
        compiler_params=pltpu.CompilerParams(collective_id=0, has_side_effects=True, vmem_limit_bytes=8 * MIB),
        name="face_exchange",
    )(*[pltpu.with_memory_space_constraint(x, pltpu.HBM) for x in arrays])


def ghost_exchange(to_lower, to_upper):
    box = jax.ShapeDtypeStruct(to_lower.shape, F32)
    return pl.pallas_call(
        ghost_kernel,
        out_shape=(box, box),
        in_specs=[VMEM_SPEC] * 2,
        out_specs=(VMEM_SPEC,) * 2,
        scratch_shapes=[pltpu.VMEM(to_lower.shape, F32)] * 2 + [pltpu.SemaphoreType.DMA((4,))],
        compiler_params=pltpu.CompilerParams(collective_id=1, has_side_effects=True, vmem_limit_bytes=4 * MIB),
        name="ghost_exchange",
    )(to_lower, to_upper)


def sum_everywhere(x):
    groups, count = lax.axis_size("dp"), lax.axis_size("space")
    return pl.pallas_call(
        sum_kernel,
        out_shape=jax.ShapeDtypeStruct(x.shape, F32),
        in_specs=[VMEM_SPEC],
        out_specs=VMEM_SPEC,
        scratch_shapes=[
            pltpu.VMEM((groups,) + x.shape, F32),
            pltpu.VMEM(x.shape, F32),
            pltpu.VMEM((count,) + x.shape, F32),
            pltpu.SemaphoreType.DMA((groups - 1,)),
            pltpu.SemaphoreType.DMA((groups - 1,)),
            pltpu.SemaphoreType.DMA((count - 1,)),
            pltpu.SemaphoreType.DMA((count - 1,)),
        ],
        compiler_params=pltpu.CompilerParams(
            collective_id=2, has_side_effects=True, vmem_limit_bytes=8 * MIB
        ),
        name="sum_everywhere",
    )(x)


def finish(summed, nb, ns, atoms):
    hid = summed.shape[1]
    domains = lax.axis_size("space")
    shapes = ((1, 1), (nb, hid), (ns, hid), (ns, hid), (1, hid))
    return pl.pallas_call(
        functools.partial(final_kernel, nb, ns, float(atoms), float(domains)),
        out_shape=tuple(jax.ShapeDtypeStruct(s, F32) for s in shapes),
        in_specs=[VMEM_SPEC],
        out_specs=(VMEM_SPEC,) * len(shapes),
        compiler_params=pltpu.CompilerParams(vmem_limit_bytes=4 * MIB),
        name="finish",
    )(summed)


def body(positions, species, ref_forces, send_lists, tile_lists, weights, w_rad, emb_center, emb_other, w_out):
    nb = w_rad.shape[0]
    ns = emb_center.shape[0]
    positions, ref_forces = positions.transpose(1, 0, 2), ref_forces.transpose(1, 0, 2)
    tile_lists = tile_lists.transpose(0, 2, 1)
    lower, upper, positions, species, ref_forces, send_lists, tile_lists, *params = face_exchange(
        positions, species, ref_forces, send_lists, tile_lists, w_rad, emb_center, emb_other, w_out[None]
    )
    own_grad, to_lower, to_upper, pairs, counts = pool_force(
        tile_lists, positions, species, send_lists, lower, upper, params, 4 * LANES
    )
    from_lower, from_upper = ghost_exchange(to_lower, to_upper)
    forces, grads = pool_params(
        counts, tile_lists, weights, send_lists, ref_forces, (lower, upper),
        (own_grad, to_lower, to_upper, from_lower, from_upper), pairs, params, 2 * LANES,
    )
    summed = sum_everywhere(grads)
    loss, grad_rad, grad_center, grad_other, grad_out = finish(summed, nb, ns, positions.shape[2])
    forces = forces.transpose(1, 0, 2)
    return forces, loss[0, 0], grad_rad, grad_center, grad_other, grad_out[0]


def solution(mesh):
    return jax.shard_map(
        body,
        mesh=mesh,
        in_specs=(
            P("dp", None, "space"),
            P("dp", "space"),
            P("dp", None, "space"),
            P("dp", "space", None),
            P("dp", "space", None),
            P("dp"),
            P(),
            P(),
            P(),
            P(),
        ),
        out_specs=(P("dp", None, "space"), P(), P(), P(), P(), P()),
        check_vma=False,
    )
```
